32 devices in a mesh: row: 4 (over y, x), col: 8 (over z, core).
Axes of the slice: x: 2, y: 2, z: 4, core: 2. Of those that a mesh axis runs over, the one named last changes fastest.
Arguments:
- p_tiles: float32 [2304, 4608], P('row', 'col'), may hold values from -0.6 to 0.6
- square_kept: int32 [36, 72], P('row', 'col'), may hold values 0 or 1
- result_kept: int32 [36, 72], P('row', 'col'), may hold values 0 or 1
Outputs:
- purified: float32 [2304, 4608], P('row', 'col')
The draws below stay inside these ranges and needn't reach their ends.
Inputs may be any that keep to these rules, and one draw needn't show every extreme that they name: `square_kept`: one entry for each block of the layout of p_tiles. `result_kept`: one entry for each block of the layout of p_tiles.
All inputs are finite; a program needn't handle non-finite values.
Results may differ from the reference program's by a relative error of at most 0.0003.
Values sent between devices are 32-bit elements; how exact they have to be, the bound alone decides.
No kernel may reach another device: no remote copies, remote signals or barrier semaphores. Data moves between devices by JAX's collectives and lax.ppermute only.
A program may use at most 64 MiB of HBM per device.

```python
import jax
import jax.numpy as jnp
from jax import lax

LZ = 3
LX = 4
LY = 8
GROUP = 192
TILE = 576
N_ROW = 4
N_COL = 8


def set_ends(values, stream_key, low, top_value):
    shape = values.shape
    place = [jax.random.randint(jax.random.fold_in(stream_key, axis), (), 0, shape[axis]) for axis in range(len(shape))]
    values = values.at[tuple(place)].set(low)
    longest = shape.index(max(shape))
    place[longest] = (place[longest] + 1) % shape[longest]
    return values.at[tuple(place)].set(top_value)


def block_scale(own_key, extent, cuts, low, high):
    gain = 1.0
    for dim, parts in cuts:
        heights = jax.random.uniform(jax.random.fold_in(jax.random.fold_in(own_key, 6), dim), (parts,), jnp.float32, low / len(cuts), high / len(cuts))
        gain = gain * jnp.repeat(jnp.exp(heights), extent[dim] // parts).reshape((-1,) + (1,) * (len(extent) - 1 - dim))
    return gain


def noise(key, extent, scale, limit, pieces=(), kind=jnp.bfloat16):
    drawn = jax.random.normal(key, extent, jnp.float32) * scale
    if len(pieces) > 0:
        drawn = block_scale(key, extent, pieces, -0.22, 0.18) * drawn
    return jnp.clip(drawn, min=-limit, max=limit).astype(kind)


def setup_inputs(seed: int = 0) -> dict:
    key_list = jax.random.split(jax.random.key(seed), 4)
    return {
        "p_tiles": noise(key_list[0], (LX * TILE, LY * TILE), 0.1, 0.6, ((0, 4), (1, 8)), jnp.float32),
        "square_kept": set_ends((jax.random.randint(key_list[1], (LX * 3 * LZ, LY * 3 * LZ), 0, 5) < 4).astype(jnp.int32), jax.random.fold_in(key_list[1], 1), 0, 1),
        "result_kept": set_ends((jax.random.randint(key_list[2], (LX * 3 * LZ, LY * 3 * LZ), 0, 5) < 4).astype(jnp.int32), jax.random.fold_in(key_list[2], 1), 0, 1),
    }


def mask_blocks(own_tile, kept_mask):
    block_count = kept_mask.shape[0]
    block_size = own_tile.shape[0] // block_count
    block_grid = own_tile.reshape(block_count, block_size, kept_mask.shape[1], block_size)
    block_grid = block_grid * kept_mask.astype(jnp.float32)[:, None, :, None]
    return block_grid.reshape(own_tile.shape)


def block_product(left_own, left_prev, left_next, right_own, right_prev, right_next):
    group_rows = left_own.shape[0] // 3
    full_side = 3 * group_rows
    lefts = ((0, left_own, 0), (1, left_next, group_rows), (-1, left_prev, 0))
    rights = ((0, right_own, 0), (1, right_next, group_rows), (-1, right_prev, 0))
    summed = jnp.zeros((full_side, full_side), jnp.float32)
    for row_step, left_part, row_start in lefts:
        for col_step, right_part, col_start in rights:
            product_term = jnp.dot(
                left_part[:, (col_step + 1) * group_rows:(col_step + 2) * group_rows],
                right_part[(row_step + 1) * group_rows:(row_step + 2) * group_rows, :],
                precision=lax.Precision.HIGHEST, preferred_element_type=jnp.float32)
            row_after = full_side - row_start - product_term.shape[0]
            col_after = full_side - col_start - product_term.shape[1]
            summed = summed + jnp.pad(product_term, ((row_start, row_after), (col_start, col_after)))
    return summed


def product_rows(left_tiles, right_tiles):
    def one_row(row_index):
        own_left = lax.dynamic_index_in_dim(left_tiles, row_index, 0, keepdims=False)
        prev_left = jnp.roll(own_left, 1, axis=0)[:, GROUP:, :]
        next_left = jnp.roll(own_left, -1, axis=0)[:, :2 * GROUP, :]
        own_right = lax.dynamic_index_in_dim(right_tiles, row_index, 0, keepdims=False)
        prev_index = ((row_index + N_ROW - 1) % N_ROW).astype(jnp.int32)
        next_index = ((row_index + 1) % N_ROW).astype(jnp.int32)
        prev_right = lax.dynamic_index_in_dim(right_tiles, prev_index, 0, keepdims=False)[:, :, GROUP:]
        next_right = lax.dynamic_index_in_dim(right_tiles, next_index, 0, keepdims=False)[:, :, :2 * GROUP]
        return jax.vmap(block_product)(own_left, prev_left, next_left, own_right, prev_right, next_right)
    return lax.map(one_row, jnp.arange(N_ROW, dtype=jnp.int32))


def reference(p_tiles, square_kept, result_kept):
    tiles = p_tiles.reshape(N_ROW, TILE, N_COL, TILE).transpose(0, 2, 1, 3)
    blocks_side = 3 * LZ
    square_masks = square_kept.reshape(N_ROW, blocks_side, N_COL, blocks_side).transpose(0, 2, 1, 3)
    result_masks = result_kept.reshape(N_ROW, blocks_side, N_COL, blocks_side).transpose(0, 2, 1, 3)
    masked = jax.vmap(jax.vmap(mask_blocks))
    square = masked(product_rows(tiles, tiles), square_masks)
    cubed = product_rows(square, tiles)
    purified = masked(3.0 * square - 2.0 * cubed, result_masks)
    return purified.transpose(0, 2, 1, 3).reshape(N_ROW * TILE, N_COL * TILE)
```

```python
import functools

import jax
import jax.numpy as jnp
from jax import lax
from jax.experimental import pallas as pl
from jax.experimental.pallas import tpu as pltpu
from jax.sharding import PartitionSpec as P

LANES = 128
WIDE = 256
F32 = jnp.float32
BF16 = jnp.bfloat16


def low_half(rows):
    return lax.broadcasted_iota(jnp.int32, (rows, LANES), 1) < LANES // 2


def fold(first, second):
    half = first.shape[0] // 2
    tail = jnp.where(low_half(half), second[:half], pltpu.roll(second[half:], LANES // 2, 1))
    return first, tail


def unfold(packed):
    rows = packed.shape[0] * 2 // 3
    half = rows // 2
    tail = packed[rows:]
    keep = low_half(half)
    upper = jnp.where(keep, tail, 0.0)
    lower = jnp.where(keep, pltpu.roll(tail, LANES // 2, 1), 0.0)
    return jnp.concatenate([packed[:rows], jnp.concatenate([upper, lower], 0)], 1)


def column_group(tile_ref, group, start, rows):
    keep = low_half(rows)
    at = pl.ds(start, rows)
    if group == 0:
        return tile_ref[at, 0:128], jnp.where(keep, tile_ref[at, 128:256], 0.0)
    if group == 1:
        one = pltpu.roll(tile_ref[at, 128:256], LANES // 2, 1)
        two = pltpu.roll(tile_ref[at, 256:384], LANES // 2, 1)
        return jnp.where(keep, one, two), jnp.where(keep, two, 0.0)
    last = tile_ref[at, 512:576]
    return tile_ref[at, 384:512], jnp.concatenate([last, jnp.zeros_like(last)], 1)


def split(value):
    high = value.astype(BF16)
    return high, (value - high.astype(F32)).astype(BF16)


def store_fold(out_ref, base, first, second):
    rows = first.shape[0]
    one, two = fold(first, second)
    out_ref[pl.ds(base, rows), :] = one
    out_ref[pl.ds(base + rows, rows // 2), :] = two


def pack_body(tile_ref, to_next, to_prev, middle, left, right):
    side = tile_ref.shape[0]
    group = side // 3
    for g in range(3):
        first, second = column_group(tile_ref, g, 0, side)
        store_fold((left, middle, right)[g], 0, first, second)
        store_fold(to_next, g * 3 * group, first[group:], second[group:])
        store_fold(to_prev, g * 3 * group, first[: 2 * group], second[: 2 * group])


def left_factors(value):
    high, low = split(value)
    return high, low


def right_rows(high, low, ky, group):
    at = slice(ky * group, (ky + 1) * group)
    pad = jnp.zeros((WIDE - group, WIDE), BF16)
    return jnp.concatenate([high[at], pad], 0), jnp.concatenate([low[at], pad], 0)


def passes(lefts, rights):
    wide = [high for high, _ in lefts] + [low for _, low in lefts] + [high for high, _ in lefts]
    tall = [high for high, _ in rights] + [high for high, _ in rights] + [low for _, low in rights]
    return jnp.dot(jnp.concatenate(wide, 1), jnp.concatenate(tall, 0), preferred_element_type=F32)


def mask_lanes(kept_ref, row, first_block):
    lane = lax.broadcasted_iota(jnp.int32, (8, WIDE), 1)
    flags = [kept_ref[row, first_block + j] for j in range(3)]
    chosen = jnp.where(lane < 64, flags[0], jnp.where(lane < 128, flags[1], flags[2]))
    return chosen.astype(F32)[:1]


def masked(value, kept_ref, group_index):
    rows = value.shape[0] // 9
    return jnp.concatenate(
        [value[i * rows : (i + 1) * rows] * mask_lanes(kept_ref, i, 3 * group_index) for i in range(9)], 0
    )


def stacked(own, before, after):
    group = own.shape[0] // 3
    return jnp.concatenate(
        [
            own[:group] + before[:group],
            own[group : 2 * group] + before[group:] + after[:group],
            own[2 * group :] + after[group:],
        ],
        0,
    )


def product(lefts, rights, group):
    parts = [
        passes(lefts[ky], [right_rows(high, low, ky, group) for high, low in rights]) for ky in range(3)
    ]
    return stacked(parts[1], parts[0], parts[2])


def load_left(packed_ref, group):
    return [split(unfold(packed_ref[g * 3 * group : (g + 1) * 3 * group, :])) for g in range(3)]


def own_group(tile_ref, g):
    side = tile_ref.shape[0]
    return split(jnp.concatenate(column_group(tile_ref, g, 0, side), 1))


def store_sides(value, g, to_next, to_prev, base):
    group = value.shape[0] // 3
    store_fold(to_next, base, value[group:, :LANES], value[group:, LANES:])
    store_fold(to_prev, base, value[: 2 * group, :LANES], value[: 2 * group, LANES:])


def neighbours(odd_ref, near_ref, far_ref):
    odd = odd_ref[0] == 1
    near, far = near_ref[...], far_ref[...]
    prev = jnp.where(odd, near, far)
    after = jnp.where(odd, far, near)
    return prev, after


def sides_body(odd, kept, tile, from_prev, from_next, near, far, out_first, out_last, to_next, to_prev):
    group = tile.shape[0] // 3
    own = [own_group(tile, g) for g in range(3)]
    lefts = [load_left(from_prev, group), own, load_left(from_next, group)]
    prev, after = neighbours(odd, near, far)
    first = product([l[:2] for l in lefts], [split(unfold(prev)), own[0]], group)
    first = masked(first, kept, 0)
    out_first[...] = first
    store_sides(first, 0, to_next, to_prev, 0)
    last = product([l[1:] for l in lefts], [own[2], split(unfold(after))], group)
    last = masked(last, kept, 2)
    out_last[...] = last
    store_sides(last, 2, to_next, to_prev, 3 * group)


def middle_body(kept, tile, from_prev, from_next, prev_right, next_left, out, to_next, to_prev):
    group = tile.shape[0] // 3
    own = [own_group(tile, g) for g in range(3)]
    lefts = [load_left(from_prev, group), own, load_left(from_next, group)]
    value = product(lefts, [split(unfold(prev_right[...])), own[1], split(unfold(next_left[...]))], group)
    value = masked(value, kept, 1)
    out[...] = value
    store_sides(value, 1, to_next, to_prev, 0)


def cube_own_body(odd, tile, near, far, prev_right, next_left, first, middle, last, out):
    group = tile.shape[0] // 3
    own = [own_group(tile, g) for g in range(3)]
    prev, after = neighbours(odd, near, far)
    squares = [split(ref[...]) for ref in (first, middle, last)]
    columns = (
        (squares[:2], [split(unfold(prev)), own[0]]),
        (squares, [split(unfold(prev_right[...])), own[1], split(unfold(next_left[...]))]),
        (squares[1:], [own[2], split(unfold(after))]),
    )
    for g, (lefts, rights) in enumerate(columns):
        out[g] = passes(lefts, [right_rows(high, low, 1, group) for high, low in rights])


def add_sides(out, g, total, before, after):
    out[g] = total + jnp.concatenate([before, jnp.zeros_like(before[: before.shape[0] // 2])], 0) + jnp.concatenate(
        [jnp.zeros_like(after[: after.shape[0] // 2]), after], 0
    )


def cube_sides_body(odd, near, far, prev_right, next_left, from_prev, from_next, total, out):
    group = from_prev.shape[0] // 6
    prev, after = neighbours(odd, near, far)
    rights = {
        (0, 0): split(unfold(prev)),
        (0, 1): split(unfold(prev_right[...])),
        (2, 1): split(unfold(next_left[...])),
        (2, 2): split(unfold(after)),
    }
    lefts = {
        (source, kx): split(unfold(ref[at * 3 * group : (at + 1) * 3 * group, :]))
        for source, ref in ((0, from_prev), (2, from_next))
        for at, kx in ((0, 0), (1, 2))
    }
    for g, kxs in ((0, (0,)), (1, (0, 2)), (2, (2,))):
        before, later = (
            passes([lefts[source, kx] for kx in kxs], [right_rows(*rights[kx, g], source, group) for kx in kxs])
            for source in (0, 2)
        )
        add_sides(out, g, total[g], before, later)


def finish_body(kept, tile, from_prev, from_next, first, middle, last, total, out):
    group = tile.shape[0] // 3
    lefts = [split(unfold(ref[...])) for ref in (from_prev, from_next)]
    pieces = []
    for g, square in enumerate((first, middle, last)):
        own = own_group(tile, g)
        before = passes([lefts[0]], [right_rows(*own, 0, group)])
        after = passes([lefts[1]], [right_rows(*own, 2, group)])
        cubed = stacked(total[g], before, after)
        pieces.append(masked(3.0 * square[...] - 2.0 * cubed, kept, g))
    for g, (value, start) in enumerate(zip(pieces, (0, group, 2 * group))):
        out[:, start : start + group] = value[:, :group]


VMEM = pl.BlockSpec(memory_space=pltpu.VMEM)
SMEM = pl.BlockSpec(memory_space=pltpu.SMEM)


def call(body, scalars, arrays, outs, name):
    return pl.pallas_call(
        body,
        out_shape=[jax.ShapeDtypeStruct(shape, F32) for shape in outs],
        in_specs=[SMEM] * len(scalars) + [VMEM] * len(arrays),
        out_specs=[VMEM] * len(outs),
        compiler_params=pltpu.CompilerParams(vmem_limit_bytes=40 << 20),
        name=name,
    )(*scalars, *arrays)


def shifted(block, axis, distance):
    size = lax.axis_size(axis)
    return lax.ppermute(block, axis, [((i - distance) % size, i) for i in range(size)])


def on_device(p_tiles, square_kept, result_kept):
    side = p_tiles.shape[0]
    group = side // 3
    rows = lax.axis_size("row")
    odd = (lax.axis_index("row") % 2).astype(jnp.int32).reshape(1)
    strip = (3 * side // 2, LANES)
    slab = (3 * group, LANES)
    wide = (side, WIDE)

    to_next, to_prev, middle, left, right = call(
        pack_body, (), (p_tiles,), [(9 * group, LANES)] * 2 + [strip] * 3, "pack"
    )
    near = lax.ppermute(middle, "row", [(i, i ^ 1) for i in range(rows)])
    from_prev = shifted(to_next, "col", 1)
    from_next = shifted(to_prev, "col", -1)
    prev_right = shifted(right, "row", 1)
    next_left = shifted(left, "row", -1)
    far = lax.ppermute(near, "row", [(i, (i + (2 if i % 2 == 0 else -2)) % rows) for i in range(rows)])

    first, last, out_next, out_prev = call(
        sides_body,
        (odd, square_kept),
        (p_tiles, from_prev, from_next, near, far),
        [wide] * 2 + [(6 * group, LANES)] * 2,
        "square_sides",
    )
    sides_prev = shifted(out_next, "col", 1)
    sides_next = shifted(out_prev, "col", -1)
    centre, out_next, out_prev = call(
        middle_body,
        (square_kept,),
        (p_tiles, from_prev, from_next, prev_right, next_left),
        [wide] + [slab] * 2,
        "square_middle",
    )
    centre_prev = shifted(out_next, "col", 1)
    centre_next = shifted(out_prev, "col", -1)
    (total,) = call(
        cube_own_body,
        (odd,),
        (p_tiles, near, far, prev_right, next_left, first, centre, last),
        [(3,) + wide],
        "cube_own",
    )
    (total,) = call(
        cube_sides_body,
        (odd,),
        (near, far, prev_right, next_left, sides_prev, sides_next, total),
        [(3,) + wide],
        "cube_sides",
    )
    (purified,) = call(
        finish_body,
        (result_kept,),
        (p_tiles, centre_prev, centre_next, first, centre, last, total),
        [(side, side)],
        "cube_finish",
    )
    return purified


def solution(mesh):
    return jax.shard_map(
        on_device,
        mesh=mesh,
        in_specs=(P("row", "col"), P("row", "col"), P("row", "col")),
        out_specs=P("row", "col"),
        check_vma=False,
    )
```

```python
import jax
import jax.numpy as jnp
from jax import lax
from jax.experimental import pallas as pl
from jax.experimental.pallas import tpu as pltpu
from jax.sharding import PartitionSpec as P

LANES = 128
WIDE = 256
F32 = jnp.float32
BF16 = jnp.bfloat16
NEAR, MID, FAR = range(3)


def low_half(rows):
    return lax.broadcasted_iota(jnp.int32, (rows, LANES), 1) < LANES // 2


def store_fold(out_ref, base, value):
    rows = value.shape[0]
    half = rows // 2
    tail = value[:, LANES:]
    out_ref[pl.ds(base, rows), :] = value[:, :LANES]
    out_ref[pl.ds(base + rows, half), :] = jnp.where(
        low_half(half), tail[:half], pltpu.roll(tail[half:], LANES // 2, 1)
    )


def unfold(packed):
    rows = packed.shape[0] * 2 // 3
    half = rows // 2
    tail = packed[rows:]
    keep = low_half(half)
    upper = jnp.where(keep, tail, 0.0)
    lower = jnp.where(keep, pltpu.roll(tail, LANES // 2, 1), 0.0)
    return jnp.concatenate([packed[:rows], jnp.concatenate([upper, lower], 0)], 1)


def tile_groups(odd_ref, tile_ref):
    rows = tile_ref.shape[0]
    keep = low_half(rows)
    first = jnp.concatenate([tile_ref[:, 0:128], jnp.where(keep, tile_ref[:, 128:256], 0.0)], 1)
    one = pltpu.roll(tile_ref[:, 128:256], LANES // 2, 1)
    two = pltpu.roll(tile_ref[:, 256:384], LANES // 2, 1)
    middle = jnp.concatenate([jnp.where(keep, one, two), jnp.where(keep, two, 0.0)], 1)
    end = tile_ref[:, 512:576]
    last = jnp.concatenate([tile_ref[:, 384:512], jnp.concatenate([end, jnp.zeros_like(end)], 1)], 1)
    odd = odd_ref[0] == 1
    return jnp.where(odd, first, last), middle, jnp.where(odd, last, first)


def split(value):
    high = value.astype(BF16)
    return high, (value - high.astype(F32)).astype(BF16)


def store_left(out_ref, at, value):
    out_ref[(0,) + at], out_ref[(1,) + at] = split(value)


def store_right(out_ref, at, value):
    group = value.shape[0] // 3
    for half, part in enumerate(split(value)):
        for ky in range(3):
            out_ref[(half,) + at + (pl.ds(ky * WIDE, group),)] = part[ky * group : (ky + 1) * group]
            out_ref[(half,) + at + (pl.ds(ky * WIDE + group, WIDE - group),)] = jnp.zeros((WIDE - group, WIDE), BF16)


def left(ref, *at):
    return ref[(0,) + at], ref[(1,) + at]


def right(ref, ky, *at):
    rows = (pl.ds(ky * WIDE, WIDE),)
    return ref[(0,) + at + rows], ref[(1,) + at + rows]


def passes(lefts, rights):
    wide = [high for high, _ in lefts] + [low for _, low in lefts] + [high for high, _ in lefts]
    tall = [high for high, _ in rights] + [high for high, _ in rights] + [low for _, low in rights]
    return jnp.dot(jnp.concatenate(wide, 1), jnp.concatenate(tall, 0), preferred_element_type=F32)


def stacked(before, own, after):
    group = own.shape[0] // 3
    return jnp.concatenate(
        [
            own[:group] + before[:group],
            own[group : 2 * group] + before[group:] + after[:group],
            own[2 * group :] + after[group:],
        ],
        0,
    )


def first_block(odd_ref, part):
    return 3 if part == MID else jnp.where((odd_ref[0] == 1) == (part == NEAR), 0, 6)


def masked(value, kept_ref, start):
    rows = value.shape[0] // 9
    lane = lax.broadcasted_iota(jnp.int32, (8, WIDE), 1)

    def flags(i):
        one, two, three = (kept_ref[i, start + j] for j in range(3))
        return jnp.where(lane < 64, one, jnp.where(lane < 128, two, three)).astype(F32)[:1]

    return jnp.concatenate([value[i * rows : (i + 1) * rows] * flags(i) for i in range(9)], 0)


def store_sides(value, to_next, to_prev):
    group = value.shape[0] // 3
    store_fold(to_next, 0, value[group:])
    store_fold(to_prev, 0, value[: 2 * group])


def pack_body(odd, tile, a_next, a_prev, b_next, b_prev, mid, near, far):
    groups = tile_groups(odd, tile)
    group = tile.shape[0] // 3
    for part, out_next, out_prev, base in (
        (MID, a_next, a_prev, 0),
        (NEAR, a_next, a_prev, 3 * group),
        (FAR, b_next, b_prev, 0),
    ):
        store_fold(out_next, base, groups[part][group:])
        store_fold(out_prev, base, groups[part][: 2 * group])
    for out, part in ((mid, MID), (near, NEAR), (far, FAR)):
        store_fold(out, 0, groups[part])


def prepare_body(odd, tile, own_left, own_right):
    for part, value in enumerate(tile_groups(odd, tile)):
        store_left(own_left, (part,), value)
        store_right(own_right, (part,), value)


def square_near_body(odd, kept, a_prev, a_next, mid, own_left, own_right, out, to_next, to_prev, lefts, rights):
    group = a_prev.shape[0] // 6
    for side, ref in enumerate((a_prev, a_next)):
        for part, base in ((MID, 0), (NEAR, 3 * group)):
            store_left(lefts, (side, part), unfold(ref[base : base + 3 * group, :]))
    store_right(rights, (), unfold(mid[...]))
    sums = []
    for ky in range(3):
        if ky == 1:
            pair = [left(own_left, NEAR), left(own_left, MID)]
        else:
            pair = [left(lefts, ky // 2, NEAR), left(lefts, ky // 2, MID)]
        sums.append(passes(pair, [right(rights, ky), right(own_right, ky, NEAR)]))
    value = masked(stacked(*sums), kept, first_block(odd, NEAR))
    out[...] = value
    store_sides(value, to_next, to_prev)


def square_far_body(odd, kept, b_prev, b_next, mid, own_left, own_right, near_lefts, out, to_next, to_prev, lefts, rights):
    for side, ref in enumerate((b_prev, b_next)):
        store_left(lefts, (side,), unfold(ref[...]))
    store_right(rights, (), unfold(mid[...]))
    sums = []
    for ky in range(3):
        if ky == 1:
            pair = [left(own_left, FAR), left(own_left, MID)]
        else:
            pair = [left(lefts, ky // 2), left(near_lefts, ky // 2, MID)]
        sums.append(passes(pair, [right(rights, ky), right(own_right, ky, FAR)]))
    value = masked(stacked(*sums), kept, first_block(odd, FAR))
    out[...] = value
    store_sides(value, to_next, to_prev)


def square_mid_start_body(near, own_left, own_right, near_lefts, out, rights):
    store_right(rights, (), unfold(near[...]))
    sums = []
    for ky in range(3):
        if ky == 1:
            pair = [left(own_left, NEAR), left(own_left, MID)]
        else:
            pair = [left(near_lefts, ky // 2, NEAR), left(near_lefts, ky // 2, MID)]
        sums.append(passes(pair, [right(rights, ky), right(own_right, ky, MID)]))
    out[...] = stacked(*sums)


def square_mid_body(kept, far, own_left, far_lefts, begun, out, to_next, to_prev, rights):
    store_right(rights, (), unfold(far[...]))
    sums = []
    for ky in range(3):
        one = left(own_left, FAR) if ky == 1 else left(far_lefts, ky // 2)
        sums.append(passes([one], [right(rights, ky)]))
    value = masked(begun[...] + stacked(*sums), kept, 3)
    out[...] = value
    store_sides(value, to_next, to_prev)


def cube_own_body(near, mid, far, own_right, right_near, right_far, right_mid_near, right_mid_far, out):
    squares = [split(ref[...]) for ref in (near, mid, far)]
    out[NEAR] = passes(squares[:2], [right(right_near, 1), right(own_right, 1, NEAR)])
    out[MID] = passes(squares, [right(right_mid_near, 1), right(own_right, 1, MID), right(right_mid_far, 1)])
    out[FAR] = passes(squares[1:], [right(own_right, 1, FAR), right(right_far, 1)])


def cube_side_body(side, from_prev, from_next, right_side, right_mid, total, out):
    lefts = [split(unfold(ref[...])) for ref in (from_prev, from_next)]
    for part, ref in ((side, right_side), (MID, right_mid)):
        before, after = (passes([lefts[k // 2]], [right(ref, k)]) for k in (0, 2))
        out[part] = stacked(before, total[part], after)
    rest = NEAR + FAR - side
    out[rest] = total[rest]


def finish_body(odd, kept, from_prev, from_next, own_right, near, mid, far, total, out):
    group = out.shape[0] // 3
    lefts = [split(unfold(ref[...])) for ref in (from_prev, from_next)]
    values = []
    for part, square in enumerate((near, mid, far)):
        before, after = (passes([lefts[k // 2]], [right(own_right, k, part)]) for k in (0, 2))
        cubed = stacked(before, total[part], after)
        values.append(masked(3.0 * square[...] - 2.0 * cubed, kept, first_block(odd, part)))
    is_odd = odd[0] == 1
    out[:, :group] = jnp.where(is_odd, values[NEAR], values[FAR])[:, :group]
    out[:, group : 2 * group] = values[MID][:, :group]
    out[:, 2 * group :] = jnp.where(is_odd, values[FAR], values[NEAR])[:, :group]


VMEM = pl.BlockSpec(memory_space=pltpu.VMEM)
SMEM = pl.BlockSpec(memory_space=pltpu.SMEM)


def call(body, name, scalars, arrays, outs):
    return pl.pallas_call(
        body,
        out_shape=[jax.ShapeDtypeStruct(shape, kind) for shape, kind in outs],
        in_specs=[SMEM] * len(scalars) + [VMEM] * len(arrays),
        out_specs=[VMEM] * len(outs),
        compiler_params=pltpu.CompilerParams(vmem_limit_bytes=24 << 20),
        name=name,
    )(*scalars, *arrays)


def on_device(p_tiles, square_kept, result_kept):
    side = p_tiles.shape[0]
    group = side // 3
    n_row, n_col = lax.axis_size("row"), lax.axis_size("col")
    odd = (lax.axis_index("row") % 2).astype(jnp.int32).reshape(1)
    strip = ((3 * side // 2, LANES), F32)
    slab = ((3 * group, LANES), F32)
    two_slabs = ((6 * group, LANES), F32)
    wide = ((side, WIDE), F32)
    rights = ((2, 3 * WIDE, WIDE), BF16)

    def from_columns(to_next, to_prev):
        up = [(i, (i + 1) % n_col) for i in range(n_col)]
        down = [(i, (i - 1) % n_col) for i in range(n_col)]
        return lax.ppermute(to_next, "col", up), lax.ppermute(to_prev, "col", down)

    def on_rows(value, even_step):
        return lax.ppermute(
            value, "row", [(i, (i + (even_step if i % 2 == 0 else -even_step)) % n_row) for i in range(n_row)]
        )

    a_next, a_prev, b_next, b_prev, mid, near, far = call(
        pack_body, "pack", (odd,), (p_tiles,), [two_slabs] * 2 + [slab] * 2 + [strip] * 3
    )
    partner_mid = on_rows(mid, 1)
    a_prev, a_next = from_columns(a_next, a_prev)
    b_prev, b_next = from_columns(b_next, b_prev)
    other_mid = on_rows(partner_mid, 2)
    partner_near = on_rows(near, 1)
    other_far = on_rows(far, -1)

    own_left, own_right = call(
        prepare_body, "prepare", (odd,), (p_tiles,), [((2, 3, side, WIDE), BF16), ((2, 3, 3 * WIDE, WIDE), BF16)]
    )
    s_near, out_next, out_prev, near_lefts, right_near = call(
        square_near_body,
        "square_near",
        (odd, square_kept),
        (a_prev, a_next, partner_mid, own_left, own_right),
        [wide, slab, slab, ((2, 2, 2, 2 * group, WIDE), BF16), rights],
    )
    near_prev, near_next = from_columns(out_next, out_prev)
    s_far, out_next, out_prev, far_lefts, right_far = call(
        square_far_body,
        "square_far",
        (odd, square_kept),
        (b_prev, b_next, other_mid, own_left, own_right, near_lefts),
        [wide, slab, slab, ((2, 2, 2 * group, WIDE), BF16), rights],
    )
    far_prev, far_next = from_columns(out_next, out_prev)
    begun, right_mid_near = call(
        square_mid_start_body,
        "square_mid_start",
        (),
        (partner_near, own_left, own_right, near_lefts),
        [wide, rights],
    )
    s_mid, out_next, out_prev, right_mid_far = call(
        square_mid_body,
        "square_mid",
        (square_kept,),
        (other_far, own_left, far_lefts, begun),
        [wide, slab, slab, rights],
    )
    mid_prev, mid_next = from_columns(out_next, out_prev)
    (total,) = call(
        cube_own_body,
        "cube_own",
        (),
        (s_near, s_mid, s_far, own_right, right_near, right_far, right_mid_near, right_mid_far),
        [((3, side, WIDE), F32)],
    )
    for part, prev, after, right_side, right_mid in (
        (NEAR, near_prev, near_next, right_near, right_mid_near),
        (FAR, far_prev, far_next, right_far, right_mid_far),
    ):
        (total,) = call(
            lambda *refs, part=part: cube_side_body(part, *refs),
            ("cube_near", "cube_mid", "cube_far")[part],
            (),
            (prev, after, right_side, right_mid, total),
            [((3, side, WIDE), F32)],
        )
    (purified,) = call(
        finish_body,
        "finish",
        (odd, result_kept),
        (mid_prev, mid_next, own_right, s_near, s_mid, s_far, total),
        [((side, side), F32)],
    )
    return purified


def solution(mesh):
    return jax.shard_map(
        on_device,
        mesh=mesh,
        in_specs=(P("row", "col"), P("row", "col"), P("row", "col")),
        out_specs=P("row", "col"),
        check_vma=False,
    )
```

```python
import jax
import jax.numpy as jnp
from jax import lax
from jax.experimental import pallas as pl
from jax.experimental.pallas import tpu as pltpu
from jax.sharding import PartitionSpec as P

LANES = 128
WIDE = 256
F32 = jnp.float32
BF16 = jnp.bfloat16
NEAR, MID, FAR = range(3)


def low_half(rows):
    return lax.broadcasted_iota(jnp.int32, (rows, LANES), 1) < LANES // 2


def store_fold(out_ref, base, value):
    rows = value.shape[0]
    half = rows // 2
    tail = value[:, LANES:]
    out_ref[pl.ds(base, rows), :] = value[:, :LANES]
    out_ref[pl.ds(base + rows, half), :] = jnp.where(
        low_half(half), tail[:half], pltpu.roll(tail[half:], LANES // 2, 1)
    )


def unfold(packed):
    rows = packed.shape[0] * 2 // 3
    half = rows // 2
    tail = packed[rows:]
    keep = low_half(half)
    upper = jnp.where(keep, tail, 0.0)
    lower = jnp.where(keep, pltpu.roll(tail, LANES // 2, 1), 0.0)
    return jnp.concatenate([packed[:rows], jnp.concatenate([upper, lower], 0)], 1)


def tile_groups(odd_ref, tile_ref):
    rows = tile_ref.shape[0]
    keep = low_half(rows)
    first = jnp.concatenate([tile_ref[:, 0:128], jnp.where(keep, tile_ref[:, 128:256], 0.0)], 1)
    one = pltpu.roll(tile_ref[:, 128:256], LANES // 2, 1)
    two = pltpu.roll(tile_ref[:, 256:384], LANES // 2, 1)
    middle = jnp.concatenate([jnp.where(keep, one, two), jnp.where(keep, two, 0.0)], 1)
    end = tile_ref[:, 512:576]
    last = jnp.concatenate([tile_ref[:, 384:512], jnp.concatenate([end, jnp.zeros_like(end)], 1)], 1)
    odd = odd_ref[0] == 1
    return jnp.where(odd, first, last), middle, jnp.where(odd, last, first)


def split(value):
    high = value.astype(BF16)
    return high, (value - high.astype(F32)).astype(BF16)


def store_left(out_ref, at, value):
    out_ref[(0,) + at], out_ref[(1,) + at] = split(value)


def store_right(out_ref, at, value):
    group = value.shape[0] // 3
    for half, part in enumerate(split(value)):
        for ky in range(3):
            out_ref[(half,) + at + (pl.ds(ky * WIDE, group),)] = part[ky * group : (ky + 1) * group]
            out_ref[(half,) + at + (pl.ds(ky * WIDE + group, WIDE - group),)] = jnp.zeros((WIDE - group, WIDE), BF16)


def left(ref, *at):
    return ref[(0,) + at], ref[(1,) + at]


def right(ref, ky, *at):
    rows = (pl.ds(ky * WIDE, WIDE),)
    return ref[(0,) + at + rows], ref[(1,) + at + rows]


def passes(lefts, rights):
    wide = [high for high, _ in lefts] + [low for _, low in lefts] + [high for high, _ in lefts]
    tall = [high for high, _ in rights] + [high for high, _ in rights] + [low for _, low in rights]
    return jnp.dot(jnp.concatenate(wide, 1), jnp.concatenate(tall, 0), preferred_element_type=F32)


def stacked(before, own, after):
    group = own.shape[0] // 3
    return jnp.concatenate(
        [
            own[:group] + before[:group],
            own[group : 2 * group] + before[group:] + after[:group],
            own[2 * group :] + after[group:],
        ],
        0,
    )


def first_block(odd_ref, part):
    return 3 if part == MID else jnp.where((odd_ref[0] == 1) == (part == NEAR), 0, 6)


def masked(value, kept_ref, start):
    rows = value.shape[0] // 9
    lane = lax.broadcasted_iota(jnp.int32, (8, WIDE), 1)

    def flags(i):
        one, two, three = (kept_ref[i, start + j] for j in range(3))
        return jnp.where(lane < 64, one, jnp.where(lane < 128, two, three)).astype(F32)[:1]

    return jnp.concatenate([value[i * rows : (i + 1) * rows] * flags(i) for i in range(9)], 0)


def store_sides(value, to_next, to_prev):
    group = value.shape[0] // 3
    store_fold(to_next, 0, value[group:])
    store_fold(to_prev, 0, value[: 2 * group])


def pack_body(odd, tile, a_next, a_prev, b_next, b_prev, mid, near, far):
    groups = tile_groups(odd, tile)
    group = tile.shape[0] // 3
    for part, out_next, out_prev, base in (
        (MID, a_next, a_prev, 0),
        (NEAR, a_next, a_prev, 3 * group),
        (FAR, b_next, b_prev, 0),
    ):
        store_fold(out_next, base, groups[part][group:])
        store_fold(out_prev, base, groups[part][: 2 * group])
    for out, part in ((mid, MID), (near, NEAR), (far, FAR)):
        store_fold(out, 0, groups[part])


def prepare_body(odd, tile, own_left, own_right):
    for part, value in enumerate(tile_groups(odd, tile)):
        store_left(own_left, (part,), value)
        store_right(own_right, (part,), value)


def square_near_body(odd, kept, a_prev, a_next, mid, own_left, own_right, out, to_next, to_prev, lefts, rights):
    group = a_prev.shape[0] // 6
    for side, ref in enumerate((a_prev, a_next)):
        for part, base in ((MID, 0), (NEAR, 3 * group)):
            store_left(lefts, (side, part), unfold(ref[base : base + 3 * group, :]))
    store_right(rights, (), unfold(mid[...]))
    sums = []
    for ky in range(3):
        if ky == 1:
            pair = [left(own_left, NEAR), left(own_left, MID)]
        else:
            pair = [left(lefts, ky // 2, NEAR), left(lefts, ky // 2, MID)]
        sums.append(passes(pair, [right(rights, ky), right(own_right, ky, NEAR)]))
    value = masked(stacked(*sums), kept, first_block(odd, NEAR))
    out[...] = value
    store_sides(value, to_next, to_prev)


def square_far_body(odd, kept, b_prev, b_next, mid, own_left, own_right, near_lefts, out, to_next, to_prev, lefts, rights):
    for side, ref in enumerate((b_prev, b_next)):
        store_left(lefts, (side,), unfold(ref[...]))
    store_right(rights, (), unfold(mid[...]))
    sums = []
    for ky in range(3):
        if ky == 1:
            pair = [left(own_left, FAR), left(own_left, MID)]
        else:
            pair = [left(lefts, ky // 2), left(near_lefts, ky // 2, MID)]
        sums.append(passes(pair, [right(rights, ky), right(own_right, ky, FAR)]))
    value = masked(stacked(*sums), kept, first_block(odd, FAR))
    out[...] = value
    store_sides(value, to_next, to_prev)


def square_mid_start_body(near, own_left, own_right, near_lefts, out, rights):
    store_right(rights, (), unfold(near[...]))
    sums = []
    for ky in range(3):
        if ky == 1:
            pair = [left(own_left, NEAR), left(own_left, MID)]
        else:
            pair = [left(near_lefts, ky // 2, NEAR), left(near_lefts, ky // 2, MID)]
        sums.append(passes(pair, [right(rights, ky), right(own_right, ky, MID)]))
    out[...] = stacked(*sums)


def square_mid_body(kept, far, own_left, far_lefts, begun, out, to_next, to_prev, rights):
    store_right(rights, (), unfold(far[...]))
    sums = []
    for ky in range(3):
        one = left(own_left, FAR) if ky == 1 else left(far_lefts, ky // 2)
        sums.append(passes([one], [right(rights, ky)]))
    value = masked(begun[...] + stacked(*sums), kept, 3)
    out[...] = value
    store_sides(value, to_next, to_prev)


def cube_near_body(from_prev, from_next, s_near, s_far, own_right, right_near, right_far, right_mid, out):
    lefts = [split(unfold(ref[...])) for ref in (from_prev, from_next)]
    near, far = split(s_near[...]), split(s_far[...])
    out[FAR] = passes([far], [right(right_far, 1)])
    for part, ref, own in (
        (NEAR, right_near, passes([near], [right(right_near, 1)])),
        (MID, right_mid, passes([near], [right(right_mid, 1)])),
    ):
        before, after = (passes([lefts[k // 2]], [right(ref, k)]) for k in (0, 2))
        out[part] = stacked(before, own, after)


def cube_own_body(total, near, mid, far, own_right, right_mid_far, out):
    squares = [split(ref[...]) for ref in (near, mid, far)]
    rights = [right(own_right, 1, part) for part in range(3)]
    out[NEAR] = 3.0 * near[...] - 2.0 * (total[NEAR] + passes(squares[1:2], rights[NEAR:MID]))
    out[MID] = 3.0 * mid[...] - 2.0 * (total[MID] + passes(squares[1:], [rights[MID], right(right_mid_far, 1)]))
    out[FAR] = 3.0 * far[...] - 2.0 * (total[FAR] + passes(squares[1:2], rights[FAR:]))


def cube_far_body(from_prev, from_next, right_far, right_mid, base, out):
    lefts = [split(unfold(ref[...])) for ref in (from_prev, from_next)]
    out[NEAR] = base[NEAR]
    for part, ref in ((FAR, right_far), (MID, right_mid)):
        before, after = (-2.0 * passes([lefts[k // 2]], [right(ref, k)]) for k in (0, 2))
        out[part] = stacked(before, base[part], after)


def finish_body(odd, kept, from_prev, from_next, own_right, base, out):
    group = out.shape[0] // 3
    lefts = [split(unfold(ref[...])) for ref in (from_prev, from_next)]
    values = []
    for part in range(3):
        before, after = (-2.0 * passes([lefts[k // 2]], [right(own_right, k, part)]) for k in (0, 2))
        values.append(masked(stacked(before, base[part], after), kept, first_block(odd, part)))
    is_odd = odd[0] == 1
    out[:, :group] = jnp.where(is_odd, values[NEAR], values[FAR])[:, :group]
    out[:, group : 2 * group] = values[MID][:, :group]
    out[:, 2 * group :] = jnp.where(is_odd, values[FAR], values[NEAR])[:, :group]


VMEM = pl.BlockSpec(memory_space=pltpu.VMEM)
SMEM = pl.BlockSpec(memory_space=pltpu.SMEM)


def call(body, name, scalars, arrays, outs):
    return pl.pallas_call(
        body,
        out_shape=[jax.ShapeDtypeStruct(shape, kind) for shape, kind in outs],
        in_specs=[SMEM] * len(scalars) + [VMEM] * len(arrays),
        out_specs=[VMEM] * len(outs),
        compiler_params=pltpu.CompilerParams(vmem_limit_bytes=24 << 20),
        cost_estimate=pl.CostEstimate(flops=2000000000, transcendentals=0, bytes_accessed=10000000),
        name=name,
    )(*scalars, *arrays)


def on_device(p_tiles, square_kept, result_kept):
    side = p_tiles.shape[0]
    group = side // 3
    n_row, n_col = lax.axis_size("row"), lax.axis_size("col")
    odd = (lax.axis_index("row") % 2).astype(jnp.int32).reshape(1)
    strip = ((3 * side // 2, LANES), F32)
    slab = ((3 * group, LANES), F32)
    two_slabs = ((6 * group, LANES), F32)
    wide = ((side, WIDE), F32)
    rights = ((2, 3 * WIDE, WIDE), BF16)

    def from_columns(to_next, to_prev):
        up = [(i, (i + 1) % n_col) for i in range(n_col)]
        down = [(i, (i - 1) % n_col) for i in range(n_col)]
        return lax.ppermute(to_next, "col", up), lax.ppermute(to_prev, "col", down)

    def on_rows(value, even_step):
        return lax.ppermute(
            value, "row", [(i, (i + (even_step if i % 2 == 0 else -even_step)) % n_row) for i in range(n_row)]
        )

    a_next, a_prev, b_next, b_prev, mid, near, far = call(
        pack_body, "pack", (odd,), (p_tiles,), [two_slabs] * 2 + [slab] * 2 + [strip] * 3
    )
    partner_mid = on_rows(mid, 1)
    a_prev, a_next = from_columns(a_next, a_prev)
    b_prev, b_next = from_columns(b_next, b_prev)
    other_mid = on_rows(partner_mid, 2)
    partner_near = on_rows(near, 1)

    own_left, own_right = call(
        prepare_body, "prepare", (odd,), (p_tiles,), [((2, 3, side, WIDE), BF16), ((2, 3, 3 * WIDE, WIDE), BF16)]
    )
    s_near, out_next, out_prev, near_lefts, right_near = call(
        square_near_body,
        "square_near",
        (odd, square_kept),
        (a_prev, a_next, partner_mid, own_left, own_right),
        [wide, slab, slab, ((2, 2, 2, 2 * group, WIDE), BF16), rights],
    )
    near_prev, near_next = from_columns(out_next, out_prev)
    other_mid, far, near_lefts = lax.optimization_barrier((other_mid, far, near_lefts))
    other_far = on_rows(far, -1)
    s_far, out_next, out_prev, far_lefts, right_far = call(
        square_far_body,
        "square_far",
        (odd, square_kept),
        (b_prev, b_next, other_mid, own_left, own_right, near_lefts),
        [wide, slab, slab, ((2, 2, 2 * group, WIDE), BF16), rights],
    )
    far_prev, far_next = from_columns(out_next, out_prev)
    begun, right_mid_near = call(
        square_mid_start_body,
        "square_mid_start",
        (),
        (partner_near, own_left, own_right, near_lefts),
        [wide, rights],
    )
    (total,) = call(
        cube_near_body,
        "cube_near",
        (),
        (near_prev, near_next, s_near, s_far, own_right, right_near, right_far, right_mid_near),
        [((3, side, WIDE), F32)],
    )
    total, other_far = lax.optimization_barrier((total, other_far))
    s_mid, out_next, out_prev, right_mid_far = call(
        square_mid_body,
        "square_mid",
        (square_kept,),
        (other_far, own_left, far_lefts, begun),
        [wide, slab, slab, rights],
    )
    mid_prev, mid_next = from_columns(out_next, out_prev)
    (base,) = call(
        cube_own_body,
        "cube_own",
        (),
        (total, s_near, s_mid, s_far, own_right, right_mid_far),
        [((3, side, WIDE), F32)],
    )
    (base,) = call(
        cube_far_body,
        "cube_far",
        (),
        (far_prev, far_next, right_far, right_mid_far, base),
        [((3, side, WIDE), F32)],
    )
    (purified,) = call(
        finish_body,
        "finish",
        (odd, result_kept),
        (mid_prev, mid_next, own_right, base),
        [((side, side), F32)],
    )
    return purified


def solution(mesh):
    return jax.shard_map(
        on_device,
        mesh=mesh,
        in_specs=(P("row", "col"), P("row", "col"), P("row", "col")),
        out_specs=P("row", "col"),
        check_vma=False,
    )
```

```python
import jax
import jax.numpy as jnp
from jax import lax
from jax.experimental import pallas as pl
from jax.experimental.pallas import tpu as pltpu
from jax.sharding import PartitionSpec as P

LANES = 128
WIDE = 256
F32 = jnp.float32
BF16 = jnp.bfloat16
NEAR, MID, FAR = range(3)
OWN, CHIP, LINK = range(3)


def place(info, who, group):
    above = (info[1] == 1) == (who == CHIP)
    return jnp.where(above, 0, group), jnp.where(above, 0, 2)


def shared_rows(info, who, group):
    return pl.ds(pl.multiple_of(place(info, who, group)[0], 64), 2 * group)


def low_half(rows):
    return lax.broadcasted_iota(jnp.int32, (rows, LANES), 1) < LANES // 2


def store_fold(out_ref, base, value):
    rows = value.shape[0]
    half = rows // 2
    tail = value[:, LANES:]
    out_ref[pl.ds(base, rows), :] = value[:, :LANES]
    out_ref[pl.ds(base + rows, half), :] = jnp.where(
        low_half(half), tail[:half], pltpu.roll(tail[half:], LANES // 2, 1)
    )


def unfold(packed):
    rows = packed.shape[0] * 2 // 3
    half = rows // 2
    tail = packed[rows:]
    keep = low_half(half)
    upper = jnp.where(keep, tail, 0.0)
    lower = jnp.where(keep, pltpu.roll(tail, LANES // 2, 1), 0.0)
    return jnp.concatenate([packed[:rows], jnp.concatenate([upper, lower], 0)], 1)


def tile_groups(info, tile_ref, at):
    keep = low_half(at.size)
    first = jnp.concatenate([tile_ref[at, 0:128], jnp.where(keep, tile_ref[at, 128:256], 0.0)], 1)
    one = pltpu.roll(tile_ref[at, 128:256], LANES // 2, 1)
    two = pltpu.roll(tile_ref[at, 256:384], LANES // 2, 1)
    middle = jnp.concatenate([jnp.where(keep, one, two), jnp.where(keep, two, 0.0)], 1)
    end = tile_ref[at, 512:576]
    last = jnp.concatenate([tile_ref[at, 384:512], jnp.concatenate([end, jnp.zeros_like(end)], 1)], 1)
    odd = info[0] == 1
    return jnp.where(odd, first, last), middle, jnp.where(odd, last, first)


def split(value):
    high = value.astype(BF16)
    return high, (value - high.astype(F32)).astype(BF16)


def store_left(out_ref, at, value):
    out_ref[(0,) + at], out_ref[(1,) + at] = split(value)


def store_right(out_ref, at, value):
    group = value.shape[0] // 3
    for half, part in enumerate(split(value)):
        for ky in range(3):
            out_ref[(half,) + at + (pl.ds(ky * WIDE, group),)] = part[ky * group : (ky + 1) * group]
            out_ref[(half,) + at + (pl.ds(ky * WIDE + group, WIDE - group),)] = jnp.zeros((WIDE - group, WIDE), BF16)


def left(ref, *at):
    return ref[(0,) + at], ref[(1,) + at]


def right(ref, info, who, *at):
    start = WIDE if who == OWN else pl.multiple_of(place(info, who, 0)[1] * WIDE, WIDE)
    rows = (pl.ds(start, WIDE),)
    return ref[(0,) + at + rows], ref[(1,) + at + rows]


def passes(lefts, rights):
    wide = [high for high, _ in lefts] + [low for _, low in lefts] + [high for high, _ in lefts]
    tall = [high for high, _ in rights] + [high for high, _ in rights] + [low for _, low in rights]
    return jnp.dot(jnp.concatenate(wide, 1), jnp.concatenate(tall, 0), preferred_element_type=F32)


def mask_at(info, part):
    return 3 if part == MID else jnp.where((info[0] == 1) == (part == NEAR), 0, 6)


def masked(value, kept_ref, start, first_row=0):
    lane = lax.broadcasted_iota(jnp.int32, (8, WIDE), 1)

    def flags(i):
        one, two, three = (kept_ref[first_row + i, start + j] for j in range(3))
        return jnp.where(lane < 64, one, jnp.where(lane < 128, two, three)).astype(F32)[:1]

    return jnp.concatenate([value[i * 64 : (i + 1) * 64] * flags(i) for i in range(value.shape[0] // 64)], 0)


def pack_body(info, tile, chip, link_a, link_b, mid, near, far):
    side = tile.shape[0]
    group = side // 3
    groups = tile_groups(info, tile, shared_rows(info, LINK, group))
    store_fold(link_a, 0, groups[MID])
    store_fold(link_a, 3 * group, groups[NEAR])
    store_fold(link_b, 0, groups[FAR])
    groups = tile_groups(info, tile, pl.ds(0, side))
    for out, part in ((mid, MID), (near, NEAR), (far, FAR)):
        store_fold(out, 0, groups[part])
    groups = tile_groups(info, tile, shared_rows(info, CHIP, group))
    for part in range(3):
        store_fold(chip, part * 3 * group, groups[part])


def prepare_body(info, tile, chip, own_left, own_right, chip_left):
    side = tile.shape[0]
    for part, value in enumerate(tile_groups(info, tile, pl.ds(0, side))):
        store_left(own_left, (part,), value)
        store_right(own_right, (part,), value)
        store_left(chip_left, (part,), unfold(chip[part * side : (part + 1) * side, :]))


def near_start_body(info, mid, own_left, own_right, chip_left, out, rights):
    group = mid.shape[0] * 2 // 9
    store_right(rights, (), unfold(mid[...]))
    for who, lefts in ((OWN, own_left), (CHIP, chip_left)):
        value = passes(
            [left(lefts, NEAR), left(lefts, MID)], [right(rights, info, who), right(own_right, info, who, NEAR)]
        )
        if who == OWN:
            out[...] = value
        else:
            out[shared_rows(info, who, group), :] += value


def near_body(info, kept, link_a, begun, own_right, right_near, out, link, link_left):
    group = link_a.shape[0] // 6
    for part, base in ((MID, 0), (NEAR, 3 * group)):
        store_left(link_left, (part,), unfold(link_a[base : base + 3 * group, :]))
    out[...] = begun[...]
    out[shared_rows(info, LINK, group), :] += passes(
        [left(link_left, NEAR), left(link_left, MID)],
        [right(right_near, info, LINK), right(own_right, info, LINK, NEAR)],
    )
    out[...] = masked(out[...], kept, mask_at(info, NEAR))
    store_fold(link, 0, out[shared_rows(info, LINK, group), :])


def far_start_body(info, own_left, own_right, chip_left, link_left, out):
    group = out.shape[0] // 3
    for who, lefts in ((OWN, own_left), (CHIP, chip_left), (LINK, link_left)):
        value = passes([left(lefts, MID)], [right(own_right, info, who, FAR)])
        if who == OWN:
            out[...] = value
        else:
            out[shared_rows(info, who, group), :] += value


def far_body(info, kept, link_b, mid, begun, near, own_left, chip_left, out, chip, link, link_left, rights):
    group = out.shape[0] // 3
    store_left(link_left, (), unfold(link_b[...]))
    store_right(rights, (), unfold(mid[...]))
    out[...] = begun[...] + passes([left(own_left, FAR)], [right(rights, info, OWN)])
    for who, factor in ((CHIP, left(chip_left, FAR)), (LINK, left(link_left))):
        out[shared_rows(info, who, group), :] += passes([factor], [right(rights, info, who)])
    out[...] = masked(out[...], kept, mask_at(info, FAR))
    store_fold(link, 0, out[shared_rows(info, LINK, group), :])
    store_fold(chip, 0, near[shared_rows(info, CHIP, group), :])
    store_fold(chip, 3 * group, out[shared_rows(info, CHIP, group), :])


def mid_start_body(info, near, own_left, own_right, chip_left, link_left, out, rights):
    group = out.shape[0] // 3
    store_right(rights, (), unfold(near[...]))
    for who, lefts in ((OWN, own_left), (CHIP, chip_left), (LINK, link_left)):
        value = passes(
            [left(lefts, NEAR), left(lefts, MID)], [right(rights, info, who), right(own_right, info, who, MID)]
        )
        if who == OWN:
            out[...] = value
        else:
            out[shared_rows(info, who, group), :] += value


def mid_body(info, kept, far, own_left, chip_left, link_left, begun, out, chip, link, rights):
    group = out.shape[0] // 3
    store_right(rights, (), unfold(far[...]))
    out[...] = begun[...] + passes([left(own_left, FAR)], [right(rights, info, OWN)])
    for who, factor in ((CHIP, left(chip_left, FAR)), (LINK, left(link_left))):
        out[shared_rows(info, who, group), :] += passes([factor], [right(rights, info, who)])
    out[...] = masked(out[...], kept, 3)
    store_fold(link, 0, out[shared_rows(info, LINK, group), :])
    store_fold(chip, 0, out[shared_rows(info, CHIP, group), :])


def cube_near_body(info, link, near, right_near, right_mid, out):
    group = near.shape[0] // 3
    own, other = split(near[...]), split(unfold(link[...]))
    out[FAR] = jnp.zeros(near.shape, F32)
    for part, ref in ((NEAR, right_near), (MID, right_mid)):
        out[part] = passes([own], [right(ref, info, OWN)])
        out[part, shared_rows(info, LINK, group), :] += passes([other], [right(ref, info, LINK)])


def cube_own_body(info, chip, total, near, mid, far, own_right, right_near, right_far, mid_near, mid_far, out):
    group = near.shape[0] // 3
    own_mid, own_far = split(mid[...]), split(far[...])
    chip_near, chip_far = (split(unfold(chip[at * 3 * group : (at + 1) * 3 * group, :])) for at in range(2))

    def add(part, square, own, other):
        out[part] = 3.0 * square[...] - 2.0 * (total[part] + passes(*own))
        out[part, shared_rows(info, CHIP, group), :] -= 2.0 * passes(*other)

    add(
        NEAR,
        near,
        ([own_mid], [right(own_right, info, OWN, NEAR)]),
        ([chip_near], [right(right_near, info, CHIP)]),
    )
    add(
        MID,
        mid,
        ([own_mid, own_far], [right(own_right, info, OWN, MID), right(mid_far, info, OWN)]),
        ([chip_near, chip_far], [right(mid_near, info, CHIP), right(mid_far, info, CHIP)]),
    )
    add(
        FAR,
        far,
        ([own_mid, own_far], [right(own_right, info, OWN, FAR), right(right_far, info, OWN)]),
        ([chip_far], [right(right_far, info, CHIP)]),
    )


def cube_far_body(info, kept, link, chip, own_right, right_far, mid_far, base, out):
    group = base.shape[1] // 3
    link_far, chip_mid = split(unfold(link[...])), split(unfold(chip[...]))
    out[...] = base[...]
    for part in range(3):
        out[part, shared_rows(info, CHIP, group), :] -= 2.0 * passes(
            [chip_mid], [right(own_right, info, CHIP, part)]
        )
    for part, ref in ((MID, mid_far), (FAR, right_far)):
        out[part, shared_rows(info, LINK, group), :] -= 2.0 * passes([link_far], [right(ref, info, LINK)])
    for part in range(3):
        out[part] = masked(out[part], kept, mask_at(info, part))


def finish_body(info, kept, link, own_right, base, out):
    group = out.shape[0] // 3
    link_mid = split(unfold(link[...]))
    at = shared_rows(info, LINK, group)
    first_row = place(info, LINK, 3)[0]
    values = []
    for part in range(3):
        value = -2.0 * passes([link_mid], [right(own_right, info, LINK, part)])
        values.append(base[part, at, :] + masked(value, kept, mask_at(info, part), first_row))
    odd = info[0] == 1

    def store(rows, near, mid, far):
        out[rows, :group] = jnp.where(odd, near, far)[:, :group]
        out[rows, group : 2 * group] = mid[:, :group]
        out[rows, 2 * group :] = jnp.where(odd, far, near)[:, :group]

    store(at, *values)
    rest = pl.ds(pl.multiple_of(2 * place(info, CHIP, group)[0], 64), group)
    store(rest, *(base[part, rest, :] for part in range(3)))


VMEM = pl.BlockSpec(memory_space=pltpu.VMEM)
SMEM = pl.BlockSpec(memory_space=pltpu.SMEM)


def call(body, name, scalars, arrays, outs):
    return pl.pallas_call(
        body,
        out_shape=[jax.ShapeDtypeStruct(shape, kind) for shape, kind in outs],
        in_specs=[SMEM] * len(scalars) + [VMEM] * len(arrays),
        out_specs=[VMEM] * len(outs),
        compiler_params=pltpu.CompilerParams(vmem_limit_bytes=24 << 20),
        cost_estimate=pl.CostEstimate(flops=4000000000, transcendentals=0, bytes_accessed=20000000),
        name=name,
    )(*scalars, *arrays)


def on_device(p_tiles, square_kept, result_kept):
    side = p_tiles.shape[0]
    group = side // 3
    n_row, n_col = lax.axis_size("row"), lax.axis_size("col")
    info = jnp.stack([lax.axis_index("row") % 2, lax.axis_index("col") % 2]).astype(jnp.int32)
    strip = ((3 * side // 2, LANES), F32)
    slab = ((3 * group, LANES), F32)
    two_slabs = ((6 * group, LANES), F32)
    three_slabs = ((9 * group, LANES), F32)
    wide = ((side, WIDE), F32)
    three_wide = ((3, side, WIDE), F32)
    rights = ((2, 3 * WIDE, WIDE), BF16)

    def exchange(value, axis, even_step):
        size = n_row if axis == "row" else n_col
        return lax.ppermute(
            value, axis, [(i, (i + (even_step if i % 2 == 0 else -even_step)) % size) for i in range(size)]
        )

    chip, link_a, link_b, mid, near, far = call(
        pack_body, "pack", (info,), (p_tiles,), [three_slabs, two_slabs, slab] + [strip] * 3
    )
    link_a = exchange(link_a, "col", -1)
    partner_mid = exchange(mid, "row", 1)
    chip = exchange(chip, "col", 1)
    chip, link_b, near = lax.optimization_barrier((chip, link_b, near))
    link_b = exchange(link_b, "col", -1)
    partner_near = exchange(near, "row", 1)
    other_mid = exchange(partner_mid, "row", 2)

    own_left, own_right, chip_left = call(
        prepare_body,
        "prepare",
        (info,),
        (p_tiles, chip),
        [((2, 3, side, WIDE), BF16), ((2, 3, 3 * WIDE, WIDE), BF16), ((2, 3, 2 * group, WIDE), BF16)],
    )
    begun, right_near = call(
        near_start_body, "near_start", (info,), (partner_mid, own_left, own_right, chip_left), [wide, rights]
    )
    s_near, near_link, link_left = call(
        near_body,
        "square_near",
        (info, square_kept),
        (link_a, begun, own_right, right_near),
        [wide, slab, ((2, 2, 2 * group, WIDE), BF16)],
    )
    near_link = exchange(near_link, "col", -1)
    (begun,) = call(
        far_start_body, "far_start", (info,), (own_left, own_right, chip_left, link_left), [wide]
    )
    other_mid, far, begun = lax.optimization_barrier((other_mid, far, begun))
    other_far = exchange(far, "row", -1)
    s_far, sides_chip, far_link, link_left_far, right_far = call(
        far_body,
        "square_far",
        (info, square_kept),
        (link_b, other_mid, begun, s_near, own_left, chip_left),
        [wide, two_slabs, slab, ((2, 2 * group, WIDE), BF16), rights],
    )
    far_link = exchange(far_link, "col", -1)
    sides_chip = exchange(sides_chip, "col", 1)
    begun, mid_near = call(
        mid_start_body,
        "mid_start",
        (info,),
        (partner_near, own_left, own_right, chip_left, link_left),
        [wide, rights],
    )
    (total,) = call(cube_near_body, "cube_near", (info,), (near_link, s_near, right_near, mid_near), [three_wide])
    total, other_far = lax.optimization_barrier((total, other_far))
    s_mid, mid_chip, mid_link, mid_far = call(
        mid_body,
        "square_mid",
        (info, square_kept),
        (other_far, own_left, chip_left, link_left_far, begun),
        [wide, slab, slab, rights],
    )
    mid_link = exchange(mid_link, "col", -1)
    mid_chip = exchange(mid_chip, "col", 1)
    (base,) = call(
        cube_own_body,
        "cube_own",
        (info,),
        (sides_chip, total, s_near, s_mid, s_far, own_right, right_near, right_far, mid_near, mid_far),
        [three_wide],
    )
    (base,) = call(
        cube_far_body,
        "cube_far",
        (info, result_kept),
        (far_link, mid_chip, own_right, right_far, mid_far, base),
        [three_wide],
    )
    (purified,) = call(
        finish_body, "finish", (info, result_kept), (mid_link, own_right, base), [((side, side), F32)]
    )
    return purified


def solution(mesh):
    return jax.shard_map(
        on_device,
        mesh=mesh,
        in_specs=(P("row", "col"), P("row", "col"), P("row", "col")),
        out_specs=P("row", "col"),
        check_vma=False,
    )
```

```python
import jax
import jax.numpy as jnp
from jax import lax
from jax.experimental import pallas as pl
from jax.experimental.pallas import tpu as pltpu
from jax.sharding import PartitionSpec as P

LANES = 128
WIDE = 256
F32 = jnp.float32
BF16 = jnp.bfloat16
NEAR, MID, FAR = range(3)
OWN, CHIP, LINK = range(3)


def place(info, who, group):
    above = (info[1] == 1) == (who == CHIP)
    return jnp.where(above, 0, group), jnp.where(above, 0, 2)


def shared_rows(info, who, group):
    return pl.ds(pl.multiple_of(place(info, who, group)[0], 64), 2 * group)


def low_half(rows):
    return lax.broadcasted_iota(jnp.int32, (rows, LANES), 1) < LANES // 2


def store_fold(out_ref, base, value):
    rows = value.shape[0]
    half = rows // 2
    tail = value[:, LANES:]
    out_ref[pl.ds(base, rows), :] = value[:, :LANES]
    out_ref[pl.ds(base + rows, half), :] = jnp.where(
        low_half(half), tail[:half], pltpu.roll(tail[half:], LANES // 2, 1)
    )


def unfold(packed):
    rows = packed.shape[0] * 2 // 3
    half = rows // 2
    tail = packed[rows:]
    keep = low_half(half)
    upper = jnp.where(keep, tail, 0.0)
    lower = jnp.where(keep, pltpu.roll(tail, LANES // 2, 1), 0.0)
    return jnp.concatenate([packed[:rows], jnp.concatenate([upper, lower], 0)], 1)


def tile_groups(info, tile_ref, at):
    keep = low_half(at.size)
    first = jnp.concatenate([tile_ref[at, 0:128], jnp.where(keep, tile_ref[at, 128:256], 0.0)], 1)
    one = pltpu.roll(tile_ref[at, 128:256], LANES // 2, 1)
    two = pltpu.roll(tile_ref[at, 256:384], LANES // 2, 1)
    middle = jnp.concatenate([jnp.where(keep, one, two), jnp.where(keep, two, 0.0)], 1)
    end = tile_ref[at, 512:576]
    last = jnp.concatenate([tile_ref[at, 384:512], jnp.concatenate([end, jnp.zeros_like(end)], 1)], 1)
    odd = info[0] == 1
    return jnp.where(odd, first, last), middle, jnp.where(odd, last, first)


def split(value):
    high = value.astype(BF16)
    return high, (value - high.astype(F32)).astype(BF16)


def store_left(out_ref, at, value):
    out_ref[(0,) + at], out_ref[(1,) + at] = split(value)


def store_right(out_ref, at, value):
    group = value.shape[0] // 3
    for half, part in enumerate(split(value)):
        for ky in range(3):
            out_ref[(half,) + at + (pl.ds(ky * WIDE, group),)] = part[ky * group : (ky + 1) * group]
            out_ref[(half,) + at + (pl.ds(ky * WIDE + group, WIDE - group),)] = jnp.zeros((WIDE - group, WIDE), BF16)


def left(ref, *at):
    return ref[(0,) + at], ref[(1,) + at]


def right(ref, info, who, *at):
    start = WIDE if who == OWN else pl.multiple_of(place(info, who, 0)[1] * WIDE, WIDE)
    rows = (pl.ds(start, WIDE),)
    return ref[(0,) + at + rows], ref[(1,) + at + rows]


def passes(lefts, rights):
    wide = [high for high, _ in lefts] + [low for _, low in lefts] + [high for high, _ in lefts]
    tall = [high for high, _ in rights] + [high for high, _ in rights] + [low for _, low in rights]
    return jnp.dot(jnp.concatenate(wide, 1), jnp.concatenate(tall, 0), preferred_element_type=F32)


def mask_at(info, part):
    return 3 if part == MID else jnp.where((info[0] == 1) == (part == NEAR), 0, 6)


def masked(value, kept_ref, start, first_row=0):
    lane = lax.broadcasted_iota(jnp.int32, (8, WIDE), 1)

    def flags(i):
        one, two, three = (kept_ref[first_row + i, start + j] for j in range(3))
        return jnp.where(lane < 64, one, jnp.where(lane < 128, two, three)).astype(F32)[:1]

    return jnp.concatenate([value[i * 64 : (i + 1) * 64] * flags(i) for i in range(value.shape[0] // 64)], 0)


def pack_body(info, tile, chip, link_a, link_b, mid, near, far):
    side = tile.shape[0]
    group = side // 3
    groups = tile_groups(info, tile, shared_rows(info, LINK, group))
    store_fold(link_a, 0, groups[MID])
    store_fold(link_a, 3 * group, groups[NEAR])
    store_fold(link_b, 0, groups[FAR])
    groups = tile_groups(info, tile, pl.ds(0, side))
    for out, part in ((mid, MID), (near, NEAR), (far, FAR)):
        store_fold(out, 0, groups[part])
    groups = tile_groups(info, tile, shared_rows(info, CHIP, group))
    for part in range(3):
        store_fold(chip, part * 3 * group, groups[part])


def prepare_body(info, tile, chip, own_left, own_right, chip_left):
    side = tile.shape[0]
    for part, value in enumerate(tile_groups(info, tile, pl.ds(0, side))):
        store_left(own_left, (part,), value)
        store_right(own_right, (part,), value)
        store_left(chip_left, (part,), unfold(chip[part * side : (part + 1) * side, :]))


def near_start_body(info, mid, own_left, own_right, chip_left, out, rights):
    group = mid.shape[0] * 2 // 9
    store_right(rights, (), unfold(mid[...]))
    for who, lefts in ((OWN, own_left), (CHIP, chip_left)):
        value = passes(
            [left(lefts, NEAR), left(lefts, MID)], [right(rights, info, who), right(own_right, info, who, NEAR)]
        )
        if who == OWN:
            out[...] = value
        else:
            out[shared_rows(info, who, group), :] += value


def near_body(info, kept, link_a, begun, own_right, right_near, out, link, link_left):
    group = link_a.shape[0] // 6
    for part, base in ((MID, 0), (NEAR, 3 * group)):
        store_left(link_left, (part,), unfold(link_a[base : base + 3 * group, :]))
    out[...] = begun[...]
    out[shared_rows(info, LINK, group), :] += passes(
        [left(link_left, NEAR), left(link_left, MID)],
        [right(right_near, info, LINK), right(own_right, info, LINK, NEAR)],
    )
    out[...] = masked(out[...], kept, mask_at(info, NEAR))
    store_fold(link, 0, out[shared_rows(info, LINK, group), :])


def far_start_body(info, own_left, own_right, chip_left, link_left, out):
    group = out.shape[0] // 3
    for who, lefts in ((OWN, own_left), (CHIP, chip_left), (LINK, link_left)):
        value = passes([left(lefts, MID)], [right(own_right, info, who, FAR)])
        if who == OWN:
            out[...] = value
        else:
            out[shared_rows(info, who, group), :] += value


def far_body(info, kept, link_b, mid, begun, near, own_left, chip_left, out, chip, link, link_left, rights):
    group = out.shape[0] // 3
    store_left(link_left, (), unfold(link_b[...]))
    store_right(rights, (), unfold(mid[...]))
    out[...] = begun[...] + passes([left(own_left, FAR)], [right(rights, info, OWN)])
    for who, factor in ((CHIP, left(chip_left, FAR)), (LINK, left(link_left))):
        out[shared_rows(info, who, group), :] += passes([factor], [right(rights, info, who)])
    out[...] = masked(out[...], kept, mask_at(info, FAR))
    store_fold(link, 0, out[shared_rows(info, LINK, group), :])
    store_fold(chip, 0, near[shared_rows(info, CHIP, group), :])
    store_fold(chip, 3 * group, out[shared_rows(info, CHIP, group), :])


def mid_start_body(info, near, own_left, own_right, chip_left, link_left, out, rights):
    group = out.shape[0] // 3
    store_right(rights, (), unfold(near[...]))
    for who, lefts in ((OWN, own_left), (CHIP, chip_left), (LINK, link_left)):
        value = passes(
            [left(lefts, NEAR), left(lefts, MID)], [right(rights, info, who), right(own_right, info, who, MID)]
        )
        if who == OWN:
            out[...] = value
        else:
            out[shared_rows(info, who, group), :] += value


def mid_body(info, kept, far, own_left, chip_left, link_left, begun, out, chip, link, rights):
    group = out.shape[0] // 3
    store_right(rights, (), unfold(far[...]))
    out[...] = begun[...] + passes([left(own_left, FAR)], [right(rights, info, OWN)])
    for who, factor in ((CHIP, left(chip_left, FAR)), (LINK, left(link_left))):
        out[shared_rows(info, who, group), :] += passes([factor], [right(rights, info, who)])
    out[...] = masked(out[...], kept, 3)
    store_fold(link, 0, out[shared_rows(info, LINK, group), :])
    store_fold(chip, 0, out[shared_rows(info, CHIP, group), :])


def cube_near_body(info, link, near, right_near, right_mid, out):
    group = near.shape[0] // 3
    own, other = split(near[...]), split(unfold(link[...]))
    out[FAR] = jnp.zeros(near.shape, F32)
    for part, ref in ((NEAR, right_near), (MID, right_mid)):
        out[part] = passes([own], [right(ref, info, OWN)])
        out[part, shared_rows(info, LINK, group), :] += passes([other], [right(ref, info, LINK)])


def cube_own_body(info, chip, link, total, near, mid, far, own_right, right_near, right_far, mid_near, mid_far, out):
    group = near.shape[0] // 3
    own_mid, own_far = split(mid[...]), split(far[...])
    chip_near, chip_far = (split(unfold(chip[at * 3 * group : (at + 1) * 3 * group, :])) for at in range(2))
    link_far = split(unfold(link[...]))

    def add(part, square, own, from_chip, from_link):
        out[part] = 3.0 * square[...] - 2.0 * (total[part] + passes(*own))
        out[part, shared_rows(info, CHIP, group), :] -= 2.0 * passes(*from_chip)
        if from_link is not None:
            out[part, shared_rows(info, LINK, group), :] -= 2.0 * passes([link_far], [from_link])

    add(
        NEAR,
        near,
        ([own_mid], [right(own_right, info, OWN, NEAR)]),
        ([chip_near], [right(right_near, info, CHIP)]),
        None,
    )
    add(
        MID,
        mid,
        ([own_mid, own_far], [right(own_right, info, OWN, MID), right(mid_far, info, OWN)]),
        ([chip_near, chip_far], [right(mid_near, info, CHIP), right(mid_far, info, CHIP)]),
        right(mid_far, info, LINK),
    )
    add(
        FAR,
        far,
        ([own_mid, own_far], [right(own_right, info, OWN, FAR), right(right_far, info, OWN)]),
        ([chip_far], [right(right_far, info, CHIP)]),
        right(right_far, info, LINK),
    )


def cube_chip_body(info, kept, chip, own_right, base, out):
    group = base.shape[1] // 3
    chip_mid = split(unfold(chip[...]))
    for part in range(3):
        out[part] = base[part]
        out[part, shared_rows(info, CHIP, group), :] -= 2.0 * passes(
            [chip_mid], [right(own_right, info, CHIP, part)]
        )
        out[part] = masked(out[part], kept, mask_at(info, part))


def finish_body(info, kept, link, own_right, base, out):
    group = out.shape[0] // 3
    link_mid = split(unfold(link[...]))
    at = shared_rows(info, LINK, group)
    first_row = place(info, LINK, 3)[0]
    values = []
    for part in range(3):
        value = -2.0 * passes([link_mid], [right(own_right, info, LINK, part)])
        values.append(base[part, at, :] + masked(value, kept, mask_at(info, part), first_row))
    odd = info[0] == 1

    def store(rows, near, mid, far):
        out[rows, :group] = jnp.where(odd, near, far)[:, :group]
        out[rows, group : 2 * group] = mid[:, :group]
        out[rows, 2 * group :] = jnp.where(odd, far, near)[:, :group]

    store(at, *values)
    rest = pl.ds(pl.multiple_of(2 * place(info, CHIP, group)[0], 64), group)
    store(rest, *(base[part, rest, :] for part in range(3)))


VMEM = pl.BlockSpec(memory_space=pltpu.VMEM)
SMEM = pl.BlockSpec(memory_space=pltpu.SMEM)


def call(body, name, scalars, arrays, outs, work=4):
    return pl.pallas_call(
        body,
        out_shape=[jax.ShapeDtypeStruct(shape, kind) for shape, kind in outs],
        in_specs=[SMEM] * len(scalars) + [VMEM] * len(arrays),
        out_specs=[VMEM] * len(outs),
        compiler_params=pltpu.CompilerParams(vmem_limit_bytes=24 << 20),
        cost_estimate=pl.CostEstimate(flops=work * 1000000000, transcendentals=0, bytes_accessed=work * 5000000),
        name=name,
    )(*scalars, *arrays)


def on_device(p_tiles, square_kept, result_kept):
    side = p_tiles.shape[0]
    group = side // 3
    n_row, n_col = lax.axis_size("row"), lax.axis_size("col")
    info = jnp.stack([lax.axis_index("row") % 2, lax.axis_index("col") % 2]).astype(jnp.int32)
    strip = ((3 * side // 2, LANES), F32)
    slab = ((3 * group, LANES), F32)
    two_slabs = ((6 * group, LANES), F32)
    three_slabs = ((9 * group, LANES), F32)
    wide = ((side, WIDE), F32)
    three_wide = ((3, side, WIDE), F32)
    rights = ((2, 3 * WIDE, WIDE), BF16)

    def exchange(value, axis, even_step):
        size = n_row if axis == "row" else n_col
        return lax.ppermute(
            value, axis, [(i, (i + (even_step if i % 2 == 0 else -even_step)) % size) for i in range(size)]
        )

    chip, link_a, link_b, mid, near, far = call(
        pack_body, "pack", (info,), (p_tiles,), [three_slabs, two_slabs, slab] + [strip] * 3
    )
    link_a = exchange(link_a, "col", -1)
    partner_mid = exchange(mid, "row", 1)
    chip = exchange(chip, "col", 1)
    chip, link_b, near = lax.optimization_barrier((chip, link_b, near))
    link_b = exchange(link_b, "col", -1)
    partner_near = exchange(near, "row", 1)
    own_left, own_right, chip_left = call(
        prepare_body,
        "prepare",
        (info,),
        (p_tiles, chip),
        [((2, 3, side, WIDE), BF16), ((2, 3, 3 * WIDE, WIDE), BF16), ((2, 3, 2 * group, WIDE), BF16)],
    )
    partner_mid, own_left = lax.optimization_barrier((partner_mid, own_left))
    other_mid = exchange(partner_mid, "row", 2)
    begun, right_near = call(
        near_start_body, "near_start", (info,), (partner_mid, own_left, own_right, chip_left), [wide, rights]
    )
    s_near, near_link, link_left = call(
        near_body,
        "square_near",
        (info, square_kept),
        (link_a, begun, own_right, right_near),
        [wide, slab, ((2, 2, 2 * group, WIDE), BF16)],
    )
    near_link = exchange(near_link, "col", -1)
    (begun,) = call(
        far_start_body, "far_start", (info,), (own_left, own_right, chip_left, link_left), [wide]
    )
    far, begun = lax.optimization_barrier((far, begun))
    other_far = exchange(far, "row", -1)
    s_far, sides_chip, far_link, link_left_far, right_far = call(
        far_body,
        "square_far",
        (info, square_kept),
        (link_b, other_mid, begun, s_near, own_left, chip_left),
        [wide, two_slabs, slab, ((2, 2 * group, WIDE), BF16), rights],
    )
    far_link = exchange(far_link, "col", -1)
    sides_chip = exchange(sides_chip, "col", 1)
    begun, mid_near = call(
        mid_start_body,
        "mid_start",
        (info,),
        (partner_near, own_left, own_right, chip_left, link_left),
        [wide, rights],
    )
    (total,) = call(cube_near_body, "cube_near", (info,), (near_link, s_near, right_near, mid_near), [three_wide])
    total, other_far = lax.optimization_barrier((total, other_far))
    s_mid, mid_chip, mid_link, mid_far = call(
        mid_body,
        "square_mid",
        (info, square_kept),
        (other_far, own_left, chip_left, link_left_far, begun),
        [wide, slab, slab, rights],
        work=0,
    )
    mid_link = exchange(mid_link, "col", -1)
    mid_chip = exchange(mid_chip, "col", 1)
    (base,) = call(
        cube_own_body,
        "cube_own",
        (info,),
        (sides_chip, far_link, total, s_near, s_mid, s_far, own_right, right_near, right_far, mid_near, mid_far),
        [three_wide],
    )
    (base,) = call(
        cube_chip_body,
        "cube_chip",
        (info, result_kept),
        (mid_chip, own_right, base),
        [three_wide],
    )
    (purified,) = call(
        finish_body, "finish", (info, result_kept), (mid_link, own_right, base), [((side, side), F32)]
    )
    return purified


def solution(mesh):
    return jax.shard_map(
        on_device,
        mesh=mesh,
        in_specs=(P("row", "col"), P("row", "col"), P("row", "col")),
        out_specs=P("row", "col"),
        check_vma=False,
    )
```

```python
import jax
import jax.numpy as jnp
from jax import lax
from jax.experimental import pallas as pl
from jax.experimental.pallas import tpu as pltpu
from jax.sharding import PartitionSpec as P

LANES = 128
WIDE = 256
F32 = jnp.float32
BF16 = jnp.bfloat16
NEAR, MID, FAR = range(3)
OWN, CHIP, LINK = range(3)


def place(info, who, group):
    above = (info[1] == 1) == (who == CHIP)
    return jnp.where(above, 0, group), jnp.where(above, 0, 2)


def shared_rows(info, who, group):
    return pl.ds(pl.multiple_of(place(info, who, group)[0], 64), 2 * group)


def low_half(rows):
    return lax.broadcasted_iota(jnp.int32, (rows, LANES), 1) < LANES // 2


def store_fold(out_ref, base, value):
    rows = value.shape[0]
    half = rows // 2
    tail = value[:, LANES:]
    out_ref[pl.ds(base, rows), :] = value[:, :LANES]
    out_ref[pl.ds(base + rows, half), :] = jnp.where(
        low_half(half), tail[:half], pltpu.roll(tail[half:], LANES // 2, 1)
    )


def unfold(packed):
    rows = packed.shape[0] * 2 // 3
    half = rows // 2
    tail = packed[rows:]
    keep = low_half(half)
    upper = jnp.where(keep, tail, 0.0)
    lower = jnp.where(keep, pltpu.roll(tail, LANES // 2, 1), 0.0)
    return jnp.concatenate([packed[:rows], jnp.concatenate([upper, lower], 0)], 1)


def tile_groups(info, tile_ref, at):
    keep = low_half(at.size)
    first = jnp.concatenate([tile_ref[at, 0:128], jnp.where(keep, tile_ref[at, 128:256], 0.0)], 1)
    one = pltpu.roll(tile_ref[at, 128:256], LANES // 2, 1)
    two = pltpu.roll(tile_ref[at, 256:384], LANES // 2, 1)
    middle = jnp.concatenate([jnp.where(keep, one, two), jnp.where(keep, two, 0.0)], 1)
    end = tile_ref[at, 512:576]
    last = jnp.concatenate([tile_ref[at, 384:512], jnp.concatenate([end, jnp.zeros_like(end)], 1)], 1)
    odd = info[0] == 1
    return jnp.where(odd, first, last), middle, jnp.where(odd, last, first)


def split(value):
    high = value.astype(BF16)
    return high, (value - high.astype(F32)).astype(BF16)


def store_left(out_ref, at, value):
    out_ref[(0,) + at], out_ref[(1,) + at] = split(value)


def store_right(out_ref, at, value):
    group = value.shape[0] // 3
    for half, part in enumerate(split(value)):
        for ky in range(3):
            out_ref[(half,) + at + (pl.ds(ky * WIDE, group),)] = part[ky * group : (ky + 1) * group]
            out_ref[(half,) + at + (pl.ds(ky * WIDE + group, WIDE - group),)] = jnp.zeros((WIDE - group, WIDE), BF16)


def left(ref, *at):
    return ref[(0,) + at], ref[(1,) + at]


def right(ref, info, who, *at):
    start = WIDE if who == OWN else pl.multiple_of(place(info, who, 0)[1] * WIDE, WIDE)
    rows = (pl.ds(start, WIDE),)
    return ref[(0,) + at + rows], ref[(1,) + at + rows]


def passes(lefts, rights):
    wide = [high for high, _ in lefts] + [low for _, low in lefts] + [high for high, _ in lefts]
    tall = [high for high, _ in rights] + [high for high, _ in rights] + [low for _, low in rights]
    return jnp.dot(jnp.concatenate(wide, 1), jnp.concatenate(tall, 0), preferred_element_type=F32)


def mask_at(info, part):
    return 3 if part == MID else jnp.where((info[0] == 1) == (part == NEAR), 0, 6)


def masked(value, kept_ref, start, first_row=0):
    lane = lax.broadcasted_iota(jnp.int32, (8, WIDE), 1)

    def flags(i):
        one, two, three = (kept_ref[first_row + i, start + j] for j in range(3))
        return jnp.where(lane < 64, one, jnp.where(lane < 128, two, three)).astype(F32)[:1]

    return jnp.concatenate([value[i * 64 : (i + 1) * 64] * flags(i) for i in range(value.shape[0] // 64)], 0)


def pack_body(info, tile, chip, link_a, link_b, mid, near, far):
    side = tile.shape[0]
    group = side // 3
    groups = tile_groups(info, tile, shared_rows(info, LINK, group))
    store_fold(link_a, 0, groups[MID])
    store_fold(link_a, 3 * group, groups[NEAR])
    store_fold(link_b, 0, groups[FAR])
    groups = tile_groups(info, tile, pl.ds(0, side))
    for out, part in ((mid, MID), (near, NEAR), (far, FAR)):
        store_fold(out, 0, groups[part])
    groups = tile_groups(info, tile, shared_rows(info, CHIP, group))
    for part in range(3):
        store_fold(chip, part * 3 * group, groups[part])


def prepare_body(info, tile, chip, own_left, own_right, chip_left):
    side = tile.shape[0]
    for part, value in enumerate(tile_groups(info, tile, pl.ds(0, side))):
        store_left(own_left, (part,), value)
        store_right(own_right, (part,), value)
        store_left(chip_left, (part,), unfold(chip[part * side : (part + 1) * side, :]))


def near_start_body(info, mid, own_left, own_right, chip_left, out, rights):
    group = mid.shape[0] * 2 // 9
    store_right(rights, (), unfold(mid[...]))
    for who, lefts in ((OWN, own_left), (CHIP, chip_left)):
        value = passes(
            [left(lefts, NEAR), left(lefts, MID)], [right(rights, info, who), right(own_right, info, who, NEAR)]
        )
        if who == OWN:
            out[...] = value
        else:
            out[shared_rows(info, who, group), :] += value


def near_body(info, kept, link_a, begun, own_right, right_near, out, link, link_left):
    group = link_a.shape[0] // 6
    for part, base in ((MID, 0), (NEAR, 3 * group)):
        store_left(link_left, (part,), unfold(link_a[base : base + 3 * group, :]))
    out[...] = begun[...]
    out[shared_rows(info, LINK, group), :] += passes(
        [left(link_left, NEAR), left(link_left, MID)],
        [right(right_near, info, LINK), right(own_right, info, LINK, NEAR)],
    )
    out[...] = masked(out[...], kept, mask_at(info, NEAR))
    store_fold(link, 0, out[shared_rows(info, LINK, group), :])


def far_start_body(info, own_left, own_right, chip_left, link_left, out):
    group = out.shape[0] // 3
    for who, lefts in ((OWN, own_left), (CHIP, chip_left), (LINK, link_left)):
        value = passes([left(lefts, MID)], [right(own_right, info, who, FAR)])
        if who == OWN:
            out[...] = value
        else:
            out[shared_rows(info, who, group), :] += value


def far_body(info, kept, link_b, mid, begun, near, own_left, chip_left, out, chip, link, link_left, rights):
    group = out.shape[0] // 3
    store_left(link_left, (), unfold(link_b[...]))
    store_right(rights, (), unfold(mid[...]))
    out[...] = begun[...] + passes([left(own_left, FAR)], [right(rights, info, OWN)])
    for who, factor in ((CHIP, left(chip_left, FAR)), (LINK, left(link_left))):
        out[shared_rows(info, who, group), :] += passes([factor], [right(rights, info, who)])
    out[...] = masked(out[...], kept, mask_at(info, FAR))
    store_fold(link, 0, out[shared_rows(info, LINK, group), :])
    store_fold(chip, 0, near[shared_rows(info, CHIP, group), :])
    store_fold(chip, 3 * group, out[shared_rows(info, CHIP, group), :])


def mid_start_body(info, near, own_left, own_right, chip_left, link_left, out, rights):
    group = out.shape[0] // 3
    store_right(rights, (), unfold(near[...]))
    for who, lefts in ((OWN, own_left), (CHIP, chip_left), (LINK, link_left)):
        value = passes(
            [left(lefts, NEAR), left(lefts, MID)], [right(rights, info, who), right(own_right, info, who, MID)]
        )
        if who == OWN:
            out[...] = value
        else:
            out[shared_rows(info, who, group), :] += value


def mid_body(info, kept, far, own_left, chip_left, link_left, begun, out, chip, link, rights):
    group = out.shape[0] // 3
    store_right(rights, (), unfold(far[...]))
    out[...] = begun[...] + passes([left(own_left, FAR)], [right(rights, info, OWN)])
    for who, factor in ((CHIP, left(chip_left, FAR)), (LINK, left(link_left))):
        out[shared_rows(info, who, group), :] += passes([factor], [right(rights, info, who)])
    out[...] = masked(out[...], kept, 3)
    store_fold(link, 0, out[shared_rows(info, LINK, group), :])
    store_fold(chip, 0, out[shared_rows(info, CHIP, group), :])


def cube_near_body(info, link, near, right_near, right_mid, out):
    group = near.shape[0] // 3
    own, other = split(near[...]), split(unfold(link[...]))
    out[FAR] = jnp.zeros(near.shape, F32)
    for part, ref in ((NEAR, right_near), (MID, right_mid)):
        out[part] = passes([own], [right(ref, info, OWN)])
        out[part, shared_rows(info, LINK, group), :] += passes([other], [right(ref, info, LINK)])


def cube_own_body(info, chip, link, total, near, mid, far, own_right, right_near, right_far, mid_near, mid_far, out):
    group = near.shape[0] // 3
    own_mid, own_far = split(mid[...]), split(far[...])
    chip_near, chip_far = (split(unfold(chip[at * 3 * group : (at + 1) * 3 * group, :])) for at in range(2))
    link_far = split(unfold(link[...]))

    def add(part, square, own, from_chip, from_link):
        out[part] = 3.0 * square[...] - 2.0 * (total[part] + passes(*own))
        out[part, shared_rows(info, CHIP, group), :] -= 2.0 * passes(*from_chip)
        if from_link is not None:
            out[part, shared_rows(info, LINK, group), :] -= 2.0 * passes([link_far], [from_link])

    add(
        NEAR,
        near,
        ([own_mid], [right(own_right, info, OWN, NEAR)]),
        ([chip_near], [right(right_near, info, CHIP)]),
        None,
    )
    add(
        MID,
        mid,
        ([own_mid, own_far], [right(own_right, info, OWN, MID), right(mid_far, info, OWN)]),
        ([chip_near, chip_far], [right(mid_near, info, CHIP), right(mid_far, info, CHIP)]),
        right(mid_far, info, LINK),
    )
    add(
        FAR,
        far,
        ([own_mid, own_far], [right(own_right, info, OWN, FAR), right(right_far, info, OWN)]),
        ([chip_far], [right(right_far, info, CHIP)]),
        right(right_far, info, LINK),
    )


def cube_chip_body(info, kept, chip, own_right, base, out):
    group = base.shape[1] // 3
    chip_mid = split(unfold(chip[...]))
    for part in range(3):
        out[part] = base[part]
        out[part, shared_rows(info, CHIP, group), :] -= 2.0 * passes(
            [chip_mid], [right(own_right, info, CHIP, part)]
        )
        out[part] = masked(out[part], kept, mask_at(info, part))


def finish_body(info, kept, link, own_right, base, out):
    group = out.shape[0] // 3
    link_mid = split(unfold(link[...]))
    at = shared_rows(info, LINK, group)
    first_row = place(info, LINK, 3)[0]
    values = []
    for part in range(3):
        value = -2.0 * passes([link_mid], [right(own_right, info, LINK, part)])
        values.append(base[part, at, :] + masked(value, kept, mask_at(info, part), first_row))
    odd = info[0] == 1

    def store(rows, near, mid, far):
        out[rows, :group] = jnp.where(odd, near, far)[:, :group]
        out[rows, group : 2 * group] = mid[:, :group]
        out[rows, 2 * group :] = jnp.where(odd, far, near)[:, :group]

    store(at, *values)
    rest = pl.ds(pl.multiple_of(2 * place(info, CHIP, group)[0], 64), group)
    store(rest, *(base[part, rest, :] for part in range(3)))


VMEM = pl.BlockSpec(memory_space=pltpu.VMEM)
SMEM = pl.BlockSpec(memory_space=pltpu.SMEM)


def call(body, name, scalars, arrays, outs, work=4):
    return pl.pallas_call(
        body,
        out_shape=[jax.ShapeDtypeStruct(shape, kind) for shape, kind in outs],
        in_specs=[SMEM] * len(scalars) + [VMEM] * len(arrays),
        out_specs=[VMEM] * len(outs),
        compiler_params=pltpu.CompilerParams(vmem_limit_bytes=24 << 20),
        cost_estimate=pl.CostEstimate(flops=work * 1000000000, transcendentals=0, bytes_accessed=work * 5000000),
        name=name,
    )(*scalars, *arrays)


def on_device(p_tiles, square_kept, result_kept):
    side = p_tiles.shape[0]
    group = side // 3
    n_row, n_col = lax.axis_size("row"), lax.axis_size("col")
    info = jnp.stack([lax.axis_index("row") % 2, lax.axis_index("col") % 2]).astype(jnp.int32)
    strip = ((3 * side // 2, LANES), F32)
    slab = ((3 * group, LANES), F32)
    two_slabs = ((6 * group, LANES), F32)
    three_slabs = ((9 * group, LANES), F32)
    wide = ((side, WIDE), F32)
    three_wide = ((3, side, WIDE), F32)
    rights = ((2, 3 * WIDE, WIDE), BF16)

    def exchange(value, axis, even_step):
        size = n_row if axis == "row" else n_col
        return lax.ppermute(
            value, axis, [(i, (i + (even_step if i % 2 == 0 else -even_step)) % size) for i in range(size)]
        )

    chip, link_a, link_b, mid, near, far = call(
        pack_body, "pack", (info,), (p_tiles,), [three_slabs, two_slabs, slab] + [strip] * 3
    )
    link_a = exchange(link_a, "col", -1)
    partner_mid = exchange(mid, "row", 1)
    passed_far = exchange(far, "row", -2)
    chip = exchange(chip, "col", 1)
    chip, link_b, near = lax.optimization_barrier((chip, link_b, near))
    link_b = exchange(link_b, "col", -1)
    partner_near = exchange(near, "row", 1)
    own_left, own_right, chip_left = call(
        prepare_body,
        "prepare",
        (info,),
        (p_tiles, chip),
        [((2, 3, side, WIDE), BF16), ((2, 3, 3 * WIDE, WIDE), BF16), ((2, 3, 2 * group, WIDE), BF16)],
    )
    partner_mid, own_left = lax.optimization_barrier((partner_mid, own_left))
    other_mid = exchange(partner_mid, "row", 2)
    begun, right_near = call(
        near_start_body, "near_start", (info,), (partner_mid, own_left, own_right, chip_left), [wide, rights]
    )
    passed_far, begun = lax.optimization_barrier((passed_far, begun))
    other_far = exchange(passed_far, "row", 1)
    s_near, near_link, link_left = call(
        near_body,
        "square_near",
        (info, square_kept),
        (link_a, begun, own_right, right_near),
        [wide, slab, ((2, 2, 2 * group, WIDE), BF16)],
    )
    near_link = exchange(near_link, "col", -1)
    (begun,) = call(
        far_start_body, "far_start", (info,), (own_left, own_right, chip_left, link_left), [wide]
    )
    s_far, sides_chip, far_link, link_left_far, right_far = call(
        far_body,
        "square_far",
        (info, square_kept),
        (link_b, other_mid, begun, s_near, own_left, chip_left),
        [wide, two_slabs, slab, ((2, 2 * group, WIDE), BF16), rights],
    )
    far_link = exchange(far_link, "col", -1)
    sides_chip = exchange(sides_chip, "col", 1)
    begun, mid_near = call(
        mid_start_body,
        "mid_start",
        (info,),
        (partner_near, own_left, own_right, chip_left, link_left),
        [wide, rights],
    )
    (total,) = call(cube_near_body, "cube_near", (info,), (near_link, s_near, right_near, mid_near), [three_wide])
    total, other_far = lax.optimization_barrier((total, other_far))
    s_mid, mid_chip, mid_link, mid_far = call(
        mid_body,
        "square_mid",
        (info, square_kept),
        (other_far, own_left, chip_left, link_left_far, begun),
        [wide, slab, slab, rights],
        work=0,
    )
    mid_link = exchange(mid_link, "col", -1)
    mid_chip = exchange(mid_chip, "col", 1)
    (base,) = call(
        cube_own_body,
        "cube_own",
        (info,),
        (sides_chip, far_link, total, s_near, s_mid, s_far, own_right, right_near, right_far, mid_near, mid_far),
        [three_wide],
    )
    (base,) = call(
        cube_chip_body,
        "cube_chip",
        (info, result_kept),
        (mid_chip, own_right, base),
        [three_wide],
    )
    (purified,) = call(
        finish_body, "finish", (info, result_kept), (mid_link, own_right, base), [((side, side), F32)]
    )
    return purified


def solution(mesh):
    return jax.shard_map(
        on_device,
        mesh=mesh,
        in_specs=(P("row", "col"), P("row", "col"), P("row", "col")),
        out_specs=P("row", "col"),
        check_vma=False,
    )
```

```python
import jax
import jax.numpy as jnp
from jax import lax
from jax.experimental import pallas as pl
from jax.experimental.pallas import tpu as pltpu
from jax.sharding import PartitionSpec as P

LANES = 128
WIDE = 256
F32 = jnp.float32
BF16 = jnp.bfloat16
NEAR, MID, FAR = range(3)
OWN, CHIP, LINK = range(3)
COPIES = 6


def place(info, who, group):
    above = (info[1] == 1) == (who == CHIP)
    return jnp.where(above, 0, group), jnp.where(above, 0, 2)


def shared_rows(info, who, group):
    return pl.ds(pl.multiple_of(place(info, who, group)[0], 64), 2 * group)


def low_half(rows):
    return lax.broadcasted_iota(jnp.int32, (rows, LANES), 1) < LANES // 2


def store_fold(out_ref, base, value):
    rows = value.shape[0]
    half = rows // 2
    tail = value[:, LANES:]
    out_ref[pl.ds(base, rows), :] = value[:, :LANES]
    out_ref[pl.ds(base + rows, half), :] = jnp.where(
        low_half(half), tail[:half], pltpu.roll(tail[half:], LANES // 2, 1)
    )


def unfold(packed):
    rows = packed.shape[0] * 2 // 3
    half = rows // 2
    tail = packed[rows:]
    keep = low_half(half)
    upper = jnp.where(keep, tail, 0.0)
    lower = jnp.where(keep, pltpu.roll(tail, LANES // 2, 1), 0.0)
    return jnp.concatenate([packed[:rows], jnp.concatenate([upper, lower], 0)], 1)


def tile_groups(info, tile_ref, at):
    keep = low_half(at.size)
    first = jnp.concatenate([tile_ref[at, 0:128], jnp.where(keep, tile_ref[at, 128:256], 0.0)], 1)
    one = pltpu.roll(tile_ref[at, 128:256], LANES // 2, 1)
    two = pltpu.roll(tile_ref[at, 256:384], LANES // 2, 1)
    middle = jnp.concatenate([jnp.where(keep, one, two), jnp.where(keep, two, 0.0)], 1)
    end = tile_ref[at, 512:576]
    last = jnp.concatenate([tile_ref[at, 384:512], jnp.concatenate([end, jnp.zeros_like(end)], 1)], 1)
    odd = info[0] == 1
    return jnp.where(odd, first, last), middle, jnp.where(odd, last, first)


def split(value):
    high = value.astype(BF16)
    return high, (value - high.astype(F32)).astype(BF16)


def store_left(out_ref, at, value):
    out_ref[(0,) + at], out_ref[(1,) + at] = split(value)


def store_right(out_ref, at, value):
    group = value.shape[0] // 3
    for half, part in enumerate(split(value)):
        for ky in range(3):
            out_ref[(half,) + at + (pl.ds(ky * WIDE, group),)] = part[ky * group : (ky + 1) * group]
            out_ref[(half,) + at + (pl.ds(ky * WIDE + group, WIDE - group),)] = jnp.zeros((WIDE - group, WIDE), BF16)


def left(ref, *at):
    return ref[(0,) + at], ref[(1,) + at]


def right(ref, info, who, *at):
    start = WIDE if who == OWN else pl.multiple_of(place(info, who, 0)[1] * WIDE, WIDE)
    rows = (pl.ds(start, WIDE),)
    return ref[(0,) + at + rows], ref[(1,) + at + rows]


def passes(lefts, rights):
    wide = [high for high, _ in lefts] + [low for _, low in lefts] + [high for high, _ in lefts]
    tall = [high for high, _ in rights] + [high for high, _ in rights] + [low for _, low in rights]
    return jnp.dot(jnp.concatenate(wide, 1), jnp.concatenate(tall, 0), preferred_element_type=F32)


def mask_at(info, part):
    return 3 if part == MID else jnp.where((info[0] == 1) == (part == NEAR), 0, 6)


def masked(value, kept_ref, start, first_row=0):
    lane = lax.broadcasted_iota(jnp.int32, (8, WIDE), 1)

    def flags(i):
        one, two, three = (kept_ref[first_row + i, start + j] for j in range(3))
        return jnp.where(lane < 64, one, jnp.where(lane < 128, two, three)).astype(F32)[:1]

    return jnp.concatenate([value[i * 64 : (i + 1) * 64] * flags(i) for i in range(value.shape[0] // 64)], 0)


def pack_link_body(info, source, tile, link_a, sems):
    side = tile.shape[0]
    group = side // 3
    step = side // COPIES
    copies = [
        pltpu.make_async_copy(source.at[pl.ds(i * step, step), :], tile.at[pl.ds(i * step, step), :], sems.at[i])
        for i in range(COPIES)
    ]
    for copy in copies:
        copy.start()
    for copy in copies:
        copy.wait()
    groups = tile_groups(info, tile, shared_rows(info, LINK, group))
    store_fold(link_a, 0, groups[MID])
    store_fold(link_a, 3 * group, groups[NEAR])


def pack_body(info, tile, chip, link_b, mid, near, far):
    side = tile.shape[0]
    group = side // 3
    groups = tile_groups(info, tile, pl.ds(0, side))
    for out, part in ((mid, MID), (near, NEAR), (far, FAR)):
        store_fold(out, 0, groups[part])
    store_fold(link_b, 0, tile_groups(info, tile, shared_rows(info, LINK, group))[FAR])
    groups = tile_groups(info, tile, shared_rows(info, CHIP, group))
    for part in range(3):
        store_fold(chip, part * 3 * group, groups[part])


def prepare_body(info, tile, chip, own_left, own_right, chip_left):
    side = tile.shape[0]
    for part, value in enumerate(tile_groups(info, tile, pl.ds(0, side))):
        store_left(own_left, (part,), value)
        store_right(own_right, (part,), value)
        store_left(chip_left, (part,), unfold(chip[part * side : (part + 1) * side, :]))


def near_start_body(info, mid, own_left, own_right, chip_left, out, rights):
    group = mid.shape[0] * 2 // 9
    store_right(rights, (), unfold(mid[...]))
    for who, lefts in ((OWN, own_left), (CHIP, chip_left)):
        value = passes(
            [left(lefts, NEAR), left(lefts, MID)], [right(rights, info, who), right(own_right, info, who, NEAR)]
        )
        if who == OWN:
            out[...] = value
        else:
            out[shared_rows(info, who, group), :] += value


def near_body(info, kept, link_a, begun, own_right, right_near, out, link, link_left):
    group = link_a.shape[0] // 6
    for part, base in ((MID, 0), (NEAR, 3 * group)):
        store_left(link_left, (part,), unfold(link_a[base : base + 3 * group, :]))
    out[...] = begun[...]
    out[shared_rows(info, LINK, group), :] += passes(
        [left(link_left, NEAR), left(link_left, MID)],
        [right(right_near, info, LINK), right(own_right, info, LINK, NEAR)],
    )
    out[...] = masked(out[...], kept, mask_at(info, NEAR))
    store_fold(link, 0, out[shared_rows(info, LINK, group), :])


def middle_products_body(info, own_left, own_right, chip_left, link_left, far, mid):
    group = far.shape[0] // 3
    for out, part in ((far, FAR), (mid, MID)):
        for who, lefts in ((OWN, own_left), (CHIP, chip_left), (LINK, link_left)):
            value = passes([left(lefts, MID)], [right(own_right, info, who, part)])
            if who == OWN:
                out[...] = value
            else:
                out[shared_rows(info, who, group), :] += value


def far_body(info, kept, link_b, mid, begun, own_left, chip_left, out, link, link_left, rights):
    group = out.shape[0] // 3
    store_left(link_left, (), unfold(link_b[...]))
    store_right(rights, (), unfold(mid[...]))
    out[...] = begun[...] + passes([left(own_left, FAR)], [right(rights, info, OWN)])
    for who, factor in ((CHIP, left(chip_left, FAR)), (LINK, left(link_left))):
        out[shared_rows(info, who, group), :] += passes([factor], [right(rights, info, who)])
    out[...] = masked(out[...], kept, mask_at(info, FAR))
    store_fold(link, 0, out[shared_rows(info, LINK, group), :])


def mid_start_body(info, near, begun, own_left, chip_left, link_left, s_near, s_far, out, sides, rights):
    group = out.shape[0] // 3
    store_fold(sides, 0, s_near[shared_rows(info, CHIP, group), :])
    store_fold(sides, 3 * group, s_far[shared_rows(info, CHIP, group), :])
    store_right(rights, (), unfold(near[...]))
    out[...] = begun[...] + passes([left(own_left, NEAR)], [right(rights, info, OWN)])
    for who, lefts in ((CHIP, chip_left), (LINK, link_left)):
        out[shared_rows(info, who, group), :] += passes([left(lefts, NEAR)], [right(rights, info, who)])


def mid_body(info, kept, far, own_left, chip_left, link_left, begun, out, chip, link, rights):
    group = out.shape[0] // 3
    store_right(rights, (), unfold(far[...]))
    out[...] = begun[...] + passes([left(own_left, FAR)], [right(rights, info, OWN)])
    for who, factor in ((CHIP, left(chip_left, FAR)), (LINK, left(link_left))):
        out[shared_rows(info, who, group), :] += passes([factor], [right(rights, info, who)])
    out[...] = masked(out[...], kept, 3)
    store_fold(link, 0, out[shared_rows(info, LINK, group), :])
    store_fold(chip, 0, out[shared_rows(info, CHIP, group), :])


def cube_near_body(info, link, near, far, right_near, right_far, right_mid, out):
    group = near.shape[0] // 3
    own, other = split(near[...]), split(unfold(link[...]))
    out[FAR] = passes([split(far[...])], [right(right_far, info, OWN)])
    for part, ref in ((NEAR, right_near), (MID, right_mid)):
        out[part] = passes([own], [right(ref, info, OWN)])
        out[part, shared_rows(info, LINK, group), :] += passes([other], [right(ref, info, LINK)])


def cube_own_body(info, link, total, near, mid, far, own_right, right_far, mid_far, out):
    group = near.shape[0] // 3
    own_mid, own_far = split(mid[...]), split(far[...])
    link_far = split(unfold(link[...]))
    rights = [right(own_right, info, OWN, part) for part in range(3)]
    out[NEAR] = 3.0 * near[...] - 2.0 * (total[NEAR] + passes([own_mid], rights[NEAR:MID]))
    out[MID] = 3.0 * mid[...] - 2.0 * (total[MID] + passes([own_mid, own_far], [rights[MID], right(mid_far, info, OWN)]))
    out[FAR] = 3.0 * far[...] - 2.0 * (total[FAR] + passes([own_mid], rights[FAR:]))
    for part, ref in ((MID, mid_far), (FAR, right_far)):
        out[part, shared_rows(info, LINK, group), :] -= 2.0 * passes([link_far], [right(ref, info, LINK)])


def cube_chip_body(info, kept, sides, chip, own_right, right_near, right_far, mid_near, mid_far, base, out):
    group = base.shape[1] // 3
    at = shared_rows(info, CHIP, group)
    chips = [split(unfold(value)) for value in (sides[: 3 * group, :], chip[...], sides[3 * group :, :])]
    own = [right(own_right, info, CHIP, part) for part in range(3)]
    products = (
        (chips[:2], [right(right_near, info, CHIP), own[NEAR]]),
        (chips, [right(mid_near, info, CHIP), own[MID], right(mid_far, info, CHIP)]),
        (chips[1:], [own[FAR], right(right_far, info, CHIP)]),
    )
    for part, factors in enumerate(products):
        out[part] = base[part]
        out[part, at, :] -= 2.0 * passes(*factors)
        out[part] = masked(out[part], kept, mask_at(info, part))


def finish_body(info, kept, link, own_right, base, out, tile, sems):
    group = tile.shape[0] // 3
    odd = info[0] == 1
    start = place(info, LINK, group)[0]
    first_row = place(info, LINK, 3)[0]

    def send(k, row, near, mid, far):
        rows = pl.ds(pl.multiple_of(row, 64), group)
        tile[rows, :group] = jnp.where(odd, near, far)[:, :group]
        tile[rows, group : 2 * group] = mid[:, :group]
        tile[rows, 2 * group :] = jnp.where(odd, far, near)[:, :group]
        copy = pltpu.make_async_copy(tile.at[rows, :], out.at[rows, :], sems.at[k])
        copy.start()
        return copy

    rest = pl.multiple_of(2 * place(info, CHIP, group)[0], 64)
    copies = [send(0, rest, *(base[part, pl.ds(rest, group), :] for part in range(3)))]
    link_mid = split(unfold(link[...]))
    values = []
    for part in range(3):
        value = -2.0 * passes([link_mid], [right(own_right, info, LINK, part)])
        values.append(masked(value, kept, mask_at(info, part), first_row))
    for k in range(2):
        row = pl.multiple_of(start + k * group, 64)
        copies.append(
            send(
                k + 1,
                row,
                *(base[part, pl.ds(row, group), :] + values[part][k * group : (k + 1) * group] for part in range(3)),
            )
        )
    for copy in copies:
        copy.wait()


VMEM = pl.BlockSpec(memory_space=pltpu.VMEM)
SMEM = pl.BlockSpec(memory_space=pltpu.SMEM)
ANY = pl.BlockSpec(memory_space=pl.ANY)


def call(body, name, scalars, arrays, outs, work=4, source=VMEM, target=VMEM, scratch=()):
    return pl.pallas_call(
        body,
        out_shape=[jax.ShapeDtypeStruct(shape, kind) for shape, kind in outs],
        in_specs=[SMEM] * len(scalars) + [source] * len(arrays),
        out_specs=[target] * len(outs),
        scratch_shapes=scratch,
        compiler_params=pltpu.CompilerParams(vmem_limit_bytes=24 << 20),
        cost_estimate=pl.CostEstimate(flops=work * 1000000000, transcendentals=0, bytes_accessed=work * 5000000),
        name=name,
    )(*scalars, *arrays)


def on_device(p_tiles, square_kept, result_kept):
    side = p_tiles.shape[0]
    group = side // 3
    n_row, n_col = lax.axis_size("row"), lax.axis_size("col")
    info = jnp.stack([lax.axis_index("row") % 2, lax.axis_index("col") % 2]).astype(jnp.int32)
    strip = ((3 * side // 2, LANES), F32)
    slab = ((3 * group, LANES), F32)
    two_slabs = ((6 * group, LANES), F32)
    three_slabs = ((9 * group, LANES), F32)
    wide = ((side, WIDE), F32)
    three_wide = ((3, side, WIDE), F32)
    rights = ((2, 3 * WIDE, WIDE), BF16)

    def exchange(value, axis, even_step):
        size = n_row if axis == "row" else n_col
        return lax.ppermute(
            value, axis, [(i, (i + (even_step if i % 2 == 0 else -even_step)) % size) for i in range(size)]
        )

    tile, link_a = call(
        pack_link_body,
        "pack_link",
        (info,),
        (p_tiles,),
        [((side, side), F32), two_slabs],
        source=ANY,
        scratch=[pltpu.SemaphoreType.DMA((COPIES,))],
    )
    chip, link_b, mid, near, far = call(
        pack_body, "pack", (info,), (tile,), [three_slabs, slab] + [strip] * 3
    )
    link_a = exchange(link_a, "col", -1)
    partner_mid = exchange(mid, "row", 1)
    passed_far = exchange(far, "row", -2)
    chip = exchange(chip, "col", 1)
    chip, link_b, near = lax.optimization_barrier((chip, link_b, near))
    link_b = exchange(link_b, "col", -1)
    partner_near = exchange(near, "row", 1)

    own_left, own_right, chip_left = call(
        prepare_body,
        "prepare",
        (info,),
        (tile, chip),
        [((2, 3, side, WIDE), BF16), ((2, 3, 3 * WIDE, WIDE), BF16), ((2, 3, 2 * group, WIDE), BF16)],
    )
    partner_mid, own_left = lax.optimization_barrier((partner_mid, own_left))
    other_mid = exchange(partner_mid, "row", 2)
    begun, right_near = call(
        near_start_body, "near_start", (info,), (partner_mid, own_left, own_right, chip_left), [wide, rights]
    )
    s_near, near_link, link_left = call(
        near_body,
        "square_near",
        (info, square_kept),
        (link_a, begun, own_right, right_near),
        [wide, slab, ((2, 2, 2 * group, WIDE), BF16)],
    )
    near_link = exchange(near_link, "col", -1)
    passed_far, link_left = lax.optimization_barrier((passed_far, link_left))
    other_far = exchange(passed_far, "row", 1)
    begun, begun_mid = call(
        middle_products_body, "middle_products", (info,), (own_left, own_right, chip_left, link_left), [wide] * 2
    )
    s_far, far_link, link_left_far, right_far = call(
        far_body,
        "square_far",
        (info, square_kept),
        (link_b, other_mid, begun, own_left, chip_left),
        [wide, slab, ((2, 2 * group, WIDE), BF16), rights],
    )
    far_link = exchange(far_link, "col", -1)
    partner_near, link_left_far = lax.optimization_barrier((partner_near, link_left_far))
    begun, sides_chip, mid_near = call(
        mid_start_body,
        "mid_start",
        (info,),
        (partner_near, begun_mid, own_left, chip_left, link_left, s_near, s_far),
        [wide, two_slabs, rights],
    )
    (total,) = call(
        cube_near_body,
        "cube_near",
        (info,),
        (near_link, s_near, s_far, right_near, right_far, mid_near),
        [three_wide],
    )
    total, other_far = lax.optimization_barrier((total, other_far))
    s_mid, mid_chip, mid_link, mid_far = call(
        mid_body,
        "square_mid",
        (info, square_kept),
        (other_far, own_left, chip_left, link_left_far, begun),
        [wide, slab, slab, rights],
        work=0,
    )
    mid_link = exchange(mid_link, "col", -1)
    sides_chip = exchange(sides_chip, "col", 1)
    mid_chip = exchange(mid_chip, "col", 1)
    (base,) = call(
        cube_own_body,
        "cube_own",
        (info,),
        (far_link, total, s_near, s_mid, s_far, own_right, right_far, mid_far),
        [three_wide],
    )
    (base,) = call(
        cube_chip_body,
        "cube_chip",
        (info, result_kept),
        (sides_chip, mid_chip, own_right, right_near, right_far, mid_near, mid_far, base),
        [three_wide],
    )
    (purified,) = call(
        finish_body,
        "finish",
        (info, result_kept),
        (mid_link, own_right, base),
        [((side, side), F32)],
        target=ANY,
        scratch=[pltpu.VMEM((side, side), F32), pltpu.SemaphoreType.DMA((3,))],
    )
    return purified


def solution(mesh):
    return jax.shard_map(
        on_device,
        mesh=mesh,
        in_specs=(P("row", "col"), P("row", "col"), P("row", "col")),
        out_specs=P("row", "col"),
        check_vma=False,
    )
```

```python
import functools

import jax
import jax.numpy as jnp
from jax import lax
from jax.experimental import pallas as pl
from jax.experimental.pallas import tpu as pltpu
from jax.sharding import PartitionSpec as P

LANES = 128
WIDE = 256
F32 = jnp.float32
BF16 = jnp.bfloat16
NEAR, MID, FAR = range(3)
OWN, CHIP, LINK = range(3)


def place(info, who, group):
    above = (info[1] == 1) == (who == CHIP)
    return jnp.where(above, 0, group), jnp.where(above, 0, 2)


def shared_rows(info, who, group):
    return pl.ds(pl.multiple_of(place(info, who, group)[0], 64), 2 * group)


def low_half(rows):
    return lax.broadcasted_iota(jnp.int32, (rows, LANES), 1) < LANES // 2


def store_fold(out_ref, base, value):
    rows = value.shape[0]
    half = rows // 2
    tail = value[:, LANES:]
    out_ref[pl.ds(base, rows), :] = value[:, :LANES]
    out_ref[pl.ds(base + rows, half), :] = jnp.where(
        low_half(half), tail[:half], pltpu.roll(tail[half:], LANES // 2, 1)
    )


def unfold(packed):
    rows = packed.shape[0] * 2 // 3
    half = rows // 2
    tail = packed[rows:]
    keep = low_half(half)
    upper = jnp.where(keep, tail, 0.0)
    lower = jnp.where(keep, pltpu.roll(tail, LANES // 2, 1), 0.0)
    return jnp.concatenate([packed[:rows], jnp.concatenate([upper, lower], 0)], 1)


def tile_groups(info, tile_ref, at):
    keep = low_half(at.size)
    first = jnp.concatenate([tile_ref[at, 0:128], jnp.where(keep, tile_ref[at, 128:256], 0.0)], 1)
    one = pltpu.roll(tile_ref[at, 128:256], LANES // 2, 1)
    two = pltpu.roll(tile_ref[at, 256:384], LANES // 2, 1)
    middle = jnp.concatenate([jnp.where(keep, one, two), jnp.where(keep, two, 0.0)], 1)
    end = tile_ref[at, 512:576]
    last = jnp.concatenate([tile_ref[at, 384:512], jnp.concatenate([end, jnp.zeros_like(end)], 1)], 1)
    odd = info[0] == 1
    return jnp.where(odd, first, last), middle, jnp.where(odd, last, first)


def split(value):
    high = value.astype(BF16)
    return high, (value - high.astype(F32)).astype(BF16)


def store_left(out_ref, at, value):
    out_ref[(0,) + at], out_ref[(1,) + at] = split(value)


def store_right(out_ref, at, value):
    group = value.shape[0] // 3
    for half, part in enumerate(split(value)):
        for ky in range(3):
            out_ref[(half,) + at + (pl.ds(ky * WIDE, group),)] = part[ky * group : (ky + 1) * group]
            out_ref[(half,) + at + (pl.ds(ky * WIDE + group, WIDE - group),)] = jnp.zeros((WIDE - group, WIDE), BF16)


def left(ref, *at):
    return ref[(0,) + at], ref[(1,) + at]


def right(ref, info, who, *at):
    start = WIDE if who == OWN else pl.multiple_of(place(info, who, 0)[1] * WIDE, WIDE)
    rows = (pl.ds(start, WIDE),)
    return ref[(0,) + at + rows], ref[(1,) + at + rows]


def passes(lefts, rights):
    wide = [high for high, _ in lefts] + [low for _, low in lefts] + [high for high, _ in lefts]
    tall = [high for high, _ in rights] + [high for high, _ in rights] + [low for _, low in rights]
    return jnp.dot(jnp.concatenate(wide, 1), jnp.concatenate(tall, 0), preferred_element_type=F32)


def mask_at(info, part):
    return 3 if part == MID else jnp.where((info[0] == 1) == (part == NEAR), 0, 6)


def masked(value, kept_ref, start, first_row=0):
    lane = lax.broadcasted_iota(jnp.int32, (8, WIDE), 1)

    def flags(i):
        one, two, three = (kept_ref[first_row + i, start + j] for j in range(3))
        return jnp.where(lane < 64, one, jnp.where(lane < 128, two, three)).astype(F32)[:1]

    return jnp.concatenate([value[i * 64 : (i + 1) * 64] * flags(i) for i in range(value.shape[0] // 64)], 0)


def pack_first_body(info, tile, mid, link_a, chip):
    side = tile.shape[0]
    group = side // 3
    store_fold(mid, 0, tile_groups(info, tile, pl.ds(0, side))[MID])
    groups = tile_groups(info, tile, shared_rows(info, LINK, group))
    store_fold(link_a, 0, groups[MID])
    store_fold(link_a, 3 * group, groups[NEAR])
    groups = tile_groups(info, tile, shared_rows(info, CHIP, group))
    for part in range(3):
        store_fold(chip, part * 3 * group, groups[part])


def pack_rest_body(info, tile, link_b, near, far):
    side = tile.shape[0]
    groups = tile_groups(info, tile, pl.ds(0, side))
    store_fold(near, 0, groups[NEAR])
    store_fold(far, 0, groups[FAR])
    store_fold(link_b, 0, tile_groups(info, tile, shared_rows(info, LINK, side // 3))[FAR])


def prepare_body(info, tile, chip, own_left, own_right, chip_left):
    side = tile.shape[0]
    for part, value in enumerate(tile_groups(info, tile, pl.ds(0, side))):
        store_left(own_left, (part,), value)
        store_right(own_right, (part,), value)
        store_left(chip_left, (part,), unfold(chip[part * side : (part + 1) * side, :]))


def near_start_body(info, mid, own_left, own_right, chip_left, out, rights):
    group = mid.shape[0] * 2 // 9
    store_right(rights, (), unfold(mid[...]))
    for who, lefts in ((OWN, own_left), (CHIP, chip_left)):
        value = passes(
            [left(lefts, NEAR), left(lefts, MID)], [right(rights, info, who), right(own_right, info, who, NEAR)]
        )
        if who == OWN:
            out[...] = value
        else:
            out[shared_rows(info, who, group), :] += value


def near_body(info, kept, link_a, begun, own_right, right_near, out, link, link_left):
    group = link_a.shape[0] // 6
    for part, base in ((MID, 0), (NEAR, 3 * group)):
        store_left(link_left, (part,), unfold(link_a[base : base + 3 * group, :]))
    out[...] = begun[...]
    out[shared_rows(info, LINK, group), :] += passes(
        [left(link_left, NEAR), left(link_left, MID)],
        [right(right_near, info, LINK), right(own_right, info, LINK, NEAR)],
    )
    out[...] = masked(out[...], kept, mask_at(info, NEAR))
    store_fold(link, 0, out[shared_rows(info, LINK, group), :])


def middle_products_body(info, own_left, own_right, chip_left, link_left, far, mid):
    group = far.shape[0] // 3
    for out, part in ((far, FAR), (mid, MID)):
        for who, lefts in ((OWN, own_left), (CHIP, chip_left), (LINK, link_left)):
            value = passes([left(lefts, MID)], [right(own_right, info, who, part)])
            if who == OWN:
                out[...] = value
            else:
                out[shared_rows(info, who, group), :] += value


def far_body(info, kept, link_b, mid, begun, own_left, chip_left, out, link, link_left, rights):
    group = out.shape[0] // 3
    store_left(link_left, (), unfold(link_b[...]))
    store_right(rights, (), unfold(mid[...]))
    out[...] = begun[...] + passes([left(own_left, FAR)], [right(rights, info, OWN)])
    for who, factor in ((CHIP, left(chip_left, FAR)), (LINK, left(link_left))):
        out[shared_rows(info, who, group), :] += passes([factor], [right(rights, info, who)])
    out[...] = masked(out[...], kept, mask_at(info, FAR))
    store_fold(link, 0, out[shared_rows(info, LINK, group), :])


def mid_start_body(info, near, begun, own_left, chip_left, link_left, s_near, s_far, out, sides, rights):
    group = out.shape[0] // 3
    store_fold(sides, 0, s_near[shared_rows(info, CHIP, group), :])
    store_fold(sides, 3 * group, s_far[shared_rows(info, CHIP, group), :])
    store_right(rights, (), unfold(near[...]))
    out[...] = begun[...] + passes([left(own_left, NEAR)], [right(rights, info, OWN)])
    for who, lefts in ((CHIP, chip_left), (LINK, link_left)):
        out[shared_rows(info, who, group), :] += passes([left(lefts, NEAR)], [right(rights, info, who)])


def mid_body(info, kept, far, own_left, chip_left, link_left, begun, out, chip, link_first, link_second, rights):
    group = out.shape[0] // 3
    store_right(rights, (), unfold(far[...]))
    out[...] = begun[...] + passes([left(own_left, FAR)], [right(rights, info, OWN)])
    for who, factor in ((CHIP, left(chip_left, FAR)), (LINK, left(link_left))):
        out[shared_rows(info, who, group), :] += passes([factor], [right(rights, info, who)])
    out[...] = masked(out[...], kept, 3)
    start = place(info, LINK, group)[0]
    for k, link in enumerate((link_first, link_second)):
        store_fold(link, 0, out[pl.ds(pl.multiple_of(start + k * group, 64), group), :])
    store_fold(chip, 0, out[shared_rows(info, CHIP, group), :])


def cube_near_body(info, link, near, far, right_near, right_far, right_mid, out):
    group = near.shape[0] // 3
    own, other = split(near[...]), split(unfold(link[...]))
    out[FAR] = passes([split(far[...])], [right(right_far, info, OWN)])
    for part, ref in ((NEAR, right_near), (MID, right_mid)):
        out[part] = passes([own], [right(ref, info, OWN)])
        out[part, shared_rows(info, LINK, group), :] += passes([other], [right(ref, info, LINK)])


def cube_own_body(info, link, total, near, mid, far, own_right, right_far, mid_far, out):
    group = near.shape[0] // 3
    own_mid, own_far = split(mid[...]), split(far[...])
    link_far = split(unfold(link[...]))
    rights = [right(own_right, info, OWN, part) for part in range(3)]
    out[NEAR] = 3.0 * near[...] - 2.0 * (total[NEAR] + passes([own_mid], rights[NEAR:MID]))
    out[MID] = 3.0 * mid[...] - 2.0 * (total[MID] + passes([own_mid, own_far], [rights[MID], right(mid_far, info, OWN)]))
    out[FAR] = 3.0 * far[...] - 2.0 * (total[FAR] + passes([own_mid], rights[FAR:]))
    for part, ref in ((MID, mid_far), (FAR, right_far)):
        out[part, shared_rows(info, LINK, group), :] -= 2.0 * passes([link_far], [right(ref, info, LINK)])


def send_rows(info, tile, out, sem, row, near, mid, far):
    odd = info[0] == 1
    group = near.shape[0]
    tile[:, :group] = jnp.where(odd, near, far)[:, :group]
    tile[:, group : 2 * group] = mid[:, :group]
    tile[:, 2 * group :] = jnp.where(odd, far, near)[:, :group]
    copy = pltpu.make_async_copy(tile, out.at[pl.ds(row, group), :], sem)
    copy.start()
    return copy


def cube_chip_body(info, kept, sides, chip, own_right, right_near, right_far, mid_near, mid_far, base, out, result, tile, sem):
    group = base.shape[1] // 3
    at = shared_rows(info, CHIP, group)
    chips = [split(unfold(value)) for value in (sides[: 3 * group, :], chip[...], sides[3 * group :, :])]
    own = [right(own_right, info, CHIP, part) for part in range(3)]
    products = (
        (chips[:2], [right(right_near, info, CHIP), own[NEAR]]),
        (chips, [right(mid_near, info, CHIP), own[MID], right(mid_far, info, CHIP)]),
        (chips[1:], [own[FAR], right(right_far, info, CHIP)]),
    )
    for part, factors in enumerate(products):
        out[part] = base[part]
        out[part, at, :] -= 2.0 * passes(*factors)
        out[part] = masked(out[part], kept, mask_at(info, part))
    rest = pl.multiple_of(2 * place(info, CHIP, group)[0], 64)
    send_rows(info, tile, result, sem, rest, *(out[part, pl.ds(rest, group), :] for part in range(3))).wait()


def finish_body(half, info, kept, link, own_right, base, begun, result, tile, sem):
    del begun
    group = tile.shape[0]
    row = pl.multiple_of(place(info, LINK, group)[0] + half * group, 64)
    first_row = place(info, LINK, 3)[0] + 3 * half
    link_mid = split(unfold(link[...]))
    values = []
    for part in range(3):
        value = -2.0 * passes([link_mid], [right(own_right, info, LINK, part)])
        values.append(base[part, pl.ds(row, group), :] + masked(value, kept, mask_at(info, part), first_row))
    send_rows(info, tile, result, sem, row, *values).wait()


VMEM = pl.BlockSpec(memory_space=pltpu.VMEM)
SMEM = pl.BlockSpec(memory_space=pltpu.SMEM)
ANY = pl.BlockSpec(memory_space=pl.ANY)


def call(body, name, scalars, arrays, outs, work=4, result=False, begun=(), scratch=()):
    count = len(scalars) + len(arrays)
    return pl.pallas_call(
        body,
        out_shape=[jax.ShapeDtypeStruct(shape, kind) for shape, kind in outs],
        in_specs=[SMEM] * len(scalars) + [VMEM] * len(arrays) + [ANY] * len(begun),
        out_specs=[VMEM] * (len(outs) - result) + [ANY] * result,
        scratch_shapes=scratch,
        input_output_aliases={count: len(outs) - 1} if begun else {},
        compiler_params=pltpu.CompilerParams(vmem_limit_bytes=24 << 20),
        cost_estimate=pl.CostEstimate(flops=work * 1000000000, transcendentals=0, bytes_accessed=work * 5000000),
        name=name,
    )(*scalars, *arrays, *begun)


def on_device(p_tiles, square_kept, result_kept):
    side = p_tiles.shape[0]
    group = side // 3
    n_row, n_col = lax.axis_size("row"), lax.axis_size("col")
    info = jnp.stack([lax.axis_index("row") % 2, lax.axis_index("col") % 2]).astype(jnp.int32)
    strip = ((3 * side // 2, LANES), F32)
    slab = ((3 * group, LANES), F32)
    half_slab = ((3 * group // 2, LANES), F32)
    two_slabs = ((6 * group, LANES), F32)
    three_slabs = ((9 * group, LANES), F32)
    wide = ((side, WIDE), F32)
    three_wide = ((3, side, WIDE), F32)
    rights = ((2, 3 * WIDE, WIDE), BF16)

    def exchange(value, axis, even_step):
        size = n_row if axis == "row" else n_col
        return lax.ppermute(
            value, axis, [(i, (i + (even_step if i % 2 == 0 else -even_step)) % size) for i in range(size)]
        )

    mid, link_a, chip = call(
        pack_first_body, "pack_first", (info,), (p_tiles,), [strip, two_slabs, three_slabs]
    )
    link_a = exchange(link_a, "col", -1)
    partner_mid = exchange(mid, "row", 1)
    chip = exchange(chip, "col", 1)
    chip, tile = lax.optimization_barrier((chip, p_tiles))
    link_b, near, far = call(pack_rest_body, "pack_rest", (info,), (tile,), [slab, strip, strip])
    partner_near = exchange(near, "row", 1)
    link_b = exchange(link_b, "col", -1)
    passed_far = exchange(far, "row", -2)

    own_left, own_right, chip_left = call(
        prepare_body,
        "prepare",
        (info,),
        (p_tiles, chip),
        [((2, 3, side, WIDE), BF16), ((2, 3, 3 * WIDE, WIDE), BF16), ((2, 3, 2 * group, WIDE), BF16)],
    )
    partner_mid, own_left = lax.optimization_barrier((partner_mid, own_left))
    other_mid = exchange(partner_mid, "row", 2)
    begun, right_near = call(
        near_start_body, "near_start", (info,), (partner_mid, own_left, own_right, chip_left), [wide, rights]
    )
    s_near, near_link, link_left = call(
        near_body,
        "square_near",
        (info, square_kept),
        (link_a, begun, own_right, right_near),
        [wide, slab, ((2, 2, 2 * group, WIDE), BF16)],
    )
    near_link = exchange(near_link, "col", -1)
    passed_far, link_left = lax.optimization_barrier((passed_far, link_left))
    other_far = exchange(passed_far, "row", 1)
    begun, begun_mid = call(
        middle_products_body, "middle_products", (info,), (own_left, own_right, chip_left, link_left), [wide] * 2
    )
    s_far, far_link, link_left_far, right_far = call(
        far_body,
        "square_far",
        (info, square_kept),
        (link_b, other_mid, begun, own_left, chip_left),
        [wide, slab, ((2, 2 * group, WIDE), BF16), rights],
    )
    far_link = exchange(far_link, "col", -1)
    partner_near, link_left_far = lax.optimization_barrier((partner_near, link_left_far))
    begun, sides_chip, mid_near = call(
        mid_start_body,
        "mid_start",
        (info,),
        (partner_near, begun_mid, own_left, chip_left, link_left, s_near, s_far),
        [wide, two_slabs, rights],
    )
    (total,) = call(
        cube_near_body,
        "cube_near",
        (info,),
        (near_link, s_near, s_far, right_near, right_far, mid_near),
        [three_wide],
    )
    total, other_far = lax.optimization_barrier((total, other_far))
    s_mid, mid_chip, link_first, link_second, mid_far = call(
        mid_body,
        "square_mid",
        (info, square_kept),
        (other_far, own_left, chip_left, link_left_far, begun),
        [wide, slab, half_slab, half_slab, rights],
        work=0,
    )
    link_first = exchange(link_first, "col", -1)
    sides_chip = exchange(sides_chip, "col", 1)
    link_second, sides_chip = lax.optimization_barrier((link_second, sides_chip))
    link_second = exchange(link_second, "col", -1)
    mid_chip = exchange(mid_chip, "col", 1)
    (base,) = call(
        cube_own_body,
        "cube_own",
        (info,),
        (far_link, total, s_near, s_mid, s_far, own_right, right_far, mid_far),
        [three_wide],
    )
    result = ((side, side), F32)
    row_scratch = [pltpu.VMEM((group, side), F32), pltpu.SemaphoreType.DMA(())]
    base, purified = call(
        cube_chip_body,
        "cube_chip",
        (info, result_kept),
        (sides_chip, mid_chip, own_right, right_near, right_far, mid_near, mid_far, base),
        [three_wide, result],
        result=True,
        scratch=row_scratch,
    )
    for half, link in enumerate((link_first, link_second)):
        (purified,) = call(
            functools.partial(finish_body, half),
            ("finish_first", "finish_second")[half],
            (info, result_kept),
            (link, own_right, base),
            [result],
            result=True,
            begun=(purified,),
            scratch=row_scratch,
        )
    return purified


def solution(mesh):
    return jax.shard_map(
        on_device,
        mesh=mesh,
        in_specs=(P("row", "col"), P("row", "col"), P("row", "col")),
        out_specs=P("row", "col"),
        check_vma=False,
    )
```

```python
import jax
import jax.numpy as jnp
from jax import lax
from jax.experimental import pallas as pl
from jax.experimental.pallas import tpu as pltpu
from jax.sharding import PartitionSpec as P

LANES = 128
WIDE = 256
F32 = jnp.float32
BF16 = jnp.bfloat16
NEAR, MID, FAR = range(3)
OWN, CHIP, LINK = range(3)


def place(info, who, group):
    above = (info[1] == 1) == (who == CHIP)
    return jnp.where(above, 0, group), jnp.where(above, 0, 2)


def shared_rows(info, who, group):
    return pl.ds(pl.multiple_of(place(info, who, group)[0], 64), 2 * group)


def low_half(rows):
    return lax.broadcasted_iota(jnp.int32, (rows, LANES), 1) < LANES // 2


def store_fold(out_ref, base, value):
    rows = value.shape[0]
    half = rows // 2
    tail = value[:, LANES:]
    out_ref[pl.ds(base, rows), :] = value[:, :LANES]
    out_ref[pl.ds(base + rows, half), :] = jnp.where(
        low_half(half), tail[:half], pltpu.roll(tail[half:], LANES // 2, 1)
    )


def unfold(packed):
    rows = packed.shape[0] * 2 // 3
    half = rows // 2
    tail = packed[rows:]
    keep = low_half(half)
    upper = jnp.where(keep, tail, 0.0)
    lower = jnp.where(keep, pltpu.roll(tail, LANES // 2, 1), 0.0)
    return jnp.concatenate([packed[:rows], jnp.concatenate([upper, lower], 0)], 1)


def tile_groups(info, tile_ref, at):
    keep = low_half(at.size)
    first = jnp.concatenate([tile_ref[at, 0:128], jnp.where(keep, tile_ref[at, 128:256], 0.0)], 1)
    one = pltpu.roll(tile_ref[at, 128:256], LANES // 2, 1)
    two = pltpu.roll(tile_ref[at, 256:384], LANES // 2, 1)
    middle = jnp.concatenate([jnp.where(keep, one, two), jnp.where(keep, two, 0.0)], 1)
    end = tile_ref[at, 512:576]
    last = jnp.concatenate([tile_ref[at, 384:512], jnp.concatenate([end, jnp.zeros_like(end)], 1)], 1)
    odd = info[0] == 1
    return jnp.where(odd, first, last), middle, jnp.where(odd, last, first)


def split(value):
    high = value.astype(BF16)
    return high, (value - high.astype(F32)).astype(BF16)


def store_left(out_ref, at, value):
    out_ref[(0,) + at], out_ref[(1,) + at] = split(value)


def store_right(out_ref, at, value):
    group = value.shape[0] // 3
    for half, part in enumerate(split(value)):
        for ky in range(3):
            out_ref[(half,) + at + (pl.ds(ky * WIDE, group),)] = part[ky * group : (ky + 1) * group]
            out_ref[(half,) + at + (pl.ds(ky * WIDE + group, WIDE - group),)] = jnp.zeros((WIDE - group, WIDE), BF16)


def left(ref, *at):
    return ref[(0,) + at], ref[(1,) + at]


def right(ref, info, who, *at):
    start = WIDE if who == OWN else pl.multiple_of(place(info, who, 0)[1] * WIDE, WIDE)
    rows = (pl.ds(start, WIDE),)
    return ref[(0,) + at + rows], ref[(1,) + at + rows]


def passes(lefts, rights):
    wide = [high for high, _ in lefts] + [low for _, low in lefts] + [high for high, _ in lefts]
    tall = [high for high, _ in rights] + [high for high, _ in rights] + [low for _, low in rights]
    return jnp.dot(jnp.concatenate(wide, 1), jnp.concatenate(tall, 0), preferred_element_type=F32)


def mask_at(info, part):
    return 3 if part == MID else jnp.where((info[0] == 1) == (part == NEAR), 0, 6)


def masked(value, kept_ref, start, first_row=0):
    lane = lax.broadcasted_iota(jnp.int32, (8, WIDE), 1)

    def flags(i):
        one, two, three = (kept_ref[first_row + i, start + j] for j in range(3))
        return jnp.where(lane < 64, one, jnp.where(lane < 128, two, three)).astype(F32)[:1]

    return jnp.concatenate([value[i * 64 : (i + 1) * 64] * flags(i) for i in range(value.shape[0] // 64)], 0)


def pack_first_body(info, tile, mid, link_a, chip):
    side = tile.shape[0]
    group = side // 3
    store_fold(mid, 0, tile_groups(info, tile, pl.ds(0, side))[MID])
    groups = tile_groups(info, tile, shared_rows(info, LINK, group))
    store_fold(link_a, 0, groups[MID])
    store_fold(link_a, 3 * group, groups[NEAR])
    groups = tile_groups(info, tile, shared_rows(info, CHIP, group))
    for part in range(3):
        store_fold(chip, part * 3 * group, groups[part])


def pack_rest_body(info, tile, link_b, near, far):
    side = tile.shape[0]
    groups = tile_groups(info, tile, pl.ds(0, side))
    store_fold(near, 0, groups[NEAR])
    store_fold(far, 0, groups[FAR])
    store_fold(link_b, 0, tile_groups(info, tile, shared_rows(info, LINK, side // 3))[FAR])


def prepare_body(info, tile, chip, own_left, own_right, chip_left):
    side = tile.shape[0]
    for part, value in enumerate(tile_groups(info, tile, pl.ds(0, side))):
        store_left(own_left, (part,), value)
        store_right(own_right, (part,), value)
        store_left(chip_left, (part,), unfold(chip[part * side : (part + 1) * side, :]))


def near_start_body(info, mid, own_left, own_right, chip_left, out, rights):
    group = mid.shape[0] * 2 // 9
    store_right(rights, (), unfold(mid[...]))
    for who, lefts in ((OWN, own_left), (CHIP, chip_left)):
        value = passes(
            [left(lefts, NEAR), left(lefts, MID)], [right(rights, info, who), right(own_right, info, who, NEAR)]
        )
        if who == OWN:
            out[...] = value
        else:
            out[shared_rows(info, who, group), :] += value


def near_body(info, kept, link_a, begun, own_right, right_near, out, link, link_left):
    group = link_a.shape[0] // 6
    for part, base in ((MID, 0), (NEAR, 3 * group)):
        store_left(link_left, (part,), unfold(link_a[base : base + 3 * group, :]))
    out[...] = begun[...]
    out[shared_rows(info, LINK, group), :] += passes(
        [left(link_left, NEAR), left(link_left, MID)],
        [right(right_near, info, LINK), right(own_right, info, LINK, NEAR)],
    )
    out[...] = masked(out[...], kept, mask_at(info, NEAR))
    store_fold(link, 0, out[shared_rows(info, LINK, group), :])


def middle_products_body(info, own_left, own_right, chip_left, link_left, far, mid):
    group = far.shape[0] // 3
    for out, part in ((far, FAR), (mid, MID)):
        for who, lefts in ((OWN, own_left), (CHIP, chip_left), (LINK, link_left)):
            value = passes([left(lefts, MID)], [right(own_right, info, who, part)])
            if who == OWN:
                out[...] = value
            else:
                out[shared_rows(info, who, group), :] += value


def far_body(info, kept, link_b, mid, begun, s_near, own_left, chip_left, out, link, sides, link_left, rights):
    group = out.shape[0] // 3
    store_left(link_left, (), unfold(link_b[...]))
    store_right(rights, (), unfold(mid[...]))
    out[...] = begun[...] + passes([left(own_left, FAR)], [right(rights, info, OWN)])
    for who, factor in ((CHIP, left(chip_left, FAR)), (LINK, left(link_left))):
        out[shared_rows(info, who, group), :] += passes([factor], [right(rights, info, who)])
    out[...] = masked(out[...], kept, mask_at(info, FAR))
    store_fold(link, 0, out[shared_rows(info, LINK, group), :])
    store_fold(sides, 0, s_near[shared_rows(info, CHIP, group), :])
    store_fold(sides, 3 * group, out[shared_rows(info, CHIP, group), :])


def mid_start_body(info, near, begun, own_left, chip_left, link_left, out, rights):
    group = out.shape[0] // 3
    store_right(rights, (), unfold(near[...]))
    out[...] = begun[...] + passes([left(own_left, NEAR)], [right(rights, info, OWN)])
    for who, lefts in ((CHIP, chip_left), (LINK, link_left)):
        out[shared_rows(info, who, group), :] += passes([left(lefts, NEAR)], [right(rights, info, who)])


def mid_body(info, kept, far, own_left, chip_left, link_left, begun, out, chip, link, rights):
    group = out.shape[0] // 3
    store_right(rights, (), unfold(far[...]))
    out[...] = begun[...] + passes([left(own_left, FAR)], [right(rights, info, OWN)])
    for who, factor in ((CHIP, left(chip_left, FAR)), (LINK, left(link_left))):
        out[shared_rows(info, who, group), :] += passes([factor], [right(rights, info, who)])
    out[...] = masked(out[...], kept, 3)
    store_fold(link, 0, out[shared_rows(info, LINK, group), :])
    store_fold(chip, 0, out[shared_rows(info, CHIP, group), :])


def cube_near_body(info, link, near, far, right_near, right_far, right_mid, out):
    group = near.shape[0] // 3
    own, other = split(near[...]), split(unfold(link[...]))
    out[FAR] = passes([split(far[...])], [right(right_far, info, OWN)])
    for part, ref in ((NEAR, right_near), (MID, right_mid)):
        out[part] = passes([own], [right(ref, info, OWN)])
        out[part, shared_rows(info, LINK, group), :] += passes([other], [right(ref, info, LINK)])


def cube_own_body(info, link, total, near, mid, far, own_right, right_far, mid_far, out):
    group = near.shape[0] // 3
    own_mid, own_far = split(mid[...]), split(far[...])
    link_far = split(unfold(link[...]))
    rights = [right(own_right, info, OWN, part) for part in range(3)]
    out[NEAR] = 3.0 * near[...] - 2.0 * (total[NEAR] + passes([own_mid], rights[NEAR:MID]))
    out[MID] = 3.0 * mid[...] - 2.0 * (total[MID] + passes([own_mid, own_far], [rights[MID], right(mid_far, info, OWN)]))
    out[FAR] = 3.0 * far[...] - 2.0 * (total[FAR] + passes([own_mid], rights[FAR:]))
    for part, ref in ((MID, mid_far), (FAR, right_far)):
        out[part, shared_rows(info, LINK, group), :] -= 2.0 * passes([link_far], [right(ref, info, LINK)])


def send_rows(info, tile, out, sem, row, near, mid, far):
    odd = info[0] == 1
    group = near.shape[0]
    tile[:, :group] = jnp.where(odd, near, far)[:, :group]
    tile[:, group : 2 * group] = mid[:, :group]
    tile[:, 2 * group :] = jnp.where(odd, far, near)[:, :group]
    copy = pltpu.make_async_copy(tile, out.at[pl.ds(row, group), :], sem)
    copy.start()
    return copy


def cube_chip_body(info, kept, sides, chip, own_right, right_near, right_far, mid_near, mid_far, base, out, result, tile, sem):
    group = base.shape[1] // 3
    chip_start = place(info, CHIP, group)[0]
    rest = pl.multiple_of(2 * chip_start, 64)
    link_only = pl.multiple_of(2 * (group - chip_start), 64)
    chips = [split(unfold(value)) for value in (sides[: 3 * group, :], chip[...], sides[3 * group :, :])]
    own = [right(own_right, info, CHIP, part) for part in range(3)]
    products = (
        (chips[:2], [right(right_near, info, CHIP), own[NEAR]]),
        (chips, [right(mid_near, info, CHIP), own[MID], right(mid_far, info, CHIP)]),
        (chips[1:], [own[FAR], right(right_far, info, CHIP)]),
    )
    for part, factors in enumerate(products):
        out[part, shared_rows(info, CHIP, group), :] = base[part, shared_rows(info, CHIP, group), :] - 2.0 * passes(*factors)

    def finished(row):
        at = pl.ds(row, group)
        return [masked(out[part, at, :], kept, mask_at(info, part), row // 64) for part in range(3)]

    copy = send_rows(info, tile, result, sem, rest, *finished(rest))
    for part in range(3):
        out[part, pl.ds(link_only, group), :] = base[part, pl.ds(link_only, group), :]
    for row in (group, link_only):
        for part, value in enumerate(finished(row)):
            out[part, pl.ds(row, group), :] = value
    copy.wait()


def finish_body(info, kept, link, own_right, base, begun, result, tile, sem):
    del begun
    group = tile.shape[1]
    start, first_row = place(info, LINK, group)[0], place(info, LINK, 3)[0]
    link_mid = unfold(link[...])
    copies = []
    for half in range(2):
        factor = split(link_mid[half * group : (half + 1) * group])
        row = pl.multiple_of(start + half * group, 64)
        values = []
        for part in range(3):
            value = -2.0 * passes([factor], [right(own_right, info, LINK, part)])
            value = masked(value, kept, mask_at(info, part), first_row + 3 * half)
            values.append(base[part, pl.ds(row, group), :] + value)
        copies.append(send_rows(info, tile.at[half], result, sem.at[half], row, *values))
    for copy in copies:
        copy.wait()


VMEM = pl.BlockSpec(memory_space=pltpu.VMEM)
SMEM = pl.BlockSpec(memory_space=pltpu.SMEM)
ANY = pl.BlockSpec(memory_space=pl.ANY)


def call(body, name, scalars, arrays, outs, work=4, result=False, begun=(), scratch=()):
    count = len(scalars) + len(arrays)
    return pl.pallas_call(
        body,
        out_shape=[jax.ShapeDtypeStruct(shape, kind) for shape, kind in outs],
        in_specs=[SMEM] * len(scalars) + [VMEM] * len(arrays) + [ANY] * len(begun),
        out_specs=[VMEM] * (len(outs) - result) + [ANY] * result,
        scratch_shapes=scratch,
        input_output_aliases={count: len(outs) - 1} if begun else {},
        compiler_params=pltpu.CompilerParams(vmem_limit_bytes=24 << 20),
        cost_estimate=pl.CostEstimate(flops=work * 1000000000, transcendentals=0, bytes_accessed=work * 5000000),
        name=name,
    )(*scalars, *arrays, *begun)


def on_device(p_tiles, square_kept, result_kept):
    side = p_tiles.shape[0]
    group = side // 3
    n_row, n_col = lax.axis_size("row"), lax.axis_size("col")
    info = jnp.stack([lax.axis_index("row") % 2, lax.axis_index("col") % 2]).astype(jnp.int32)
    strip = ((3 * side // 2, LANES), F32)
    slab = ((3 * group, LANES), F32)
    two_slabs = ((6 * group, LANES), F32)
    three_slabs = ((9 * group, LANES), F32)
    wide = ((side, WIDE), F32)
    three_wide = ((3, side, WIDE), F32)
    rights = ((2, 3 * WIDE, WIDE), BF16)

    def exchange(value, axis, even_step):
        size = n_row if axis == "row" else n_col
        return lax.ppermute(
            value, axis, [(i, (i + (even_step if i % 2 == 0 else -even_step)) % size) for i in range(size)]
        )

    mid, link_a, chip = call(
        pack_first_body, "pack_first", (info,), (p_tiles,), [strip, two_slabs, three_slabs]
    )
    link_a = exchange(link_a, "col", -1)
    partner_mid = exchange(mid, "row", 1)
    chip = exchange(chip, "col", 1)
    chip, tile = lax.optimization_barrier((chip, p_tiles))
    link_b, near, far = call(pack_rest_body, "pack_rest", (info,), (tile,), [slab, strip, strip])
    partner_near = exchange(near, "row", 1)
    link_b = exchange(link_b, "col", -1)
    passed_far = exchange(far, "row", -2)

    own_left, own_right, chip_left = call(
        prepare_body,
        "prepare",
        (info,),
        (p_tiles, chip),
        [((2, 3, side, WIDE), BF16), ((2, 3, 3 * WIDE, WIDE), BF16), ((2, 3, 2 * group, WIDE), BF16)],
    )
    partner_mid, own_left = lax.optimization_barrier((partner_mid, own_left))
    other_mid = exchange(partner_mid, "row", 2)
    begun, right_near = call(
        near_start_body, "near_start", (info,), (partner_mid, own_left, own_right, chip_left), [wide, rights]
    )
    s_near, near_link, link_left = call(
        near_body,
        "square_near",
        (info, square_kept),
        (link_a, begun, own_right, right_near),
        [wide, slab, ((2, 2, 2 * group, WIDE), BF16)],
    )
    near_link = exchange(near_link, "col", -1)
    passed_far, link_left = lax.optimization_barrier((passed_far, link_left))
    other_far = exchange(passed_far, "row", 1)
    begun, begun_mid = call(
        middle_products_body, "middle_products", (info,), (own_left, own_right, chip_left, link_left), [wide] * 2
    )
    begun_mid, mid_near = call(
        mid_start_body,
        "mid_start",
        (info,),
        (partner_near, begun_mid, own_left, chip_left, link_left),
        [wide, rights],
    )
    begun, begun_mid = lax.optimization_barrier((begun, begun_mid))
    s_far, far_link, sides_chip, link_left_far, right_far = call(
        far_body,
        "square_far",
        (info, square_kept),
        (link_b, other_mid, begun, s_near, own_left, chip_left),
        [wide, slab, two_slabs, ((2, 2 * group, WIDE), BF16), rights],
    )
    far_link = exchange(far_link, "col", -1)
    sides_chip = exchange(sides_chip, "col", 1)
    (total,) = call(
        cube_near_body,
        "cube_near",
        (info,),
        (near_link, s_near, s_far, right_near, right_far, mid_near),
        [three_wide],
    )
    total, other_far = lax.optimization_barrier((total, other_far))
    s_mid, mid_chip, mid_link, mid_far = call(
        mid_body,
        "square_mid",
        (info, square_kept),
        (other_far, own_left, chip_left, link_left_far, begun_mid),
        [wide, slab, slab, rights],
        work=0,
    )
    mid_link = exchange(mid_link, "col", -1)
    mid_chip = exchange(mid_chip, "col", 1)
    (base,) = call(
        cube_own_body,
        "cube_own",
        (info,),
        (far_link, total, s_near, s_mid, s_far, own_right, right_far, mid_far),
        [three_wide],
    )
    result = ((side, side), F32)
    base, purified = call(
        cube_chip_body,
        "cube_chip",
        (info, result_kept),
        (sides_chip, mid_chip, own_right, right_near, right_far, mid_near, mid_far, base),
        [three_wide, result],
        result=True,
        scratch=[pltpu.VMEM((group, side), F32), pltpu.SemaphoreType.DMA(())],
    )
    (purified,) = call(
        finish_body,
        "finish",
        (info, result_kept),
        (mid_link, own_right, base),
        [result],
        result=True,
        begun=(purified,),
        scratch=[pltpu.VMEM((2, group, side), F32), pltpu.SemaphoreType.DMA((2,))],
    )
    return purified


def solution(mesh):
    return jax.shard_map(
        on_device,
        mesh=mesh,
        in_specs=(P("row", "col"), P("row", "col"), P("row", "col")),
        out_specs=P("row", "col"),
        check_vma=False,
    )
```

```python
import jax
import jax.numpy as jnp
from jax import lax
from jax.experimental import pallas as pl
from jax.experimental.pallas import tpu as pltpu
from jax.sharding import PartitionSpec as P

LANES = 128
WIDE = 256
F32 = jnp.float32
BF16 = jnp.bfloat16
NEAR, MID, FAR = range(3)
OWN, CHIP, LINK = range(3)


def place(info, who, group):
    above = (info[1] == 1) == (who == CHIP)
    return jnp.where(above, 0, group), jnp.where(above, 0, 2)


def shared_rows(info, who, group):
    return pl.ds(pl.multiple_of(place(info, who, group)[0], 64), 2 * group)


def low_half(rows):
    return lax.broadcasted_iota(jnp.int32, (rows, LANES), 1) < LANES // 2


def store_fold(out_ref, base, value):
    rows = value.shape[0]
    half = rows // 2
    tail = value[:, LANES:]
    out_ref[pl.ds(base, rows), :] = value[:, :LANES]
    out_ref[pl.ds(base + rows, half), :] = jnp.where(
        low_half(half), tail[:half], pltpu.roll(tail[half:], LANES // 2, 1)
    )


def unfold(packed):
    rows = packed.shape[0] * 2 // 3
    half = rows // 2
    tail = packed[rows:]
    keep = low_half(half)
    upper = jnp.where(keep, tail, 0.0)
    lower = jnp.where(keep, pltpu.roll(tail, LANES // 2, 1), 0.0)
    return jnp.concatenate([packed[:rows], jnp.concatenate([upper, lower], 0)], 1)


def tile_groups(info, tile_ref, at):
    keep = low_half(at.size)
    first = jnp.concatenate([tile_ref[at, 0:128], jnp.where(keep, tile_ref[at, 128:256], 0.0)], 1)
    one = pltpu.roll(tile_ref[at, 128:256], LANES // 2, 1)
    two = pltpu.roll(tile_ref[at, 256:384], LANES // 2, 1)
    middle = jnp.concatenate([jnp.where(keep, one, two), jnp.where(keep, two, 0.0)], 1)
    end = tile_ref[at, 512:576]
    last = jnp.concatenate([tile_ref[at, 384:512], jnp.concatenate([end, jnp.zeros_like(end)], 1)], 1)
    odd = info[0] == 1
    return jnp.where(odd, first, last), middle, jnp.where(odd, last, first)


def split(value):
    high = value.astype(BF16)
    return high, (value - high.astype(F32)).astype(BF16)


def store_left(out_ref, at, value):
    out_ref[(0,) + at], out_ref[(1,) + at] = split(value)


def store_right(out_ref, at, value):
    group = value.shape[0] // 3
    for half, part in enumerate(split(value)):
        for ky in range(3):
            out_ref[(half,) + at + (pl.ds(ky * WIDE, group),)] = part[ky * group : (ky + 1) * group]
            out_ref[(half,) + at + (pl.ds(ky * WIDE + group, WIDE - group),)] = jnp.zeros((WIDE - group, WIDE), BF16)


def left(ref, *at):
    return ref[(0,) + at], ref[(1,) + at]


def right(ref, info, who, *at):
    start = WIDE if who == OWN else pl.multiple_of(place(info, who, 0)[1] * WIDE, WIDE)
    rows = (pl.ds(start, WIDE),)
    return ref[(0,) + at + rows], ref[(1,) + at + rows]


def passes(lefts, rights):
    wide = [high for high, _ in lefts] + [low for _, low in lefts] + [high for high, _ in lefts]
    tall = [high for high, _ in rights] + [high for high, _ in rights] + [low for _, low in rights]
    return jnp.dot(jnp.concatenate(wide, 1), jnp.concatenate(tall, 0), preferred_element_type=F32)


def mask_at(info, part):
    return 3 if part == MID else jnp.where((info[0] == 1) == (part == NEAR), 0, 6)


def masked(value, kept_ref, start, first_row=0):
    lane = lax.broadcasted_iota(jnp.int32, (8, WIDE), 1)

    def flags(i):
        one, two, three = (kept_ref[first_row + i, start + j] for j in range(3))
        return jnp.where(lane < 64, one, jnp.where(lane < 128, two, three)).astype(F32)[:1]

    return jnp.concatenate([value[i * 64 : (i + 1) * 64] * flags(i) for i in range(value.shape[0] // 64)], 0)


def pack_first_body(info, tile, mid, link_a, chip):
    side = tile.shape[0]
    group = side // 3
    store_fold(mid, 0, tile_groups(info, tile, pl.ds(0, side))[MID])
    groups = tile_groups(info, tile, shared_rows(info, LINK, group))
    store_fold(link_a, 0, groups[MID])
    store_fold(link_a, 3 * group, groups[NEAR])
    groups = tile_groups(info, tile, shared_rows(info, CHIP, group))
    for part in range(3):
        store_fold(chip, part * 3 * group, groups[part])


def pack_rest_body(info, tile, link_b, near, far):
    side = tile.shape[0]
    groups = tile_groups(info, tile, pl.ds(0, side))
    store_fold(near, 0, groups[NEAR])
    store_fold(far, 0, groups[FAR])
    store_fold(link_b, 0, tile_groups(info, tile, shared_rows(info, LINK, side // 3))[FAR])


def prepare_body(info, tile, chip, own_left, own_right, chip_left):
    side = tile.shape[0]
    for part, value in enumerate(tile_groups(info, tile, pl.ds(0, side))):
        store_left(own_left, (part,), value)
        store_right(own_right, (part,), value)
        store_left(chip_left, (part,), unfold(chip[part * side : (part + 1) * side, :]))


def near_start_body(info, mid, own_left, own_right, chip_left, out, rights):
    group = mid.shape[0] * 2 // 9
    store_right(rights, (), unfold(mid[...]))
    for who, lefts in ((OWN, own_left), (CHIP, chip_left)):
        value = passes(
            [left(lefts, NEAR), left(lefts, MID)], [right(rights, info, who), right(own_right, info, who, NEAR)]
        )
        if who == OWN:
            out[...] = value
        else:
            out[shared_rows(info, who, group), :] += value


def near_body(info, kept, link_a, begun, own_right, right_near, out, link, link_left):
    group = link_a.shape[0] // 6
    for part, base in ((MID, 0), (NEAR, 3 * group)):
        store_left(link_left, (part,), unfold(link_a[base : base + 3 * group, :]))
    out[...] = begun[...]
    out[shared_rows(info, LINK, group), :] += passes(
        [left(link_left, NEAR), left(link_left, MID)],
        [right(right_near, info, LINK), right(own_right, info, LINK, NEAR)],
    )
    out[...] = masked(out[...], kept, mask_at(info, NEAR))
    store_fold(link, 0, out[shared_rows(info, LINK, group), :])


def middle_products_body(info, own_left, own_right, chip_left, far, mid):
    group = far.shape[0] // 3
    for out, part in ((far, FAR), (mid, MID)):
        out[...] = passes([left(own_left, MID)], [right(own_right, info, OWN, part)])
        out[shared_rows(info, CHIP, group), :] += passes([left(chip_left, MID)], [right(own_right, info, CHIP, part)])


def middle_link_body(info, own_right, link_left, begun_far, begun_mid, far, mid):
    group = far.shape[0] // 3
    for out, begun, part in ((far, begun_far, FAR), (mid, begun_mid, MID)):
        out[...] = begun[...]
        out[shared_rows(info, LINK, group), :] += passes([left(link_left, MID)], [right(own_right, info, LINK, part)])


def far_body(info, kept, link_b, mid, begun, s_near, own_left, chip_left, out, link, sides, link_left, rights):
    group = out.shape[0] // 3
    store_left(link_left, (), unfold(link_b[...]))
    store_right(rights, (), unfold(mid[...]))
    out[...] = begun[...] + passes([left(own_left, FAR)], [right(rights, info, OWN)])
    for who, factor in ((CHIP, left(chip_left, FAR)), (LINK, left(link_left))):
        out[shared_rows(info, who, group), :] += passes([factor], [right(rights, info, who)])
    out[...] = masked(out[...], kept, mask_at(info, FAR))
    store_fold(link, 0, out[shared_rows(info, LINK, group), :])
    store_fold(sides, 0, s_near[shared_rows(info, CHIP, group), :])
    store_fold(sides, 3 * group, out[shared_rows(info, CHIP, group), :])


def mid_start_body(info, near, begun, own_left, chip_left, link_left, out, rights):
    group = out.shape[0] // 3
    store_right(rights, (), unfold(near[...]))
    out[...] = begun[...] + passes([left(own_left, NEAR)], [right(rights, info, OWN)])
    for who, lefts in ((CHIP, chip_left), (LINK, link_left)):
        out[shared_rows(info, who, group), :] += passes([left(lefts, NEAR)], [right(rights, info, who)])


def mid_body(info, kept, far, own_left, chip_left, link_left, begun, out, chip, link, rights):
    group = out.shape[0] // 3
    store_right(rights, (), unfold(far[...]))
    out[...] = begun[...] + passes([left(own_left, FAR)], [right(rights, info, OWN)])
    for who, factor in ((CHIP, left(chip_left, FAR)), (LINK, left(link_left))):
        out[shared_rows(info, who, group), :] += passes([factor], [right(rights, info, who)])
    out[...] = masked(out[...], kept, 3)
    store_fold(link, 0, out[shared_rows(info, LINK, group), :])
    store_fold(chip, 0, out[shared_rows(info, CHIP, group), :])


def cube_near_body(info, link, near, far, right_near, right_far, right_mid, out):
    group = near.shape[0] // 3
    own, other = split(near[...]), split(unfold(link[...]))
    out[FAR] = passes([split(far[...])], [right(right_far, info, OWN)])
    for part, ref in ((NEAR, right_near), (MID, right_mid)):
        out[part] = passes([own], [right(ref, info, OWN)])
        out[part, shared_rows(info, LINK, group), :] += passes([other], [right(ref, info, LINK)])


def cube_own_body(info, link, total, near, mid, far, own_right, right_far, mid_far, out):
    group = near.shape[0] // 3
    own_mid, own_far = split(mid[...]), split(far[...])
    link_far = split(unfold(link[...]))
    rights = [right(own_right, info, OWN, part) for part in range(3)]
    out[NEAR] = 3.0 * near[...] - 2.0 * (total[NEAR] + passes([own_mid], rights[NEAR:MID]))
    out[MID] = 3.0 * mid[...] - 2.0 * (total[MID] + passes([own_mid, own_far], [rights[MID], right(mid_far, info, OWN)]))
    out[FAR] = 3.0 * far[...] - 2.0 * (total[FAR] + passes([own_mid], rights[FAR:]))
    for part, ref in ((MID, mid_far), (FAR, right_far)):
        out[part, shared_rows(info, LINK, group), :] -= 2.0 * passes([link_far], [right(ref, info, LINK)])


def send_rows(info, tile, out, sem, row, near, mid, far):
    odd = info[0] == 1
    group = near.shape[0]
    tile[:, :group] = jnp.where(odd, near, far)[:, :group]
    tile[:, group : 2 * group] = mid[:, :group]
    tile[:, 2 * group :] = jnp.where(odd, far, near)[:, :group]
    copy = pltpu.make_async_copy(tile, out.at[pl.ds(row, group), :], sem)
    copy.start()
    return copy


def cube_chip_body(info, kept, sides, chip, own_right, right_near, right_far, mid_near, mid_far, base, out, result, tile, sem):
    group = base.shape[1] // 3
    chip_start = place(info, CHIP, group)[0]
    rest = pl.multiple_of(2 * chip_start, 64)
    link_only = pl.multiple_of(2 * (group - chip_start), 64)
    chips = [split(unfold(value)) for value in (sides[: 3 * group, :], chip[...], sides[3 * group :, :])]
    own = [right(own_right, info, CHIP, part) for part in range(3)]
    products = (
        (chips[:2], [right(right_near, info, CHIP), own[NEAR]]),
        (chips, [right(mid_near, info, CHIP), own[MID], right(mid_far, info, CHIP)]),
        (chips[1:], [own[FAR], right(right_far, info, CHIP)]),
    )
    for part, factors in enumerate(products):
        out[part, shared_rows(info, CHIP, group), :] = base[part, shared_rows(info, CHIP, group), :] - 2.0 * passes(*factors)

    def finished(row):
        at = pl.ds(row, group)
        return [masked(out[part, at, :], kept, mask_at(info, part), row // 64) for part in range(3)]

    copy = send_rows(info, tile, result, sem, rest, *finished(rest))
    for part in range(3):
        out[part, pl.ds(link_only, group), :] = base[part, pl.ds(link_only, group), :]
    for row in (group, link_only):
        for part, value in enumerate(finished(row)):
            out[part, pl.ds(row, group), :] = value
    copy.wait()


def finish_body(info, kept, link, own_right, base, begun, result, tile, sem):
    del begun
    group = tile.shape[1]
    start, first_row = place(info, LINK, group)[0], place(info, LINK, 3)[0]
    link_mid = unfold(link[...])
    copies = []
    for half in range(2):
        factor = split(link_mid[half * group : (half + 1) * group])
        row = pl.multiple_of(start + half * group, 64)
        values = []
        for part in range(3):
            value = -2.0 * passes([factor], [right(own_right, info, LINK, part)])
            value = masked(value, kept, mask_at(info, part), first_row + 3 * half)
            values.append(base[part, pl.ds(row, group), :] + value)
        copies.append(send_rows(info, tile.at[half], result, sem.at[half], row, *values))
    for copy in copies:
        copy.wait()


VMEM = pl.BlockSpec(memory_space=pltpu.VMEM)
SMEM = pl.BlockSpec(memory_space=pltpu.SMEM)
ANY = pl.BlockSpec(memory_space=pl.ANY)


def call(body, name, scalars, arrays, outs, work=4, result=False, begun=(), scratch=()):
    count = len(scalars) + len(arrays)
    return pl.pallas_call(
        body,
        out_shape=[jax.ShapeDtypeStruct(shape, kind) for shape, kind in outs],
        in_specs=[SMEM] * len(scalars) + [VMEM] * len(arrays) + [ANY] * len(begun),
        out_specs=[VMEM] * (len(outs) - result) + [ANY] * result,
        scratch_shapes=scratch,
        input_output_aliases={count: len(outs) - 1} if begun else {},
        compiler_params=pltpu.CompilerParams(vmem_limit_bytes=24 << 20),
        cost_estimate=pl.CostEstimate(flops=work * 1000000000, transcendentals=0, bytes_accessed=work * 5000000),
        name=name,
    )(*scalars, *arrays, *begun)


def on_device(p_tiles, square_kept, result_kept):
    side = p_tiles.shape[0]
    group = side // 3
    n_row, n_col = lax.axis_size("row"), lax.axis_size("col")
    info = jnp.stack([lax.axis_index("row") % 2, lax.axis_index("col") % 2]).astype(jnp.int32)
    strip = ((3 * side // 2, LANES), F32)
    slab = ((3 * group, LANES), F32)
    two_slabs = ((6 * group, LANES), F32)
    three_slabs = ((9 * group, LANES), F32)
    wide = ((side, WIDE), F32)
    three_wide = ((3, side, WIDE), F32)
    rights = ((2, 3 * WIDE, WIDE), BF16)

    def exchange(value, axis, even_step):
        size = n_row if axis == "row" else n_col
        return lax.ppermute(
            value, axis, [(i, (i + (even_step if i % 2 == 0 else -even_step)) % size) for i in range(size)]
        )

    mid, link_a, chip = call(
        pack_first_body, "pack_first", (info,), (p_tiles,), [strip, two_slabs, three_slabs]
    )
    link_a = exchange(link_a, "col", -1)
    partner_mid = exchange(mid, "row", 1)
    chip = exchange(chip, "col", 1)
    chip, tile = lax.optimization_barrier((chip, p_tiles))
    link_b, near, far = call(pack_rest_body, "pack_rest", (info,), (tile,), [slab, strip, strip])
    partner_near = exchange(near, "row", 1)
    link_b = exchange(link_b, "col", -1)
    passed_far = exchange(far, "row", -2)

    own_left, own_right, chip_left = call(
        prepare_body,
        "prepare",
        (info,),
        (p_tiles, chip),
        [((2, 3, side, WIDE), BF16), ((2, 3, 3 * WIDE, WIDE), BF16), ((2, 3, 2 * group, WIDE), BF16)],
    )
    begun_far, begun_mid = call(
        middle_products_body, "middle_products", (info,), (own_left, own_right, chip_left), [wide] * 2
    )
    partner_mid, own_left, begun_mid = lax.optimization_barrier((partner_mid, own_left, begun_mid))
    other_mid = exchange(partner_mid, "row", 2)
    begun, right_near = call(
        near_start_body, "near_start", (info,), (partner_mid, own_left, own_right, chip_left), [wide, rights]
    )
    s_near, near_link, link_left = call(
        near_body,
        "square_near",
        (info, square_kept),
        (link_a, begun, own_right, right_near),
        [wide, slab, ((2, 2, 2 * group, WIDE), BF16)],
    )
    near_link = exchange(near_link, "col", -1)
    passed_far, link_left = lax.optimization_barrier((passed_far, link_left))
    other_far = exchange(passed_far, "row", 1)
    begun_far, begun_mid = call(
        middle_link_body, "middle_link", (info,), (own_right, link_left, begun_far, begun_mid), [wide] * 2
    )
    begun_mid, mid_near = call(
        mid_start_body,
        "mid_start",
        (info,),
        (partner_near, begun_mid, own_left, chip_left, link_left),
        [wide, rights],
    )
    begun_far, begun_mid = lax.optimization_barrier((begun_far, begun_mid))
    s_far, far_link, sides_chip, link_left_far, right_far = call(
        far_body,
        "square_far",
        (info, square_kept),
        (link_b, other_mid, begun_far, s_near, own_left, chip_left),
        [wide, slab, two_slabs, ((2, 2 * group, WIDE), BF16), rights],
    )
    far_link = exchange(far_link, "col", -1)
    sides_chip = exchange(sides_chip, "col", 1)
    near_link, other_far = lax.optimization_barrier((near_link, other_far))
    (total,) = call(
        cube_near_body,
        "cube_near",
        (info,),
        (near_link, s_near, s_far, right_near, right_far, mid_near),
        [three_wide],
    )
    total, other_far = lax.optimization_barrier((total, other_far))
    s_mid, mid_chip, mid_link, mid_far = call(
        mid_body,
        "square_mid",
        (info, square_kept),
        (other_far, own_left, chip_left, link_left_far, begun_mid),
        [wide, slab, slab, rights],
        work=0,
    )
    mid_link = exchange(mid_link, "col", -1)
    mid_chip = exchange(mid_chip, "col", 1)
    (base,) = call(
        cube_own_body,
        "cube_own",
        (info,),
        (far_link, total, s_near, s_mid, s_far, own_right, right_far, mid_far),
        [three_wide],
    )
    result = ((side, side), F32)
    base, purified = call(
        cube_chip_body,
        "cube_chip",
        (info, result_kept),
        (sides_chip, mid_chip, own_right, right_near, right_far, mid_near, mid_far, base),
        [three_wide, result],
        result=True,
        scratch=[pltpu.VMEM((group, side), F32), pltpu.SemaphoreType.DMA(())],
    )
    (purified,) = call(
        finish_body,
        "finish",
        (info, result_kept),
        (mid_link, own_right, base),
        [result],
        result=True,
        begun=(purified,),
        scratch=[pltpu.VMEM((2, group, side), F32), pltpu.SemaphoreType.DMA((2,))],
    )
    return purified


def solution(mesh):
    return jax.shard_map(
        on_device,
        mesh=mesh,
        in_specs=(P("row", "col"), P("row", "col"), P("row", "col")),
        out_specs=P("row", "col"),
        check_vma=False,
    )
```

```python
import jax
import jax.numpy as jnp
from jax import lax
from jax.experimental import pallas as pl
from jax.experimental.pallas import tpu as pltpu
from jax.sharding import PartitionSpec as P

LANES = 128
WIDE = 256
F32 = jnp.float32
BF16 = jnp.bfloat16
NEAR, MID, FAR = range(3)
OWN, CHIP, LINK = range(3)


def place(info, who, group):
    above = (info[1] == 1) == (who == CHIP)
    return jnp.where(above, 0, group), jnp.where(above, 0, 2)


def shared_rows(info, who, group):
    return pl.ds(pl.multiple_of(place(info, who, group)[0], 64), 2 * group)


def low_half(rows):
    return lax.broadcasted_iota(jnp.int32, (rows, LANES), 1) < LANES // 2


def store_fold(out_ref, base, value):
    rows = value.shape[0]
    half = rows // 2
    tail = value[:, LANES:]
    out_ref[pl.ds(base, rows), :] = value[:, :LANES]
    out_ref[pl.ds(base + rows, half), :] = jnp.where(
        low_half(half), tail[:half], pltpu.roll(tail[half:], LANES // 2, 1)
    )


def unfold(packed):
    rows = packed.shape[0] * 2 // 3
    half = rows // 2
    tail = packed[rows:]
    keep = low_half(half)
    upper = jnp.where(keep, tail, 0.0)
    lower = jnp.where(keep, pltpu.roll(tail, LANES // 2, 1), 0.0)
    return jnp.concatenate([packed[:rows], jnp.concatenate([upper, lower], 0)], 1)


def tile_groups(info, tile_ref, at):
    keep = low_half(at.size)
    first = jnp.concatenate([tile_ref[at, 0:128], jnp.where(keep, tile_ref[at, 128:256], 0.0)], 1)
    one = pltpu.roll(tile_ref[at, 128:256], LANES // 2, 1)
    two = pltpu.roll(tile_ref[at, 256:384], LANES // 2, 1)
    middle = jnp.concatenate([jnp.where(keep, one, two), jnp.where(keep, two, 0.0)], 1)
    end = tile_ref[at, 512:576]
    last = jnp.concatenate([tile_ref[at, 384:512], jnp.concatenate([end, jnp.zeros_like(end)], 1)], 1)
    odd = info[0] == 1
    return jnp.where(odd, first, last), middle, jnp.where(odd, last, first)


def split(value):
    high = value.astype(BF16)
    return high, (value - high.astype(F32)).astype(BF16)


def store_left(out_ref, at, value):
    out_ref[(0,) + at], out_ref[(1,) + at] = split(value)


def store_right(out_ref, at, value):
    group = value.shape[0] // 3
    for half, part in enumerate(split(value)):
        for ky in range(3):
            out_ref[(half,) + at + (pl.ds(ky * WIDE, group),)] = part[ky * group : (ky + 1) * group]
            out_ref[(half,) + at + (pl.ds(ky * WIDE + group, WIDE - group),)] = jnp.zeros((WIDE - group, WIDE), BF16)


def left(ref, *at):
    return ref[(0,) + at], ref[(1,) + at]


def right(ref, info, who, *at):
    start = WIDE if who == OWN else pl.multiple_of(place(info, who, 0)[1] * WIDE, WIDE)
    rows = (pl.ds(start, WIDE),)
    return ref[(0,) + at + rows], ref[(1,) + at + rows]


def passes(lefts, rights):
    wide = [high for high, _ in lefts] + [low for _, low in lefts] + [high for high, _ in lefts]
    tall = [high for high, _ in rights] + [high for high, _ in rights] + [low for _, low in rights]
    return jnp.dot(jnp.concatenate(wide, 1), jnp.concatenate(tall, 0), preferred_element_type=F32)


def mask_at(info, part):
    return 3 if part == MID else jnp.where((info[0] == 1) == (part == NEAR), 0, 6)


def masked(value, kept_ref, start, first_row=0):
    lane = lax.broadcasted_iota(jnp.int32, (8, WIDE), 1)

    def flags(i):
        one, two, three = (kept_ref[first_row + i, start + j] for j in range(3))
        return jnp.where(lane < 64, one, jnp.where(lane < 128, two, three)).astype(F32)[:1]

    return jnp.concatenate([value[i * 64 : (i + 1) * 64] * flags(i) for i in range(value.shape[0] // 64)], 0)


def pack_first_body(info, source, mid, link_a, chip, tile, sems):
    side = tile.shape[0]
    copies = [
        pltpu.make_async_copy(source.at[pl.ds(i * side // 3, side // 3), :], tile.at[pl.ds(i * side // 3, side // 3), :], sems.at[i])
        for i in range(3)
    ]
    for copy in copies:
        copy.start()
    for copy in copies:
        copy.wait()
    group = side // 3
    store_fold(mid, 0, tile_groups(info, tile, pl.ds(0, side))[MID])
    groups = tile_groups(info, tile, shared_rows(info, LINK, group))
    store_fold(link_a, 0, groups[MID])
    store_fold(link_a, 3 * group, groups[NEAR])
    groups = tile_groups(info, tile, shared_rows(info, CHIP, group))
    for part in range(3):
        store_fold(chip, part * 3 * group, groups[part])


def pack_rest_body(info, tile, link_b, near, far):
    side = tile.shape[0]
    groups = tile_groups(info, tile, pl.ds(0, side))
    store_fold(near, 0, groups[NEAR])
    store_fold(far, 0, groups[FAR])
    store_fold(link_b, 0, tile_groups(info, tile, shared_rows(info, LINK, side // 3))[FAR])


def prepare_body(info, tile, chip, own_left, own_right, chip_left):
    side = tile.shape[0]
    for part, value in enumerate(tile_groups(info, tile, pl.ds(0, side))):
        store_left(own_left, (part,), value)
        store_right(own_right, (part,), value)
        store_left(chip_left, (part,), unfold(chip[part * side : (part + 1) * side, :]))


def near_start_body(info, mid, own_left, own_right, chip_left, out, rights):
    group = mid.shape[0] * 2 // 9
    store_right(rights, (), unfold(mid[...]))
    for who, lefts in ((OWN, own_left), (CHIP, chip_left)):
        value = passes(
            [left(lefts, NEAR), left(lefts, MID)], [right(rights, info, who), right(own_right, info, who, NEAR)]
        )
        if who == OWN:
            out[...] = value
        else:
            out[shared_rows(info, who, group), :] += value


def near_body(info, kept, link_a, begun, own_right, right_near, out, link, link_left):
    group = link_a.shape[0] // 6
    for part, base in ((MID, 0), (NEAR, 3 * group)):
        store_left(link_left, (part,), unfold(link_a[base : base + 3 * group, :]))
    out[...] = begun[...]
    out[shared_rows(info, LINK, group), :] += passes(
        [left(link_left, NEAR), left(link_left, MID)],
        [right(right_near, info, LINK), right(own_right, info, LINK, NEAR)],
    )
    out[...] = masked(out[...], kept, mask_at(info, NEAR))
    store_fold(link, 0, out[shared_rows(info, LINK, group), :])


def middle_products_body(info, own_left, own_right, chip_left, link_left, far, mid):
    group = far.shape[0] // 3
    for out, part in ((far, FAR), (mid, MID)):
        for who, lefts in ((OWN, own_left), (CHIP, chip_left), (LINK, link_left)):
            value = passes([left(lefts, MID)], [right(own_right, info, who, part)])
            if who == OWN:
                out[...] = value
            else:
                out[shared_rows(info, who, group), :] += value


def far_body(info, kept, link_b, mid, begun, s_near, own_left, chip_left, out, link, sides, link_left, rights):
    group = out.shape[0] // 3
    store_left(link_left, (), unfold(link_b[...]))
    store_right(rights, (), unfold(mid[...]))
    out[...] = begun[...] + passes([left(own_left, FAR)], [right(rights, info, OWN)])
    for who, factor in ((CHIP, left(chip_left, FAR)), (LINK, left(link_left))):
        out[shared_rows(info, who, group), :] += passes([factor], [right(rights, info, who)])
    out[...] = masked(out[...], kept, mask_at(info, FAR))
    store_fold(link, 0, out[shared_rows(info, LINK, group), :])
    store_fold(sides, 0, s_near[shared_rows(info, CHIP, group), :])
    store_fold(sides, 3 * group, out[shared_rows(info, CHIP, group), :])


def mid_start_body(info, near, begun, own_left, chip_left, link_left, out, rights):
    group = out.shape[0] // 3
    store_right(rights, (), unfold(near[...]))
    out[...] = begun[...] + passes([left(own_left, NEAR)], [right(rights, info, OWN)])
    for who, lefts in ((CHIP, chip_left), (LINK, link_left)):
        out[shared_rows(info, who, group), :] += passes([left(lefts, NEAR)], [right(rights, info, who)])


def mid_body(info, kept, far, own_left, chip_left, link_left, begun, out, chip, link, rights):
    group = out.shape[0] // 3
    store_right(rights, (), unfold(far[...]))
    out[...] = begun[...] + passes([left(own_left, FAR)], [right(rights, info, OWN)])
    for who, factor in ((CHIP, left(chip_left, FAR)), (LINK, left(link_left))):
        out[shared_rows(info, who, group), :] += passes([factor], [right(rights, info, who)])
    out[...] = masked(out[...], kept, 3)
    store_fold(link, 0, out[shared_rows(info, LINK, group), :])
    store_fold(chip, 0, out[shared_rows(info, CHIP, group), :])


def cube_near_body(info, link, near, far, right_near, right_far, right_mid, out):
    group = near.shape[0] // 3
    own, other = split(near[...]), split(unfold(link[...]))
    out[FAR] = passes([split(far[...])], [right(right_far, info, OWN)])
    for part, ref in ((NEAR, right_near), (MID, right_mid)):
        out[part] = passes([own], [right(ref, info, OWN)])
        out[part, shared_rows(info, LINK, group), :] += passes([other], [right(ref, info, LINK)])


def cube_own_body(info, link, total, near, mid, far, own_right, right_far, mid_far, out):
    group = near.shape[0] // 3
    own_mid, own_far = split(mid[...]), split(far[...])
    link_far = split(unfold(link[...]))
    rights = [right(own_right, info, OWN, part) for part in range(3)]
    out[NEAR] = 3.0 * near[...] - 2.0 * (total[NEAR] + passes([own_mid], rights[NEAR:MID]))
    out[MID] = 3.0 * mid[...] - 2.0 * (total[MID] + passes([own_mid, own_far], [rights[MID], right(mid_far, info, OWN)]))
    out[FAR] = 3.0 * far[...] - 2.0 * (total[FAR] + passes([own_mid], rights[FAR:]))
    for part, ref in ((MID, mid_far), (FAR, right_far)):
        out[part, shared_rows(info, LINK, group), :] -= 2.0 * passes([link_far], [right(ref, info, LINK)])


def send_rows(info, tile, out, sem, row, near, mid, far):
    odd = info[0] == 1
    group = near.shape[0]
    tile[:, :group] = jnp.where(odd, near, far)[:, :group]
    tile[:, group : 2 * group] = mid[:, :group]
    tile[:, 2 * group :] = jnp.where(odd, far, near)[:, :group]
    copy = pltpu.make_async_copy(tile, out.at[pl.ds(row, group), :], sem)
    copy.start()
    return copy


def cube_chip_body(info, kept, sides, chip, own_right, right_near, right_far, mid_near, mid_far, base, out, result, tile, sem):
    group = base.shape[1] // 3
    chip_start = place(info, CHIP, group)[0]
    rest = pl.multiple_of(2 * chip_start, 64)
    link_only = pl.multiple_of(2 * (group - chip_start), 64)
    chips = [split(unfold(value)) for value in (sides[: 3 * group, :], chip[...], sides[3 * group :, :])]
    own = [right(own_right, info, CHIP, part) for part in range(3)]
    products = (
        (chips[:2], [right(right_near, info, CHIP), own[NEAR]]),
        (chips, [right(mid_near, info, CHIP), own[MID], right(mid_far, info, CHIP)]),
        (chips[1:], [own[FAR], right(right_far, info, CHIP)]),
    )
    for part, factors in enumerate(products):
        out[part, shared_rows(info, CHIP, group), :] = base[part, shared_rows(info, CHIP, group), :] - 2.0 * passes(*factors)

    def finished(row):
        at = pl.ds(row, group)
        return [masked(out[part, at, :], kept, mask_at(info, part), row // 64) for part in range(3)]

    copy = send_rows(info, tile, result, sem, rest, *finished(rest))
    for part in range(3):
        out[part, pl.ds(link_only, group), :] = base[part, pl.ds(link_only, group), :]
    for row in (group, link_only):
        for part, value in enumerate(finished(row)):
            out[part, pl.ds(row, group), :] = value
    copy.wait()


def finish_body(info, kept, link, own_right, base, begun, result, tile, sem):
    del begun
    group = tile.shape[1]
    start, first_row = place(info, LINK, group)[0], place(info, LINK, 3)[0]
    link_mid = unfold(link[...])
    copies = []
    for half in range(2):
        factor = split(link_mid[half * group : (half + 1) * group])
        row = pl.multiple_of(start + half * group, 64)
        values = []
        for part in range(3):
            value = -2.0 * passes([factor], [right(own_right, info, LINK, part)])
            value = masked(value, kept, mask_at(info, part), first_row + 3 * half)
            values.append(base[part, pl.ds(row, group), :] + value)
        copies.append(send_rows(info, tile.at[half], result, sem.at[half], row, *values))
    for copy in copies:
        copy.wait()


VMEM = pl.BlockSpec(memory_space=pltpu.VMEM)
SMEM = pl.BlockSpec(memory_space=pltpu.SMEM)
ANY = pl.BlockSpec(memory_space=pl.ANY)
HBM = pl.BlockSpec(memory_space=pltpu.HBM)


def call(body, name, scalars, arrays, outs, work=4, result=False, begun=(), unmoved=(), scratch=()):
    count = len(scalars) + len(arrays)
    return pl.pallas_call(
        body,
        out_shape=[jax.ShapeDtypeStruct(shape, kind) for shape, kind in outs],
        in_specs=[SMEM] * len(scalars) + [VMEM] * len(arrays) + [ANY] * len(begun) + [HBM] * len(unmoved),
        out_specs=[VMEM] * (len(outs) - result) + [ANY] * result,
        scratch_shapes=scratch,
        input_output_aliases={count: len(outs) - 1} if begun else {},
        compiler_params=pltpu.CompilerParams(vmem_limit_bytes=24 << 20),
        cost_estimate=pl.CostEstimate(flops=work * 1000000000, transcendentals=0, bytes_accessed=work * 5000000),
        name=name,
    )(*scalars, *arrays, *begun, *unmoved)


def on_device(p_tiles, square_kept, result_kept):
    side = p_tiles.shape[0]
    group = side // 3
    n_row, n_col = lax.axis_size("row"), lax.axis_size("col")
    info = jnp.stack([lax.axis_index("row") % 2, lax.axis_index("col") % 2]).astype(jnp.int32)
    strip = ((3 * side // 2, LANES), F32)
    slab = ((3 * group, LANES), F32)
    two_slabs = ((6 * group, LANES), F32)
    three_slabs = ((9 * group, LANES), F32)
    wide = ((side, WIDE), F32)
    three_wide = ((3, side, WIDE), F32)
    rights = ((2, 3 * WIDE, WIDE), BF16)

    def exchange(value, axis, even_step):
        size = n_row if axis == "row" else n_col
        return lax.ppermute(
            value, axis, [(i, (i + (even_step if i % 2 == 0 else -even_step)) % size) for i in range(size)]
        )

    mid, link_a, chip = call(
        pack_first_body,
        "pack_first",
        (info,),
        (),
        [strip, two_slabs, three_slabs],
        unmoved=(pltpu.with_memory_space_constraint(p_tiles, pltpu.HBM),),
        scratch=[pltpu.VMEM((side, side), F32), pltpu.SemaphoreType.DMA((3,))],
    )
    link_a = exchange(link_a, "col", -1)
    partner_mid = exchange(mid, "row", 1)
    chip = exchange(chip, "col", 1)
    chip, tile = lax.optimization_barrier((chip, p_tiles))
    link_b, near, far = call(pack_rest_body, "pack_rest", (info,), (tile,), [slab, strip, strip])
    partner_near = exchange(near, "row", 1)
    link_b = exchange(link_b, "col", -1)
    passed_far = exchange(far, "row", -2)

    own_left, own_right, chip_left = call(
        prepare_body,
        "prepare",
        (info,),
        (p_tiles, chip),
        [((2, 3, side, WIDE), BF16), ((2, 3, 3 * WIDE, WIDE), BF16), ((2, 3, 2 * group, WIDE), BF16)],
    )
    partner_mid, own_left = lax.optimization_barrier((partner_mid, own_left))
    other_mid = exchange(partner_mid, "row", 2)
    begun, right_near = call(
        near_start_body, "near_start", (info,), (partner_mid, own_left, own_right, chip_left), [wide, rights]
    )
    s_near, near_link, link_left = call(
        near_body,
        "square_near",
        (info, square_kept),
        (link_a, begun, own_right, right_near),
        [wide, slab, ((2, 2, 2 * group, WIDE), BF16)],
    )
    near_link = exchange(near_link, "col", -1)
    passed_far, link_left = lax.optimization_barrier((passed_far, link_left))
    other_far = exchange(passed_far, "row", 1)
    begun, begun_mid = call(
        middle_products_body, "middle_products", (info,), (own_left, own_right, chip_left, link_left), [wide] * 2
    )
    begun_mid, mid_near = call(
        mid_start_body,
        "mid_start",
        (info,),
        (partner_near, begun_mid, own_left, chip_left, link_left),
        [wide, rights],
    )
    begun, begun_mid = lax.optimization_barrier((begun, begun_mid))
    s_far, far_link, sides_chip, link_left_far, right_far = call(
        far_body,
        "square_far",
        (info, square_kept),
        (link_b, other_mid, begun, s_near, own_left, chip_left),
        [wide, slab, two_slabs, ((2, 2 * group, WIDE), BF16), rights],
    )
    far_link = exchange(far_link, "col", -1)
    sides_chip = exchange(sides_chip, "col", 1)
    (total,) = call(
        cube_near_body,
        "cube_near",
        (info,),
        (near_link, s_near, s_far, right_near, right_far, mid_near),
        [three_wide],
    )
    total, other_far = lax.optimization_barrier((total, other_far))
    s_mid, mid_chip, mid_link, mid_far = call(
        mid_body,
        "square_mid",
        (info, square_kept),
        (other_far, own_left, chip_left, link_left_far, begun_mid),
        [wide, slab, slab, rights],
        work=0,
    )
    mid_link = exchange(mid_link, "col", -1)
    mid_chip = exchange(mid_chip, "col", 1)
    (base,) = call(
        cube_own_body,
        "cube_own",
        (info,),
        (far_link, total, s_near, s_mid, s_far, own_right, right_far, mid_far),
        [three_wide],
    )
    result = ((side, side), F32)
    base, purified = call(
        cube_chip_body,
        "cube_chip",
        (info, result_kept),
        (sides_chip, mid_chip, own_right, right_near, right_far, mid_near, mid_far, base),
        [three_wide, result],
        result=True,
        scratch=[pltpu.VMEM((group, side), F32), pltpu.SemaphoreType.DMA(())],
    )
    (purified,) = call(
        finish_body,
        "finish",
        (info, result_kept),
        (mid_link, own_right, base),
        [result],
        result=True,
        begun=(purified,),
        scratch=[pltpu.VMEM((2, group, side), F32), pltpu.SemaphoreType.DMA((2,))],
    )
    return purified


def solution(mesh):
    return jax.shard_map(
        on_device,
        mesh=mesh,
        in_specs=(P("row", "col"), P("row", "col"), P("row", "col")),
        out_specs=P("row", "col"),
        check_vma=False,
    )
```

```python
import jax
import jax.numpy as jnp
from jax import lax
from jax.experimental import pallas as pl
from jax.experimental.pallas import tpu as pltpu
from jax.sharding import PartitionSpec as P

LANES = 128
WIDE = 256
F32 = jnp.float32
BF16 = jnp.bfloat16
NEAR, MID, FAR = range(3)
OWN, CHIP, LINK = range(3)


def place(info, who, group):
    above = (info[1] == 1) == (who == CHIP)
    return jnp.where(above, 0, group), jnp.where(above, 0, 2)


def shared_rows(info, who, group):
    return pl.ds(pl.multiple_of(place(info, who, group)[0], 64), 2 * group)


def low_half(rows):
    return lax.broadcasted_iota(jnp.int32, (rows, LANES), 1) < LANES // 2


def store_fold(out_ref, base, value):
    rows = value.shape[0]
    half = rows // 2
    tail = value[:, LANES:]
    out_ref[pl.ds(base, rows), :] = value[:, :LANES]
    out_ref[pl.ds(base + rows, half), :] = jnp.where(
        low_half(half), tail[:half], pltpu.roll(tail[half:], LANES // 2, 1)
    )


def unfold(packed):
    rows = packed.shape[0] * 2 // 3
    half = rows // 2
    tail = packed[rows:]
    keep = low_half(half)
    upper = jnp.where(keep, tail, 0.0)
    lower = jnp.where(keep, pltpu.roll(tail, LANES // 2, 1), 0.0)
    return jnp.concatenate([packed[:rows], jnp.concatenate([upper, lower], 0)], 1)


def tile_groups(info, tile_ref, at):
    keep = low_half(at.size)
    first = jnp.concatenate([tile_ref[at, 0:128], jnp.where(keep, tile_ref[at, 128:256], 0.0)], 1)
    one = pltpu.roll(tile_ref[at, 128:256], LANES // 2, 1)
    two = pltpu.roll(tile_ref[at, 256:384], LANES // 2, 1)
    middle = jnp.concatenate([jnp.where(keep, one, two), jnp.where(keep, two, 0.0)], 1)
    end = tile_ref[at, 512:576]
    last = jnp.concatenate([tile_ref[at, 384:512], jnp.concatenate([end, jnp.zeros_like(end)], 1)], 1)
    odd = info[0] == 1
    return jnp.where(odd, first, last), middle, jnp.where(odd, last, first)


def split(value):
    high = value.astype(BF16)
    return high, (value - high.astype(F32)).astype(BF16)


def store_left(out_ref, at, value):
    out_ref[(0,) + at], out_ref[(1,) + at] = split(value)


def store_right(out_ref, at, value):
    group = value.shape[0] // 3
    for half, part in enumerate(split(value)):
        for ky in range(3):
            out_ref[(half,) + at + (pl.ds(ky * WIDE, group),)] = part[ky * group : (ky + 1) * group]
            out_ref[(half,) + at + (pl.ds(ky * WIDE + group, WIDE - group),)] = jnp.zeros((WIDE - group, WIDE), BF16)


def left(ref, *at):
    return ref[(0,) + at], ref[(1,) + at]


def right(ref, info, who, *at):
    start = WIDE if who == OWN else pl.multiple_of(place(info, who, 0)[1] * WIDE, WIDE)
    rows = (pl.ds(start, WIDE),)
    return ref[(0,) + at + rows], ref[(1,) + at + rows]


def passes(lefts, rights):
    wide = [high for high, _ in lefts] + [low for _, low in lefts] + [high for high, _ in lefts]
    tall = [high for high, _ in rights] + [high for high, _ in rights] + [low for _, low in rights]
    return jnp.dot(jnp.concatenate(wide, 1), jnp.concatenate(tall, 0), preferred_element_type=F32)


def mask_at(info, part):
    return 3 if part == MID else jnp.where((info[0] == 1) == (part == NEAR), 0, 6)


def masked(value, kept_ref, start, first_row=0):
    lane = lax.broadcasted_iota(jnp.int32, (8, WIDE), 1)

    def flags(i):
        one, two, three = (kept_ref[first_row + i, start + j] for j in range(3))
        return jnp.where(lane < 64, one, jnp.where(lane < 128, two, three)).astype(F32)[:1]

    return jnp.concatenate([value[i * 64 : (i + 1) * 64] * flags(i) for i in range(value.shape[0] // 64)], 0)


def pack_first_body(info, source, mid, link_a, chip, tile, sems):
    side = tile.shape[0]
    group = side // 3
    copies = [
        pltpu.make_async_copy(source.at[pl.ds(i * group, group), :], tile.at[pl.ds(i * group, group), :], sems.at[i])
        for i in range(3)
    ]
    for copy in copies:
        copy.start()
    slabs = (
        (CHIP, ((chip, 0, NEAR), (chip, 3 * group, MID), (chip, 6 * group, FAR))),
        (LINK, ((link_a, 0, MID), (link_a, 3 * group, NEAR))),
    )
    tails = []
    for i, copy in enumerate(copies):
        copy.wait()
        parts = tile_groups(info, tile, pl.ds(i * group, group))
        mid[pl.ds(i * group, group), :] = parts[MID][:, :LANES]
        tails.append(parts[MID][:, LANES:])
        for who, targets in slabs:
            first = place(info, who, 1)[0]
            for half in range(2):
                if 0 <= i - half <= 1:

                    @pl.when(first == i - half)
                    def _(targets=targets, half=half, parts=parts):
                        for ref, base, part in targets:
                            ref[pl.ds(base + half * group, group), :] = parts[part][:, :LANES]
                            tail = parts[part][:, LANES:]
                            if half == 0:
                                ref[pl.ds(base + 2 * group, group), : LANES // 2] = tail[:, : LANES // 2]
                            else:
                                turned = pltpu.roll(tail, LANES // 2, 1)
                                ref[pl.ds(base + 2 * group, group), LANES // 2 :] = turned[:, LANES // 2 :]

    tail = jnp.concatenate(tails, 0)
    middle = side // 2
    mid[pl.ds(side, middle), :] = jnp.where(
        low_half(middle), tail[:middle], pltpu.roll(tail[middle:], LANES // 2, 1)
    )


def pack_rest_body(info, tile, link_b, near, far):
    side = tile.shape[0]
    groups = tile_groups(info, tile, pl.ds(0, side))
    store_fold(near, 0, groups[NEAR])
    store_fold(far, 0, groups[FAR])
    store_fold(link_b, 0, tile_groups(info, tile, shared_rows(info, LINK, side // 3))[FAR])


def prepare_body(info, tile, chip, own_left, own_right, chip_left):
    side = tile.shape[0]
    for part, value in enumerate(tile_groups(info, tile, pl.ds(0, side))):
        store_left(own_left, (part,), value)
        store_right(own_right, (part,), value)
        store_left(chip_left, (part,), unfold(chip[part * side : (part + 1) * side, :]))


def near_start_body(info, mid, own_left, own_right, chip_left, out, rights):
    group = mid.shape[0] * 2 // 9
    store_right(rights, (), unfold(mid[...]))
    for who, lefts in ((OWN, own_left), (CHIP, chip_left)):
        value = passes(
            [left(lefts, NEAR), left(lefts, MID)], [right(rights, info, who), right(own_right, info, who, NEAR)]
        )
        if who == OWN:
            out[...] = value
        else:
            out[shared_rows(info, who, group), :] += value


def near_body(info, kept, link_a, begun, own_right, right_near, out, link, link_left):
    group = link_a.shape[0] // 6
    for part, base in ((MID, 0), (NEAR, 3 * group)):
        store_left(link_left, (part,), unfold(link_a[base : base + 3 * group, :]))
    out[...] = begun[...]
    out[shared_rows(info, LINK, group), :] += passes(
        [left(link_left, NEAR), left(link_left, MID)],
        [right(right_near, info, LINK), right(own_right, info, LINK, NEAR)],
    )
    out[...] = masked(out[...], kept, mask_at(info, NEAR))
    store_fold(link, 0, out[shared_rows(info, LINK, group), :])


def middle_products_body(info, own_left, own_right, chip_left, link_left, far, mid):
    group = far.shape[0] // 3
    for out, part in ((far, FAR), (mid, MID)):
        for who, lefts in ((OWN, own_left), (CHIP, chip_left), (LINK, link_left)):
            value = passes([left(lefts, MID)], [right(own_right, info, who, part)])
            if who == OWN:
                out[...] = value
            else:
                out[shared_rows(info, who, group), :] += value


def far_body(info, kept, link_b, mid, begun, s_near, own_left, chip_left, out, link, sides, link_left, rights):
    group = out.shape[0] // 3
    store_left(link_left, (), unfold(link_b[...]))
    store_right(rights, (), unfold(mid[...]))
    out[...] = begun[...] + passes([left(own_left, FAR)], [right(rights, info, OWN)])
    for who, factor in ((CHIP, left(chip_left, FAR)), (LINK, left(link_left))):
        out[shared_rows(info, who, group), :] += passes([factor], [right(rights, info, who)])
    out[...] = masked(out[...], kept, mask_at(info, FAR))
    store_fold(link, 0, out[shared_rows(info, LINK, group), :])
    store_fold(sides, 0, s_near[shared_rows(info, CHIP, group), :])
    store_fold(sides, 3 * group, out[shared_rows(info, CHIP, group), :])


def mid_start_body(info, near, begun, own_left, chip_left, link_left, out, rights):
    group = out.shape[0] // 3
    store_right(rights, (), unfold(near[...]))
    out[...] = begun[...] + passes([left(own_left, NEAR)], [right(rights, info, OWN)])
    for who, lefts in ((CHIP, chip_left), (LINK, link_left)):
        out[shared_rows(info, who, group), :] += passes([left(lefts, NEAR)], [right(rights, info, who)])


def mid_body(info, kept, far, own_left, chip_left, link_left, begun, out, chip, link, rights):
    group = out.shape[0] // 3
    store_right(rights, (), unfold(far[...]))
    out[...] = begun[...] + passes([left(own_left, FAR)], [right(rights, info, OWN)])
    for who, factor in ((CHIP, left(chip_left, FAR)), (LINK, left(link_left))):
        out[shared_rows(info, who, group), :] += passes([factor], [right(rights, info, who)])
    out[...] = masked(out[...], kept, 3)
    store_fold(link, 0, out[shared_rows(info, LINK, group), :])
    store_fold(chip, 0, out[shared_rows(info, CHIP, group), :])


def cube_near_body(info, link, near, far, right_near, right_far, right_mid, out):
    group = near.shape[0] // 3
    own, other = split(near[...]), split(unfold(link[...]))
    out[FAR] = passes([split(far[...])], [right(right_far, info, OWN)])
    for part, ref in ((NEAR, right_near), (MID, right_mid)):
        out[part] = passes([own], [right(ref, info, OWN)])
        out[part, shared_rows(info, LINK, group), :] += passes([other], [right(ref, info, LINK)])


def cube_own_body(info, link, total, near, mid, far, own_right, right_far, mid_far, out):
    group = near.shape[0] // 3
    own_mid, own_far = split(mid[...]), split(far[...])
    link_far = split(unfold(link[...]))
    rights = [right(own_right, info, OWN, part) for part in range(3)]
    out[NEAR] = 3.0 * near[...] - 2.0 * (total[NEAR] + passes([own_mid], rights[NEAR:MID]))
    out[MID] = 3.0 * mid[...] - 2.0 * (total[MID] + passes([own_mid, own_far], [rights[MID], right(mid_far, info, OWN)]))
    out[FAR] = 3.0 * far[...] - 2.0 * (total[FAR] + passes([own_mid], rights[FAR:]))
    for part, ref in ((MID, mid_far), (FAR, right_far)):
        out[part, shared_rows(info, LINK, group), :] -= 2.0 * passes([link_far], [right(ref, info, LINK)])


def send_rows(info, tile, out, sem, row, near, mid, far):
    odd = info[0] == 1
    group = near.shape[0]
    tile[:, :group] = jnp.where(odd, near, far)[:, :group]
    tile[:, group : 2 * group] = mid[:, :group]
    tile[:, 2 * group :] = jnp.where(odd, far, near)[:, :group]
    copy = pltpu.make_async_copy(tile, out.at[pl.ds(row, group), :], sem)
    copy.start()
    return copy


def cube_chip_body(info, kept, sides, chip, own_right, right_near, right_far, mid_near, mid_far, base, out, result, tile, sem):
    group = base.shape[1] // 3
    chip_start = place(info, CHIP, group)[0]
    rest = pl.multiple_of(2 * chip_start, 64)
    link_only = pl.multiple_of(2 * (group - chip_start), 64)
    chips = [split(unfold(value)) for value in (sides[: 3 * group, :], chip[...], sides[3 * group :, :])]
    own = [right(own_right, info, CHIP, part) for part in range(3)]
    products = (
        (chips[:2], [right(right_near, info, CHIP), own[NEAR]]),
        (chips, [right(mid_near, info, CHIP), own[MID], right(mid_far, info, CHIP)]),
        (chips[1:], [own[FAR], right(right_far, info, CHIP)]),
    )
    for part, factors in enumerate(products):
        out[part, shared_rows(info, CHIP, group), :] = base[part, shared_rows(info, CHIP, group), :] - 2.0 * passes(*factors)

    def finished(row):
        at = pl.ds(row, group)
        return [masked(out[part, at, :], kept, mask_at(info, part), row // 64) for part in range(3)]

    copy = send_rows(info, tile, result, sem, rest, *finished(rest))
    for part in range(3):
        out[part, pl.ds(link_only, group), :] = base[part, pl.ds(link_only, group), :]
    for row in (group, link_only):
        for part, value in enumerate(finished(row)):
            out[part, pl.ds(row, group), :] = value
    copy.wait()


def finish_body(info, kept, link, own_right, base, begun, result, tile, sem):
    del begun
    group = tile.shape[1]
    start, first_row = place(info, LINK, group)[0], place(info, LINK, 3)[0]
    link_mid = unfold(link[...])
    copies = []
    for half in range(2):
        factor = split(link_mid[half * group : (half + 1) * group])
        row = pl.multiple_of(start + half * group, 64)
        values = []
        for part in range(3):
            value = -2.0 * passes([factor], [right(own_right, info, LINK, part)])
            value = masked(value, kept, mask_at(info, part), first_row + 3 * half)
            values.append(base[part, pl.ds(row, group), :] + value)
        copies.append(send_rows(info, tile.at[half], result, sem.at[half], row, *values))
    for copy in copies:
        copy.wait()


VMEM = pl.BlockSpec(memory_space=pltpu.VMEM)
SMEM = pl.BlockSpec(memory_space=pltpu.SMEM)
ANY = pl.BlockSpec(memory_space=pl.ANY)
HBM = pl.BlockSpec(memory_space=pltpu.HBM)


def call(body, name, scalars, arrays, outs, work=4, result=False, begun=(), unmoved=(), scratch=()):
    count = len(scalars) + len(arrays)
    return pl.pallas_call(
        body,
        out_shape=[jax.ShapeDtypeStruct(shape, kind) for shape, kind in outs],
        in_specs=[SMEM] * len(scalars) + [VMEM] * len(arrays) + [ANY] * len(begun) + [HBM] * len(unmoved),
        out_specs=[VMEM] * (len(outs) - result) + [ANY] * result,
        scratch_shapes=scratch,
        input_output_aliases={count: len(outs) - 1} if begun else {},
        compiler_params=pltpu.CompilerParams(vmem_limit_bytes=24 << 20),
        cost_estimate=pl.CostEstimate(flops=work * 1000000000, transcendentals=0, bytes_accessed=work * 5000000),
        name=name,
    )(*scalars, *arrays, *begun, *unmoved)


def on_device(p_tiles, square_kept, result_kept):
    side = p_tiles.shape[0]
    group = side // 3
    n_row, n_col = lax.axis_size("row"), lax.axis_size("col")
    info = jnp.stack([lax.axis_index("row") % 2, lax.axis_index("col") % 2]).astype(jnp.int32)
    strip = ((3 * side // 2, LANES), F32)
    slab = ((3 * group, LANES), F32)
    two_slabs = ((6 * group, LANES), F32)
    three_slabs = ((9 * group, LANES), F32)
    wide = ((side, WIDE), F32)
    three_wide = ((3, side, WIDE), F32)
    rights = ((2, 3 * WIDE, WIDE), BF16)

    def exchange(value, axis, even_step):
        size = n_row if axis == "row" else n_col
        return lax.ppermute(
            value, axis, [(i, (i + (even_step if i % 2 == 0 else -even_step)) % size) for i in range(size)]
        )

    mid, link_a, chip = call(
        pack_first_body,
        "pack_first",
        (info,),
        (),
        [strip, two_slabs, three_slabs],
        unmoved=(pltpu.with_memory_space_constraint(p_tiles, pltpu.HBM),),
        scratch=[pltpu.VMEM((side, side), F32), pltpu.SemaphoreType.DMA((3,))],
    )
    link_a = exchange(link_a, "col", -1)
    partner_mid = exchange(mid, "row", 1)
    chip = exchange(chip, "col", 1)
    chip, tile = lax.optimization_barrier((chip, p_tiles))
    link_b, near, far = call(pack_rest_body, "pack_rest", (info,), (tile,), [slab, strip, strip])
    partner_near = exchange(near, "row", 1)
    link_b = exchange(link_b, "col", -1)
    passed_far = exchange(far, "row", -2)

    own_left, own_right, chip_left = call(
        prepare_body,
        "prepare",
        (info,),
        (p_tiles, chip),
        [((2, 3, side, WIDE), BF16), ((2, 3, 3 * WIDE, WIDE), BF16), ((2, 3, 2 * group, WIDE), BF16)],
    )
    partner_mid, own_left = lax.optimization_barrier((partner_mid, own_left))
    other_mid = exchange(partner_mid, "row", 2)
    begun, right_near = call(
        near_start_body, "near_start", (info,), (partner_mid, own_left, own_right, chip_left), [wide, rights]
    )
    s_near, near_link, link_left = call(
        near_body,
        "square_near",
        (info, square_kept),
        (link_a, begun, own_right, right_near),
        [wide, slab, ((2, 2, 2 * group, WIDE), BF16)],
    )
    near_link = exchange(near_link, "col", -1)
    passed_far, link_left = lax.optimization_barrier((passed_far, link_left))
    other_far = exchange(passed_far, "row", 1)
    begun, begun_mid = call(
        middle_products_body, "middle_products", (info,), (own_left, own_right, chip_left, link_left), [wide] * 2
    )
    begun_mid, mid_near = call(
        mid_start_body,
        "mid_start",
        (info,),
        (partner_near, begun_mid, own_left, chip_left, link_left),
        [wide, rights],
    )
    begun, begun_mid = lax.optimization_barrier((begun, begun_mid))
    s_far, far_link, sides_chip, link_left_far, right_far = call(
        far_body,
        "square_far",
        (info, square_kept),
        (link_b, other_mid, begun, s_near, own_left, chip_left),
        [wide, slab, two_slabs, ((2, 2 * group, WIDE), BF16), rights],
    )
    far_link = exchange(far_link, "col", -1)
    sides_chip = exchange(sides_chip, "col", 1)
    (total,) = call(
        cube_near_body,
        "cube_near",
        (info,),
        (near_link, s_near, s_far, right_near, right_far, mid_near),
        [three_wide],
    )
    total, other_far = lax.optimization_barrier((total, other_far))
    s_mid, mid_chip, mid_link, mid_far = call(
        mid_body,
        "square_mid",
        (info, square_kept),
        (other_far, own_left, chip_left, link_left_far, begun_mid),
        [wide, slab, slab, rights],
        work=0,
    )
    mid_link = exchange(mid_link, "col", -1)
    mid_chip = exchange(mid_chip, "col", 1)
    (base,) = call(
        cube_own_body,
        "cube_own",
        (info,),
        (far_link, total, s_near, s_mid, s_far, own_right, right_far, mid_far),
        [three_wide],
    )
    result = ((side, side), F32)
    base, purified = call(
        cube_chip_body,
        "cube_chip",
        (info, result_kept),
        (sides_chip, mid_chip, own_right, right_near, right_far, mid_near, mid_far, base),
        [three_wide, result],
        result=True,
        scratch=[pltpu.VMEM((group, side), F32), pltpu.SemaphoreType.DMA(())],
    )
    (purified,) = call(
        finish_body,
        "finish",
        (info, result_kept),
        (mid_link, own_right, base),
        [result],
        result=True,
        begun=(purified,),
        scratch=[pltpu.VMEM((2, group, side), F32), pltpu.SemaphoreType.DMA((2,))],
    )
    return purified


def solution(mesh):
    return jax.shard_map(
        on_device,
        mesh=mesh,
        in_specs=(P("row", "col"), P("row", "col"), P("row", "col")),
        out_specs=P("row", "col"),
        check_vma=False,
    )
```

```python
import jax
import jax.numpy as jnp
from jax import lax
from jax.experimental import pallas as pl
from jax.experimental.pallas import tpu as pltpu
from jax.sharding import PartitionSpec as P

LANES = 128
WIDE = 256
F32 = jnp.float32
BF16 = jnp.bfloat16
NEAR, MID, FAR = range(3)
OWN, CHIP, LINK = range(3)


def place(info, who, group):
    above = (info[1] == 1) == (who == CHIP)
    return jnp.where(above, 0, group), jnp.where(above, 0, 2)


def shared_rows(info, who, group):
    return pl.ds(pl.multiple_of(place(info, who, group)[0], 64), 2 * group)


def low_half(rows):
    return lax.broadcasted_iota(jnp.int32, (rows, LANES), 1) < LANES // 2


def store_fold(out_ref, base, value):
    rows = value.shape[0]
    half = rows // 2
    tail = value[:, LANES:]
    out_ref[pl.ds(base, rows), :] = value[:, :LANES]
    out_ref[pl.ds(base + rows, half), :] = jnp.where(
        low_half(half), tail[:half], pltpu.roll(tail[half:], LANES // 2, 1)
    )


def unfold(packed):
    rows = packed.shape[0] * 2 // 3
    half = rows // 2
    tail = packed[rows:]
    keep = low_half(half)
    upper = jnp.where(keep, tail, 0.0)
    lower = jnp.where(keep, pltpu.roll(tail, LANES // 2, 1), 0.0)
    return jnp.concatenate([packed[:rows], jnp.concatenate([upper, lower], 0)], 1)


def tile_groups(info, tile_ref, at):
    keep = low_half(at.size)
    first = jnp.concatenate([tile_ref[at, 0:128], jnp.where(keep, tile_ref[at, 128:256], 0.0)], 1)
    one = pltpu.roll(tile_ref[at, 128:256], LANES // 2, 1)
    two = pltpu.roll(tile_ref[at, 256:384], LANES // 2, 1)
    middle = jnp.concatenate([jnp.where(keep, one, two), jnp.where(keep, two, 0.0)], 1)
    end = tile_ref[at, 512:576]
    last = jnp.concatenate([tile_ref[at, 384:512], jnp.concatenate([end, jnp.zeros_like(end)], 1)], 1)
    odd = info[0] == 1
    return jnp.where(odd, first, last), middle, jnp.where(odd, last, first)


def split(value):
    high = value.astype(BF16)
    return high, (value - high.astype(F32)).astype(BF16)


def store_left(out_ref, at, value):
    out_ref[(0,) + at], out_ref[(1,) + at] = split(value)


def store_right(out_ref, at, value):
    group = value.shape[0] // 3
    for half, part in enumerate(split(value)):
        for ky in range(3):
            out_ref[(half,) + at + (pl.ds(ky * WIDE, group),)] = part[ky * group : (ky + 1) * group]
            out_ref[(half,) + at + (pl.ds(ky * WIDE + group, WIDE - group),)] = jnp.zeros((WIDE - group, WIDE), BF16)


def left(ref, *at):
    return ref[(0,) + at], ref[(1,) + at]


def right(ref, info, who, *at):
    start = WIDE if who == OWN else pl.multiple_of(place(info, who, 0)[1] * WIDE, WIDE)
    rows = (pl.ds(start, WIDE),)
    return ref[(0,) + at + rows], ref[(1,) + at + rows]


def passes(lefts, rights):
    wide = [high for high, _ in lefts] + [low for _, low in lefts] + [high for high, _ in lefts]
    tall = [high for high, _ in rights] + [high for high, _ in rights] + [low for _, low in rights]
    return jnp.dot(jnp.concatenate(wide, 1), jnp.concatenate(tall, 0), preferred_element_type=F32)


def mask_at(info, part):
    return 3 if part == MID else jnp.where((info[0] == 1) == (part == NEAR), 0, 6)


def masked(value, kept_ref, start, first_row=0):
    lane = lax.broadcasted_iota(jnp.int32, (8, WIDE), 1)

    def flags(i):
        one, two, three = (kept_ref[first_row + i, start + j] for j in range(3))
        return jnp.where(lane < 64, one, jnp.where(lane < 128, two, three)).astype(F32)[:1]

    return jnp.concatenate([value[i * 64 : (i + 1) * 64] * flags(i) for i in range(value.shape[0] // 64)], 0)


def pack_first_body(info, source, mid, link_a, chip, tile, sems):
    side = tile.shape[0]
    group = side // 3
    copies = [
        pltpu.make_async_copy(source.at[pl.ds(i * group, group), :], tile.at[pl.ds(i * group, group), :], sems.at[i])
        for i in range(3)
    ]
    for copy in copies:
        copy.start()
    slabs = (
        (CHIP, ((chip, 0, NEAR), (chip, 3 * group, MID), (chip, 6 * group, FAR))),
        (LINK, ((link_a, 0, MID), (link_a, 3 * group, NEAR))),
    )
    tails = []
    for i, copy in enumerate(copies):
        copy.wait()
        parts = tile_groups(info, tile, pl.ds(i * group, group))
        mid[pl.ds(i * group, group), :] = parts[MID][:, :LANES]
        tails.append(parts[MID][:, LANES:])
        for who, targets in slabs:
            first = place(info, who, 1)[0]
            for half in range(2):
                if 0 <= i - half <= 1:

                    @pl.when(first == i - half)
                    def _(targets=targets, half=half, parts=parts):
                        for ref, base, part in targets:
                            ref[pl.ds(base + half * group, group), :] = parts[part][:, :LANES]
                            tail = parts[part][:, LANES:]
                            if half == 0:
                                ref[pl.ds(base + 2 * group, group), : LANES // 2] = tail[:, : LANES // 2]
                            else:
                                turned = pltpu.roll(tail, LANES // 2, 1)
                                ref[pl.ds(base + 2 * group, group), LANES // 2 :] = turned[:, LANES // 2 :]

    tail = jnp.concatenate(tails, 0)
    middle = side // 2
    mid[pl.ds(side, middle), :] = jnp.where(
        low_half(middle), tail[:middle], pltpu.roll(tail[middle:], LANES // 2, 1)
    )


def pack_rest_body(info, tile, link_b, near, far):
    side = tile.shape[0]
    groups = tile_groups(info, tile, pl.ds(0, side))
    store_fold(near, 0, groups[NEAR])
    store_fold(far, 0, groups[FAR])
    store_fold(link_b, 0, tile_groups(info, tile, shared_rows(info, LINK, side // 3))[FAR])


def prepare_body(info, tile, chip, own_left, own_right, chip_left):
    side = tile.shape[0]
    for part, value in enumerate(tile_groups(info, tile, pl.ds(0, side))):
        store_left(own_left, (part,), value)
        store_right(own_right, (part,), value)
        store_left(chip_left, (part,), unfold(chip[part * side : (part + 1) * side, :]))


def near_start_body(info, mid, own_left, own_right, chip_left, out, rights):
    group = mid.shape[0] * 2 // 9
    store_right(rights, (), unfold(mid[...]))
    for who, lefts in ((OWN, own_left), (CHIP, chip_left)):
        value = passes(
            [left(lefts, NEAR), left(lefts, MID)], [right(rights, info, who), right(own_right, info, who, NEAR)]
        )
        if who == OWN:
            out[...] = value
        else:
            out[shared_rows(info, who, group), :] += value


def near_body(info, kept, link_a, begun, own_right, right_near, out, link, link_left):
    group = link_a.shape[0] // 6
    for part, base in ((MID, 0), (NEAR, 3 * group)):
        store_left(link_left, (part,), unfold(link_a[base : base + 3 * group, :]))
    out[...] = begun[...]
    out[shared_rows(info, LINK, group), :] += passes(
        [left(link_left, NEAR), left(link_left, MID)],
        [right(right_near, info, LINK), right(own_right, info, LINK, NEAR)],
    )
    out[...] = masked(out[...], kept, mask_at(info, NEAR))
    store_fold(link, 0, out[shared_rows(info, LINK, group), :])


def middle_products_body(info, own_left, own_right, chip_left, link_left, far, mid):
    group = far.shape[0] // 3
    for out, part in ((far, FAR), (mid, MID)):
        for who, lefts in ((OWN, own_left), (CHIP, chip_left), (LINK, link_left)):
            value = passes([left(lefts, MID)], [right(own_right, info, who, part)])
            if who == OWN:
                out[...] = value
            else:
                out[shared_rows(info, who, group), :] += value


def far_body(info, kept, link_b, mid, begun, s_near, own_left, chip_left, out, link, sides, link_left, rights):
    group = out.shape[0] // 3
    store_left(link_left, (), unfold(link_b[...]))
    store_right(rights, (), unfold(mid[...]))
    out[...] = begun[...] + passes([left(own_left, FAR)], [right(rights, info, OWN)])
    for who, factor in ((CHIP, left(chip_left, FAR)), (LINK, left(link_left))):
        out[shared_rows(info, who, group), :] += passes([factor], [right(rights, info, who)])
    out[...] = masked(out[...], kept, mask_at(info, FAR))
    store_fold(link, 0, out[shared_rows(info, LINK, group), :])
    store_fold(sides, 0, s_near[shared_rows(info, CHIP, group), :])
    store_fold(sides, 3 * group, out[shared_rows(info, CHIP, group), :])


def mid_start_body(info, near, begun, own_left, chip_left, link_left, out, rights):
    group = out.shape[0] // 3
    store_right(rights, (), unfold(near[...]))
    out[...] = begun[...] + passes([left(own_left, NEAR)], [right(rights, info, OWN)])
    for who, lefts in ((CHIP, chip_left), (LINK, link_left)):
        out[shared_rows(info, who, group), :] += passes([left(lefts, NEAR)], [right(rights, info, who)])


def mid_body(info, kept, far, own_left, chip_left, link_left, begun, out, chip, link, rights):
    group = out.shape[0] // 3
    store_right(rights, (), unfold(far[...]))
    out[...] = begun[...] + passes([left(own_left, FAR)], [right(rights, info, OWN)])
    for who, factor in ((CHIP, left(chip_left, FAR)), (LINK, left(link_left))):
        out[shared_rows(info, who, group), :] += passes([factor], [right(rights, info, who)])
    out[...] = masked(out[...], kept, 3)
    store_fold(link, 0, out[shared_rows(info, LINK, group), :])
    store_fold(chip, 0, out[shared_rows(info, CHIP, group), :])


def cube_near_body(info, link, near, far, right_near, right_far, right_mid, out):
    group = near.shape[0] // 3
    own, other = split(near[...]), split(unfold(link[...]))
    out[FAR] = passes([split(far[...])], [right(right_far, info, OWN)])
    for part, ref in ((NEAR, right_near), (MID, right_mid)):
        out[part] = passes([own], [right(ref, info, OWN)])
        out[part, shared_rows(info, LINK, group), :] += passes([other], [right(ref, info, LINK)])


def cube_own_body(info, total, near, mid, far, own_right, mid_far, out):
    own_mid, own_far = split(mid[...]), split(far[...])
    rights = [right(own_right, info, OWN, part) for part in range(3)]
    out[NEAR] = 3.0 * near[...] - 2.0 * (total[NEAR] + passes([own_mid], rights[NEAR:MID]))
    out[MID] = 3.0 * mid[...] - 2.0 * (total[MID] + passes([own_mid, own_far], [rights[MID], right(mid_far, info, OWN)]))
    out[FAR] = 3.0 * far[...] - 2.0 * (total[FAR] + passes([own_mid], rights[FAR:]))


def send_rows(info, tile, out, sem, row, near, mid, far):
    odd = info[0] == 1
    group = near.shape[0]
    tile[:, :group] = jnp.where(odd, near, far)[:, :group]
    tile[:, group : 2 * group] = mid[:, :group]
    tile[:, 2 * group :] = jnp.where(odd, far, near)[:, :group]
    copy = pltpu.make_async_copy(tile, out.at[pl.ds(row, group), :], sem)
    copy.start()
    return copy


def cube_chip_body(info, kept, link, sides, chip, own_right, right_near, right_far, mid_near, mid_far, base, out, result, tile, sem):
    group = base.shape[1] // 3
    chip_start = place(info, CHIP, group)[0]
    rest = pl.multiple_of(2 * chip_start, 64)
    link_only = pl.multiple_of(2 * (group - chip_start), 64)
    chips = [split(unfold(value)) for value in (sides[: 3 * group, :], chip[...], sides[3 * group :, :])]
    own = [right(own_right, info, CHIP, part) for part in range(3)]
    products = (
        (chips[:2], [right(right_near, info, CHIP), own[NEAR]]),
        (chips, [right(mid_near, info, CHIP), own[MID], right(mid_far, info, CHIP)]),
        (chips[1:], [own[FAR], right(right_far, info, CHIP)]),
    )
    for part in range(3):
        out[part, pl.ds(link_only, group), :] = base[part, pl.ds(link_only, group), :]
    for part, factors in enumerate(products):
        out[part, shared_rows(info, CHIP, group), :] = base[part, shared_rows(info, CHIP, group), :] - 2.0 * passes(*factors)

    def finished(row):
        at = pl.ds(row, group)
        return [masked(out[part, at, :], kept, mask_at(info, part), row // 64) for part in range(3)]

    copy = send_rows(info, tile, result, sem, rest, *finished(rest))
    link_far = split(unfold(link[...]))
    for part, ref in ((MID, mid_far), (FAR, right_far)):
        out[part, shared_rows(info, LINK, group), :] -= 2.0 * passes([link_far], [right(ref, info, LINK)])
    for row in (group, link_only):
        for part, value in enumerate(finished(row)):
            out[part, pl.ds(row, group), :] = value
    copy.wait()


def finish_body(info, kept, link, own_right, base, begun, result, tile, sem):
    del begun
    group = tile.shape[1]
    start, first_row = place(info, LINK, group)[0], place(info, LINK, 3)[0]
    factor = split(unfold(link[...]))
    products = [-2.0 * passes([factor], [right(own_right, info, LINK, part)]) for part in range(3)]
    copies = []
    for half in range(2):
        row = pl.multiple_of(start + half * group, 64)
        values = []
        for part in range(3):
            value = products[part][half * group : (half + 1) * group]
            value = masked(value, kept, mask_at(info, part), first_row + 3 * half)
            values.append(base[part, pl.ds(row, group), :] + value)
        copies.append(send_rows(info, tile.at[half], result, sem.at[half], row, *values))
    for copy in copies:
        copy.wait()


VMEM = pl.BlockSpec(memory_space=pltpu.VMEM)
SMEM = pl.BlockSpec(memory_space=pltpu.SMEM)
ANY = pl.BlockSpec(memory_space=pl.ANY)
HBM = pl.BlockSpec(memory_space=pltpu.HBM)


def call(body, name, scalars, arrays, outs, work=4, result=False, begun=(), unmoved=(), scratch=()):
    count = len(scalars) + len(arrays)
    return pl.pallas_call(
        body,
        out_shape=[jax.ShapeDtypeStruct(shape, kind) for shape, kind in outs],
        in_specs=[SMEM] * len(scalars) + [VMEM] * len(arrays) + [ANY] * len(begun) + [HBM] * len(unmoved),
        out_specs=[VMEM] * (len(outs) - result) + [ANY] * result,
        scratch_shapes=scratch,
        input_output_aliases={count: len(outs) - 1} if begun else {},
        compiler_params=pltpu.CompilerParams(vmem_limit_bytes=24 << 20),
        cost_estimate=pl.CostEstimate(flops=work * 1000000000, transcendentals=0, bytes_accessed=work * 5000000),
        name=name,
    )(*scalars, *arrays, *begun, *unmoved)


def on_device(p_tiles, square_kept, result_kept):
    side = p_tiles.shape[0]
    group = side // 3
    n_row, n_col = lax.axis_size("row"), lax.axis_size("col")
    info = jnp.stack([lax.axis_index("row") % 2, lax.axis_index("col") % 2]).astype(jnp.int32)
    strip = ((3 * side // 2, LANES), F32)
    slab = ((3 * group, LANES), F32)
    two_slabs = ((6 * group, LANES), F32)
    three_slabs = ((9 * group, LANES), F32)
    wide = ((side, WIDE), F32)
    three_wide = ((3, side, WIDE), F32)
    rights = ((2, 3 * WIDE, WIDE), BF16)

    def exchange(value, axis, even_step):
        size = n_row if axis == "row" else n_col
        return lax.ppermute(
            value, axis, [(i, (i + (even_step if i % 2 == 0 else -even_step)) % size) for i in range(size)]
        )

    mid, link_a, chip = call(
        pack_first_body,
        "pack_first",
        (info,),
        (),
        [strip, two_slabs, three_slabs],
        unmoved=(pltpu.with_memory_space_constraint(p_tiles, pltpu.HBM),),
        scratch=[pltpu.VMEM((side, side), F32), pltpu.SemaphoreType.DMA((3,))],
    )
    link_a = exchange(link_a, "col", -1)
    partner_mid = exchange(mid, "row", 1)
    chip = exchange(chip, "col", 1)
    chip, tile = lax.optimization_barrier((chip, p_tiles))
    link_b, near, far = call(pack_rest_body, "pack_rest", (info,), (tile,), [slab, strip, strip])
    partner_near = exchange(near, "row", 1)
    link_b = exchange(link_b, "col", -1)
    passed_far = exchange(far, "row", -2)

    own_left, own_right, chip_left = call(
        prepare_body,
        "prepare",
        (info,),
        (p_tiles, chip),
        [((2, 3, side, WIDE), BF16), ((2, 3, 3 * WIDE, WIDE), BF16), ((2, 3, 2 * group, WIDE), BF16)],
    )
    partner_mid, own_left = lax.optimization_barrier((partner_mid, own_left))
    other_mid = exchange(partner_mid, "row", 2)
    begun, right_near = call(
        near_start_body, "near_start", (info,), (partner_mid, own_left, own_right, chip_left), [wide, rights]
    )
    s_near, near_link, link_left = call(
        near_body,
        "square_near",
        (info, square_kept),
        (link_a, begun, own_right, right_near),
        [wide, slab, ((2, 2, 2 * group, WIDE), BF16)],
    )
    near_link = exchange(near_link, "col", -1)
    passed_far, link_left = lax.optimization_barrier((passed_far, link_left))
    other_far = exchange(passed_far, "row", 1)
    begun, begun_mid = call(
        middle_products_body, "middle_products", (info,), (own_left, own_right, chip_left, link_left), [wide] * 2
    )
    begun_mid, mid_near = call(
        mid_start_body,
        "mid_start",
        (info,),
        (partner_near, begun_mid, own_left, chip_left, link_left),
        [wide, rights],
    )
    begun, begun_mid = lax.optimization_barrier((begun, begun_mid))
    s_far, far_link, sides_chip, link_left_far, right_far = call(
        far_body,
        "square_far",
        (info, square_kept),
        (link_b, other_mid, begun, s_near, own_left, chip_left),
        [wide, slab, two_slabs, ((2, 2 * group, WIDE), BF16), rights],
    )
    far_link = exchange(far_link, "col", -1)
    sides_chip = exchange(sides_chip, "col", 1)
    (total,) = call(
        cube_near_body,
        "cube_near",
        (info,),
        (near_link, s_near, s_far, right_near, right_far, mid_near),
        [three_wide],
    )
    total, other_far = lax.optimization_barrier((total, other_far))
    s_mid, mid_chip, mid_link, mid_far = call(
        mid_body,
        "square_mid",
        (info, square_kept),
        (other_far, own_left, chip_left, link_left_far, begun_mid),
        [wide, slab, slab, rights],
        work=0,
    )
    mid_link = exchange(mid_link, "col", -1)
    mid_chip = exchange(mid_chip, "col", 1)
    (base,) = call(
        cube_own_body,
        "cube_own",
        (info,),
        (total, s_near, s_mid, s_far, own_right, mid_far),
        [three_wide],
    )
    result = ((side, side), F32)
    base, purified = call(
        cube_chip_body,
        "cube_chip",
        (info, result_kept),
        (far_link, sides_chip, mid_chip, own_right, right_near, right_far, mid_near, mid_far, base),
        [three_wide, result],
        result=True,
        scratch=[pltpu.VMEM((group, side), F32), pltpu.SemaphoreType.DMA(())],
    )
    (purified,) = call(
        finish_body,
        "finish",
        (info, result_kept),
        (mid_link, own_right, base),
        [result],
        result=True,
        begun=(purified,),
        scratch=[pltpu.VMEM((2, group, side), F32), pltpu.SemaphoreType.DMA((2,))],
    )
    return purified


def solution(mesh):
    return jax.shard_map(
        on_device,
        mesh=mesh,
        in_specs=(P("row", "col"), P("row", "col"), P("row", "col")),
        out_specs=P("row", "col"),
        check_vma=False,
    )
```

```python
import functools

import jax
import jax.numpy as jnp
from jax import lax
from jax.experimental import pallas as pl
from jax.experimental.pallas import tpu as pltpu
from jax.sharding import PartitionSpec as P

LANES = 128
WIDE = 256
F32 = jnp.float32
BF16 = jnp.bfloat16
NEAR, MID, FAR = range(3)
OWN, CHIP, LINK = range(3)


def place(info, who, group):
    above = (info[1] == 1) == (who == CHIP)
    return jnp.where(above, 0, group), jnp.where(above, 0, 2)


def shared_rows(info, who, group):
    return pl.ds(pl.multiple_of(place(info, who, group)[0], 64), 2 * group)


def low_half(rows):
    return lax.broadcasted_iota(jnp.int32, (rows, LANES), 1) < LANES // 2


def store_fold(out_ref, base, value):
    rows = value.shape[0]
    half = rows // 2
    tail = value[:, LANES:]
    out_ref[pl.ds(base, rows), :] = value[:, :LANES]
    out_ref[pl.ds(base + rows, half), :] = jnp.where(
        low_half(half), tail[:half], pltpu.roll(tail[half:], LANES // 2, 1)
    )


def unfold(packed):
    rows = packed.shape[0] * 2 // 3
    half = rows // 2
    tail = packed[rows:]
    keep = low_half(half)
    upper = jnp.where(keep, tail, 0.0)
    lower = jnp.where(keep, pltpu.roll(tail, LANES // 2, 1), 0.0)
    return jnp.concatenate([packed[:rows], jnp.concatenate([upper, lower], 0)], 1)


def tile_groups(info, tile_ref, at):
    keep = low_half(at.size)
    first = jnp.concatenate([tile_ref[at, 0:128], jnp.where(keep, tile_ref[at, 128:256], 0.0)], 1)
    one = pltpu.roll(tile_ref[at, 128:256], LANES // 2, 1)
    two = pltpu.roll(tile_ref[at, 256:384], LANES // 2, 1)
    middle = jnp.concatenate([jnp.where(keep, one, two), jnp.where(keep, two, 0.0)], 1)
    end = tile_ref[at, 512:576]
    last = jnp.concatenate([tile_ref[at, 384:512], jnp.concatenate([end, jnp.zeros_like(end)], 1)], 1)
    odd = info[0] == 1
    return jnp.where(odd, first, last), middle, jnp.where(odd, last, first)


def split(value):
    high = value.astype(BF16)
    return high, (value - high.astype(F32)).astype(BF16)


def store_left(out_ref, at, value):
    out_ref[(0,) + at], out_ref[(1,) + at] = split(value)


def store_right(out_ref, at, value):
    group = value.shape[0] // 3
    for half, part in enumerate(split(value)):
        for ky in range(3):
            out_ref[(half,) + at + (pl.ds(ky * WIDE, group),)] = part[ky * group : (ky + 1) * group]
            out_ref[(half,) + at + (pl.ds(ky * WIDE + group, WIDE - group),)] = jnp.zeros((WIDE - group, WIDE), BF16)


def left(ref, *at):
    return ref[(0,) + at], ref[(1,) + at]


def right(ref, info, who, *at):
    start = WIDE if who == OWN else pl.multiple_of(place(info, who, 0)[1] * WIDE, WIDE)
    rows = (pl.ds(start, WIDE),)
    return ref[(0,) + at + rows], ref[(1,) + at + rows]


def passes(lefts, rights):
    wide = [high for high, _ in lefts] + [low for _, low in lefts] + [high for high, _ in lefts]
    tall = [high for high, _ in rights] + [high for high, _ in rights] + [low for _, low in rights]
    return jnp.dot(jnp.concatenate(wide, 1), jnp.concatenate(tall, 0), preferred_element_type=F32)


def mask_at(info, part):
    return 3 if part == MID else jnp.where((info[0] == 1) == (part == NEAR), 0, 6)


def masked(value, kept_ref, start, first_row=0):
    lane = lax.broadcasted_iota(jnp.int32, (8, WIDE), 1)

    def flags(i):
        one, two, three = (kept_ref[first_row + i, start + j] for j in range(3))
        return jnp.where(lane < 64, one, jnp.where(lane < 128, two, three)).astype(F32)[:1]

    return jnp.concatenate([value[i * 64 : (i + 1) * 64] * flags(i) for i in range(value.shape[0] // 64)], 0)


def pack_first_body(info, source, mid, link_a, chip, tile, sems):
    side = tile.shape[0]
    group = side // 3
    copies = [
        pltpu.make_async_copy(source.at[pl.ds(i * group, group), :], tile.at[pl.ds(i * group, group), :], sems.at[i])
        for i in range(3)
    ]
    for copy in copies:
        copy.start()
    slabs = (
        (CHIP, ((chip, 0, NEAR), (chip, 3 * group, MID), (chip, 6 * group, FAR))),
        (LINK, ((link_a, 0, MID), (link_a, 3 * group, NEAR))),
    )
    tails = []
    for i, copy in enumerate(copies):
        copy.wait()
        parts = tile_groups(info, tile, pl.ds(i * group, group))
        mid[pl.ds(i * group, group), :] = parts[MID][:, :LANES]
        tails.append(parts[MID][:, LANES:])
        for who, targets in slabs:
            first = place(info, who, 1)[0]
            for half in range(2):
                if 0 <= i - half <= 1:

                    @pl.when(first == i - half)
                    def _(targets=targets, half=half, parts=parts):
                        for ref, base, part in targets:
                            ref[pl.ds(base + half * group, group), :] = parts[part][:, :LANES]
                            tail = parts[part][:, LANES:]
                            if half == 0:
                                ref[pl.ds(base + 2 * group, group), : LANES // 2] = tail[:, : LANES // 2]
                            else:
                                turned = pltpu.roll(tail, LANES // 2, 1)
                                ref[pl.ds(base + 2 * group, group), LANES // 2 :] = turned[:, LANES // 2 :]

    tail = jnp.concatenate(tails, 0)
    middle = side // 2
    mid[pl.ds(side, middle), :] = jnp.where(
        low_half(middle), tail[:middle], pltpu.roll(tail[middle:], LANES // 2, 1)
    )


def pack_rest_body(info, tile, link_b, near, far):
    side = tile.shape[0]
    groups = tile_groups(info, tile, pl.ds(0, side))
    store_fold(near, 0, groups[NEAR])
    store_fold(far, 0, groups[FAR])
    store_fold(link_b, 0, tile_groups(info, tile, shared_rows(info, LINK, side // 3))[FAR])


def prepare_body(info, tile, chip, own_left, own_right, chip_left):
    side = tile.shape[0]
    for part, value in enumerate(tile_groups(info, tile, pl.ds(0, side))):
        store_left(own_left, (part,), value)
        store_right(own_right, (part,), value)
        store_left(chip_left, (part,), unfold(chip[part * side : (part + 1) * side, :]))


def near_start_body(info, mid, own_left, own_right, chip_left, out, rights):
    group = mid.shape[0] * 2 // 9
    store_right(rights, (), unfold(mid[...]))
    for who, lefts in ((OWN, own_left), (CHIP, chip_left)):
        value = passes(
            [left(lefts, NEAR), left(lefts, MID)], [right(rights, info, who), right(own_right, info, who, NEAR)]
        )
        if who == OWN:
            out[...] = value
        else:
            out[shared_rows(info, who, group), :] += value


def near_body(info, kept, link_a, begun, own_right, right_near, out, link, link_left):
    group = link_a.shape[0] // 6
    for part, base in ((MID, 0), (NEAR, 3 * group)):
        store_left(link_left, (part,), unfold(link_a[base : base + 3 * group, :]))
    out[...] = begun[...]
    out[shared_rows(info, LINK, group), :] += passes(
        [left(link_left, NEAR), left(link_left, MID)],
        [right(right_near, info, LINK), right(own_right, info, LINK, NEAR)],
    )
    out[...] = masked(out[...], kept, mask_at(info, NEAR))
    store_fold(link, 0, out[shared_rows(info, LINK, group), :])


def middle_products_body(info, own_left, own_right, chip_left, link_left, far, mid):
    group = far.shape[0] // 3
    for out, part in ((far, FAR), (mid, MID)):
        for who, lefts in ((OWN, own_left), (CHIP, chip_left), (LINK, link_left)):
            value = passes([left(lefts, MID)], [right(own_right, info, who, part)])
            if who == OWN:
                out[...] = value
            else:
                out[shared_rows(info, who, group), :] += value


def far_body(info, kept, link_b, mid, begun, s_near, own_left, chip_left, out, link, sides, link_left, rights):
    group = out.shape[0] // 3
    store_left(link_left, (), unfold(link_b[...]))
    store_right(rights, (), unfold(mid[...]))
    out[...] = begun[...] + passes([left(own_left, FAR)], [right(rights, info, OWN)])
    for who, factor in ((CHIP, left(chip_left, FAR)), (LINK, left(link_left))):
        out[shared_rows(info, who, group), :] += passes([factor], [right(rights, info, who)])
    out[...] = masked(out[...], kept, mask_at(info, FAR))
    store_fold(link, 0, out[shared_rows(info, LINK, group), :])
    store_fold(sides, 0, s_near[shared_rows(info, CHIP, group), :])
    store_fold(sides, 3 * group, out[shared_rows(info, CHIP, group), :])


def mid_start_body(info, near, begun, own_left, chip_left, link_left, out, rights):
    group = out.shape[0] // 3
    store_right(rights, (), unfold(near[...]))
    out[...] = begun[...] + passes([left(own_left, NEAR)], [right(rights, info, OWN)])
    for who, lefts in ((CHIP, chip_left), (LINK, link_left)):
        out[shared_rows(info, who, group), :] += passes([left(lefts, NEAR)], [right(rights, info, who)])


def mid_body(info, kept, far, own_left, chip_left, link_left, begun, out, chip, link_first, link_second, rights):
    group = out.shape[0] // 3
    store_right(rights, (), unfold(far[...]))
    out[...] = begun[...] + passes([left(own_left, FAR)], [right(rights, info, OWN)])
    for who, factor in ((CHIP, left(chip_left, FAR)), (LINK, left(link_left))):
        out[shared_rows(info, who, group), :] += passes([factor], [right(rights, info, who)])
    out[...] = masked(out[...], kept, 3)
    start = place(info, LINK, group)[0]
    for k, link in enumerate((link_first, link_second)):
        store_fold(link, 0, out[pl.ds(pl.multiple_of(start + k * group, 64), group), :])
    store_fold(chip, 0, out[shared_rows(info, CHIP, group), :])


def cube_near_body(info, link, near, far, right_near, right_far, right_mid, out):
    group = near.shape[0] // 3
    own, other = split(near[...]), split(unfold(link[...]))
    out[FAR] = passes([split(far[...])], [right(right_far, info, OWN)])
    for part, ref in ((NEAR, right_near), (MID, right_mid)):
        out[part] = passes([own], [right(ref, info, OWN)])
        out[part, shared_rows(info, LINK, group), :] += passes([other], [right(ref, info, LINK)])


def cube_own_body(info, total, near, mid, far, own_right, mid_far, out):
    own_mid, own_far = split(mid[...]), split(far[...])
    rights = [right(own_right, info, OWN, part) for part in range(3)]
    out[NEAR] = 3.0 * near[...] - 2.0 * (total[NEAR] + passes([own_mid], rights[NEAR:MID]))
    out[MID] = 3.0 * mid[...] - 2.0 * (total[MID] + passes([own_mid, own_far], [rights[MID], right(mid_far, info, OWN)]))
    out[FAR] = 3.0 * far[...] - 2.0 * (total[FAR] + passes([own_mid], rights[FAR:]))


def send_rows(info, tile, out, sem, row, near, mid, far):
    odd = info[0] == 1
    group = near.shape[0]
    tile[:, :group] = jnp.where(odd, near, far)[:, :group]
    tile[:, group : 2 * group] = mid[:, :group]
    tile[:, 2 * group :] = jnp.where(odd, far, near)[:, :group]
    copy = pltpu.make_async_copy(tile, out.at[pl.ds(row, group), :], sem)
    copy.start()
    return copy


def cube_chip_body(info, kept, link, sides, chip, own_right, right_near, right_far, mid_near, mid_far, base, out, result, tile, sem):
    group = base.shape[1] // 3
    chip_start = place(info, CHIP, group)[0]
    rest = pl.multiple_of(2 * chip_start, 64)
    link_only = pl.multiple_of(2 * (group - chip_start), 64)
    chips = [split(unfold(value)) for value in (sides[: 3 * group, :], chip[...], sides[3 * group :, :])]
    own = [right(own_right, info, CHIP, part) for part in range(3)]
    products = (
        (chips[:2], [right(right_near, info, CHIP), own[NEAR]]),
        (chips, [right(mid_near, info, CHIP), own[MID], right(mid_far, info, CHIP)]),
        (chips[1:], [own[FAR], right(right_far, info, CHIP)]),
    )
    for part in range(3):
        out[part, pl.ds(link_only, group), :] = base[part, pl.ds(link_only, group), :]
    for part, factors in enumerate(products):
        out[part, shared_rows(info, CHIP, group), :] = base[part, shared_rows(info, CHIP, group), :] - 2.0 * passes(*factors)

    def finished(row):
        at = pl.ds(row, group)
        return [masked(out[part, at, :], kept, mask_at(info, part), row // 64) for part in range(3)]

    copy = send_rows(info, tile, result, sem, rest, *finished(rest))
    link_far = split(unfold(link[...]))
    for part, ref in ((MID, mid_far), (FAR, right_far)):
        out[part, shared_rows(info, LINK, group), :] -= 2.0 * passes([link_far], [right(ref, info, LINK)])
    for row in (group, link_only):
        for part, value in enumerate(finished(row)):
            out[part, pl.ds(row, group), :] = value
    copy.wait()


def finish_body(half, info, kept, link, own_right, base, begun, result, tile, sem):
    del begun
    group = tile.shape[0]
    row = pl.multiple_of(place(info, LINK, group)[0] + half * group, 64)
    first_row = place(info, LINK, 3)[0] + 3 * half
    factor = split(unfold(link[...]))
    values = []
    for part in range(3):
        value = -2.0 * passes([factor], [right(own_right, info, LINK, part)])
        values.append(base[part, pl.ds(row, group), :] + masked(value, kept, mask_at(info, part), first_row))
    send_rows(info, tile, result, sem, row, *values).wait()


VMEM = pl.BlockSpec(memory_space=pltpu.VMEM)
SMEM = pl.BlockSpec(memory_space=pltpu.SMEM)
ANY = pl.BlockSpec(memory_space=pl.ANY)
HBM = pl.BlockSpec(memory_space=pltpu.HBM)


def call(body, name, scalars, arrays, outs, work=4, result=False, begun=(), unmoved=(), scratch=()):
    count = len(scalars) + len(arrays)
    return pl.pallas_call(
        body,
        out_shape=[jax.ShapeDtypeStruct(shape, kind) for shape, kind in outs],
        in_specs=[SMEM] * len(scalars) + [VMEM] * len(arrays) + [ANY] * len(begun) + [HBM] * len(unmoved),
        out_specs=[VMEM] * (len(outs) - result) + [ANY] * result,
        scratch_shapes=scratch,
        input_output_aliases={count: len(outs) - 1} if begun else {},
        compiler_params=pltpu.CompilerParams(vmem_limit_bytes=24 << 20),
        cost_estimate=pl.CostEstimate(flops=work * 1000000000, transcendentals=0, bytes_accessed=work * 5000000),
        name=name,
    )(*scalars, *arrays, *begun, *unmoved)


def on_device(p_tiles, square_kept, result_kept):
    side = p_tiles.shape[0]
    group = side // 3
    n_row, n_col = lax.axis_size("row"), lax.axis_size("col")
    info = jnp.stack([lax.axis_index("row") % 2, lax.axis_index("col") % 2]).astype(jnp.int32)
    strip = ((3 * side // 2, LANES), F32)
    slab = ((3 * group, LANES), F32)
    half_slab = ((3 * group // 2, LANES), F32)
    two_slabs = ((6 * group, LANES), F32)
    three_slabs = ((9 * group, LANES), F32)
    wide = ((side, WIDE), F32)
    three_wide = ((3, side, WIDE), F32)
    rights = ((2, 3 * WIDE, WIDE), BF16)

    def exchange(value, axis, even_step):
        size = n_row if axis == "row" else n_col
        return lax.ppermute(
            value, axis, [(i, (i + (even_step if i % 2 == 0 else -even_step)) % size) for i in range(size)]
        )

    mid, link_a, chip = call(
        pack_first_body,
        "pack_first",
        (info,),
        (),
        [strip, two_slabs, three_slabs],
        unmoved=(pltpu.with_memory_space_constraint(p_tiles, pltpu.HBM),),
        scratch=[pltpu.VMEM((side, side), F32), pltpu.SemaphoreType.DMA((3,))],
    )
    link_a = exchange(link_a, "col", -1)
    partner_mid = exchange(mid, "row", 1)
    chip = exchange(chip, "col", 1)
    chip, tile = lax.optimization_barrier((chip, p_tiles))
    link_b, near, far = call(pack_rest_body, "pack_rest", (info,), (tile,), [slab, strip, strip])
    partner_near = exchange(near, "row", 1)
    link_b = exchange(link_b, "col", -1)
    passed_far = exchange(far, "row", -2)

    own_left, own_right, chip_left = call(
        prepare_body,
        "prepare",
        (info,),
        (p_tiles, chip),
        [((2, 3, side, WIDE), BF16), ((2, 3, 3 * WIDE, WIDE), BF16), ((2, 3, 2 * group, WIDE), BF16)],
    )
    partner_mid, own_left = lax.optimization_barrier((partner_mid, own_left))
    other_mid = exchange(partner_mid, "row", 2)
    begun, right_near = call(
        near_start_body, "near_start", (info,), (partner_mid, own_left, own_right, chip_left), [wide, rights]
    )
    s_near, near_link, link_left = call(
        near_body,
        "square_near",
        (info, square_kept),
        (link_a, begun, own_right, right_near),
        [wide, slab, ((2, 2, 2 * group, WIDE), BF16)],
    )
    near_link = exchange(near_link, "col", -1)
    passed_far, link_left = lax.optimization_barrier((passed_far, link_left))
    other_far = exchange(passed_far, "row", 1)
    begun, begun_mid = call(
        middle_products_body, "middle_products", (info,), (own_left, own_right, chip_left, link_left), [wide] * 2
    )
    begun_mid, mid_near = call(
        mid_start_body,
        "mid_start",
        (info,),
        (partner_near, begun_mid, own_left, chip_left, link_left),
        [wide, rights],
    )
    begun, begun_mid = lax.optimization_barrier((begun, begun_mid))
    s_far, far_link, sides_chip, link_left_far, right_far = call(
        far_body,
        "square_far",
        (info, square_kept),
        (link_b, other_mid, begun, s_near, own_left, chip_left),
        [wide, slab, two_slabs, ((2, 2 * group, WIDE), BF16), rights],
    )
    far_link = exchange(far_link, "col", -1)
    sides_chip = exchange(sides_chip, "col", 1)
    (total,) = call(
        cube_near_body,
        "cube_near",
        (info,),
        (near_link, s_near, s_far, right_near, right_far, mid_near),
        [three_wide],
    )
    total, other_far = lax.optimization_barrier((total, other_far))
    s_mid, mid_chip, link_first, link_second, mid_far = call(
        mid_body,
        "square_mid",
        (info, square_kept),
        (other_far, own_left, chip_left, link_left_far, begun_mid),
        [wide, slab, half_slab, half_slab, rights],
        work=0,
    )
    link_first = exchange(link_first, "col", -1)
    mid_chip = exchange(mid_chip, "col", 1)
    (base,) = call(
        cube_own_body,
        "cube_own",
        (info,),
        (total, s_near, s_mid, s_far, own_right, mid_far),
        [three_wide],
    )
    link_second, sides_chip = lax.optimization_barrier((link_second, sides_chip))
    link_second = exchange(link_second, "col", -1)
    result = ((side, side), F32)
    base, purified = call(
        cube_chip_body,
        "cube_chip",
        (info, result_kept),
        (far_link, sides_chip, mid_chip, own_right, right_near, right_far, mid_near, mid_far, base),
        [three_wide, result],
        result=True,
        scratch=[pltpu.VMEM((group, side), F32), pltpu.SemaphoreType.DMA(())],
    )
    for half, link in enumerate((link_first, link_second)):
        (purified,) = call(
            functools.partial(finish_body, half),
            ("finish_first", "finish_second")[half],
            (info, result_kept),
            (link, own_right, base),
            [result],
            result=True,
            begun=(purified,),
            scratch=[pltpu.VMEM((group, side), F32), pltpu.SemaphoreType.DMA(())],
        )
    return purified


def solution(mesh):
    return jax.shard_map(
        on_device,
        mesh=mesh,
        in_specs=(P("row", "col"), P("row", "col"), P("row", "col")),
        out_specs=P("row", "col"),
        check_vma=False,
    )
```

```python
import functools

import jax
import jax.numpy as jnp
from jax import lax
from jax.experimental import pallas as pl
from jax.experimental.pallas import tpu as pltpu
from jax.sharding import PartitionSpec as P

LANES = 128
WIDE = 256
F32 = jnp.float32
BF16 = jnp.bfloat16
NEAR, MID, FAR = range(3)
OWN, CHIP, LINK = range(3)


def place(info, who, group):
    above = (info[1] == 1) == (who == CHIP)
    return jnp.where(above, 0, group), jnp.where(above, 0, 2)


def shared_rows(info, who, group):
    return pl.ds(pl.multiple_of(place(info, who, group)[0], 64), 2 * group)


def low_half(rows):
    return lax.broadcasted_iota(jnp.int32, (rows, LANES), 1) < LANES // 2


def store_fold(out_ref, base, value):
    rows = value.shape[0]
    half = rows // 2
    tail = value[:, LANES:]
    out_ref[pl.ds(base, rows), :] = value[:, :LANES]
    out_ref[pl.ds(base + rows, half), :] = jnp.where(
        low_half(half), tail[:half], pltpu.roll(tail[half:], LANES // 2, 1)
    )


def unfold(packed):
    rows = packed.shape[0] * 2 // 3
    half = rows // 2
    tail = packed[rows:]
    keep = low_half(half)
    upper = jnp.where(keep, tail, 0.0)
    lower = jnp.where(keep, pltpu.roll(tail, LANES // 2, 1), 0.0)
    return jnp.concatenate([packed[:rows], jnp.concatenate([upper, lower], 0)], 1)


def tile_groups(info, tile_ref, at):
    keep = low_half(at.size)
    first = jnp.concatenate([tile_ref[at, 0:128], jnp.where(keep, tile_ref[at, 128:256], 0.0)], 1)
    one = pltpu.roll(tile_ref[at, 128:256], LANES // 2, 1)
    two = pltpu.roll(tile_ref[at, 256:384], LANES // 2, 1)
    middle = jnp.concatenate([jnp.where(keep, one, two), jnp.where(keep, two, 0.0)], 1)
    end = tile_ref[at, 512:576]
    last = jnp.concatenate([tile_ref[at, 384:512], jnp.concatenate([end, jnp.zeros_like(end)], 1)], 1)
    odd = info[0] == 1
    return jnp.where(odd, first, last), middle, jnp.where(odd, last, first)


def split(value):
    high = value.astype(BF16)
    return high, (value - high.astype(F32)).astype(BF16)


def store_left(out_ref, at, value):
    out_ref[(0,) + at], out_ref[(1,) + at] = split(value)


def store_right(out_ref, at, value):
    group = value.shape[0] // 3
    for half, part in enumerate(split(value)):
        for ky in range(3):
            out_ref[(half,) + at + (pl.ds(ky * WIDE, group),)] = part[ky * group : (ky + 1) * group]
            out_ref[(half,) + at + (pl.ds(ky * WIDE + group, WIDE - group),)] = jnp.zeros((WIDE - group, WIDE), BF16)


def left(ref, *at):
    return ref[(0,) + at], ref[(1,) + at]


def right(ref, info, who, *at):
    start = WIDE if who == OWN else pl.multiple_of(place(info, who, 0)[1] * WIDE, WIDE)
    rows = (pl.ds(start, WIDE),)
    return ref[(0,) + at + rows], ref[(1,) + at + rows]


def passes(lefts, rights):
    wide = [high for high, _ in lefts] + [low for _, low in lefts] + [high for high, _ in lefts]
    tall = [high for high, _ in rights] + [high for high, _ in rights] + [low for _, low in rights]
    return jnp.dot(jnp.concatenate(wide, 1), jnp.concatenate(tall, 0), preferred_element_type=F32)


def mask_at(info, part):
    return 3 if part == MID else jnp.where((info[0] == 1) == (part == NEAR), 0, 6)


def masked(value, kept_ref, start, first_row=0):
    lane = lax.broadcasted_iota(jnp.int32, (8, WIDE), 1)

    def flags(i):
        one, two, three = (kept_ref[first_row + i, start + j] for j in range(3))
        return jnp.where(lane < 64, one, jnp.where(lane < 128, two, three)).astype(F32)[:1]

    return jnp.concatenate([value[i * 64 : (i + 1) * 64] * flags(i) for i in range(value.shape[0] // 64)], 0)


def pack_first_body(info, source, mid, link_a, chip, tile, sems):
    side = tile.shape[0]
    group = side // 3
    copies = [
        pltpu.make_async_copy(source.at[pl.ds(i * group, group), :], tile.at[pl.ds(i * group, group), :], sems.at[i])
        for i in range(3)
    ]
    for copy in copies:
        copy.start()
    slabs = (
        (CHIP, ((chip, 0, NEAR), (chip, 3 * group, MID), (chip, 6 * group, FAR))),
        (LINK, ((link_a, 0, MID), (link_a, 3 * group, NEAR))),
    )
    tails = []
    for i, copy in enumerate(copies):
        copy.wait()
        parts = tile_groups(info, tile, pl.ds(i * group, group))
        mid[pl.ds(i * group, group), :] = parts[MID][:, :LANES]
        tails.append(parts[MID][:, LANES:])
        for who, targets in slabs:
            first = place(info, who, 1)[0]
            for half in range(2):
                if 0 <= i - half <= 1:

                    @pl.when(first == i - half)
                    def _(targets=targets, half=half, parts=parts):
                        for ref, base, part in targets:
                            ref[pl.ds(base + half * group, group), :] = parts[part][:, :LANES]
                            tail = parts[part][:, LANES:]
                            if half == 0:
                                ref[pl.ds(base + 2 * group, group), : LANES // 2] = tail[:, : LANES // 2]
                            else:
                                turned = pltpu.roll(tail, LANES // 2, 1)
                                ref[pl.ds(base + 2 * group, group), LANES // 2 :] = turned[:, LANES // 2 :]

    tail = jnp.concatenate(tails, 0)
    middle = side // 2
    mid[pl.ds(side, middle), :] = jnp.where(
        low_half(middle), tail[:middle], pltpu.roll(tail[middle:], LANES // 2, 1)
    )


def pack_rest_body(info, tile, link_b, near, far):
    side = tile.shape[0]
    groups = tile_groups(info, tile, pl.ds(0, side))
    store_fold(near, 0, groups[NEAR])
    store_fold(far, 0, groups[FAR])
    store_fold(link_b, 0, tile_groups(info, tile, shared_rows(info, LINK, side // 3))[FAR])


def prepare_body(info, tile, chip, own_left, own_right, chip_left):
    side = tile.shape[0]
    for part, value in enumerate(tile_groups(info, tile, pl.ds(0, side))):
        store_left(own_left, (part,), value)
        store_right(own_right, (part,), value)
        store_left(chip_left, (part,), unfold(chip[part * side : (part + 1) * side, :]))


def near_start_body(info, mid, own_left, own_right, chip_left, out, rights):
    group = mid.shape[0] * 2 // 9
    store_right(rights, (), unfold(mid[...]))
    for who, lefts in ((OWN, own_left), (CHIP, chip_left)):
        value = passes(
            [left(lefts, NEAR), left(lefts, MID)], [right(rights, info, who), right(own_right, info, who, NEAR)]
        )
        if who == OWN:
            out[...] = value
        else:
            out[shared_rows(info, who, group), :] += value


def near_body(info, kept, link_a, begun, own_right, right_near, out, link, link_left):
    group = link_a.shape[0] // 6
    for part, base in ((MID, 0), (NEAR, 3 * group)):
        store_left(link_left, (part,), unfold(link_a[base : base + 3 * group, :]))
    out[...] = begun[...]
    out[shared_rows(info, LINK, group), :] += passes(
        [left(link_left, NEAR), left(link_left, MID)],
        [right(right_near, info, LINK), right(own_right, info, LINK, NEAR)],
    )
    out[...] = masked(out[...], kept, mask_at(info, NEAR))
    store_fold(link, 0, out[shared_rows(info, LINK, group), :])


def middle_products_body(info, own_left, own_right, chip_left, link_left, far, mid):
    group = far.shape[0] // 3
    for out, part in ((far, FAR), (mid, MID)):
        for who, lefts in ((OWN, own_left), (CHIP, chip_left), (LINK, link_left)):
            value = passes([left(lefts, MID)], [right(own_right, info, who, part)])
            if who == OWN:
                out[...] = value
            else:
                out[shared_rows(info, who, group), :] += value


def far_body(info, kept, link_b, mid, begun, s_near, own_left, chip_left, out, link, sides, link_left, rights):
    group = out.shape[0] // 3
    store_left(link_left, (), unfold(link_b[...]))
    store_right(rights, (), unfold(mid[...]))
    out[...] = begun[...] + passes([left(own_left, FAR)], [right(rights, info, OWN)])
    for who, factor in ((CHIP, left(chip_left, FAR)), (LINK, left(link_left))):
        out[shared_rows(info, who, group), :] += passes([factor], [right(rights, info, who)])
    out[...] = masked(out[...], kept, mask_at(info, FAR))
    store_fold(link, 0, out[shared_rows(info, LINK, group), :])
    store_fold(sides, 0, s_near[shared_rows(info, CHIP, group), :])
    store_fold(sides, 3 * group, out[shared_rows(info, CHIP, group), :])


def mid_start_body(info, near, begun, own_left, chip_left, link_left, out, rights):
    group = out.shape[0] // 3
    store_right(rights, (), unfold(near[...]))
    out[...] = begun[...] + passes([left(own_left, NEAR)], [right(rights, info, OWN)])
    for who, lefts in ((CHIP, chip_left), (LINK, link_left)):
        out[shared_rows(info, who, group), :] += passes([left(lefts, NEAR)], [right(rights, info, who)])


def mid_body(info, kept, far, own_left, chip_left, link_left, begun, out, chip, link_first, link_second, rights):
    group = out.shape[0] // 3
    store_right(rights, (), unfold(far[...]))
    out[...] = begun[...] + passes([left(own_left, FAR)], [right(rights, info, OWN)])
    for who, factor in ((CHIP, left(chip_left, FAR)), (LINK, left(link_left))):
        out[shared_rows(info, who, group), :] += passes([factor], [right(rights, info, who)])
    out[...] = masked(out[...], kept, 3)
    start = place(info, LINK, group)[0]
    for k, link in enumerate((link_first, link_second)):
        store_fold(link, 0, out[pl.ds(pl.multiple_of(start + k * group, 64), group), :])
    store_fold(chip, 0, out[shared_rows(info, CHIP, group), :])


def cube_near_body(info, link, near, far, right_near, right_far, right_mid, out):
    group = near.shape[0] // 3
    own, other = split(near[...]), split(unfold(link[...]))
    out[FAR] = passes([split(far[...])], [right(right_far, info, OWN)])
    for part, ref in ((NEAR, right_near), (MID, right_mid)):
        out[part] = passes([own], [right(ref, info, OWN)])
        out[part, shared_rows(info, LINK, group), :] += passes([other], [right(ref, info, LINK)])


def cube_own_body(info, total, near, mid, far, own_right, mid_far, out):
    own_mid, own_far = split(mid[...]), split(far[...])
    rights = [right(own_right, info, OWN, part) for part in range(3)]
    out[NEAR] = 3.0 * near[...] - 2.0 * (total[NEAR] + passes([own_mid], rights[NEAR:MID]))
    out[MID] = 3.0 * mid[...] - 2.0 * (total[MID] + passes([own_mid, own_far], [rights[MID], right(mid_far, info, OWN)]))
    out[FAR] = 3.0 * far[...] - 2.0 * (total[FAR] + passes([own_mid], rights[FAR:]))


def send_rows(info, tile, out, sem, row, near, mid, far):
    odd = info[0] == 1
    group = near.shape[0]
    tile[:, :group] = jnp.where(odd, near, far)[:, :group]
    tile[:, group : 2 * group] = mid[:, :group]
    tile[:, 2 * group :] = jnp.where(odd, far, near)[:, :group]
    copy = pltpu.make_async_copy(tile, out.at[pl.ds(row, group), :], sem)
    copy.start()
    return copy


def cube_chip_body(info, kept, link, sides, chip, own_right, right_near, right_far, mid_near, mid_far, base, out, result, tile, sem):
    group = base.shape[1] // 3
    chip_start = place(info, CHIP, group)[0]
    rest = pl.multiple_of(2 * chip_start, 64)
    link_only = pl.multiple_of(2 * (group - chip_start), 64)
    chips = [split(unfold(value)) for value in (sides[: 3 * group, :], chip[...], sides[3 * group :, :])]
    own = [right(own_right, info, CHIP, part) for part in range(3)]
    products = (
        (chips[:2], [right(right_near, info, CHIP), own[NEAR]]),
        (chips, [right(mid_near, info, CHIP), own[MID], right(mid_far, info, CHIP)]),
        (chips[1:], [own[FAR], right(right_far, info, CHIP)]),
    )
    for part in range(3):
        out[part, pl.ds(link_only, group), :] = base[part, pl.ds(link_only, group), :]
    for part, factors in enumerate(products):
        out[part, shared_rows(info, CHIP, group), :] = base[part, shared_rows(info, CHIP, group), :] - 2.0 * passes(*factors)

    def finished(row):
        at = pl.ds(row, group)
        return [masked(out[part, at, :], kept, mask_at(info, part), row // 64) for part in range(3)]

    copy = send_rows(info, tile, result, sem, rest, *finished(rest))
    link_far = split(unfold(link[...]))
    for part, ref in ((MID, mid_far), (FAR, right_far)):
        out[part, shared_rows(info, LINK, group), :] -= 2.0 * passes([link_far], [right(ref, info, LINK)])
    for row in (group, link_only):
        for part, value in enumerate(finished(row)):
            out[part, pl.ds(row, group), :] = value
    copy.wait()


def finish_body(half, info, kept, link, own_right, base, begun, result, tile, sem):
    del begun
    group = tile.shape[0]
    row = pl.multiple_of(place(info, LINK, group)[0] + half * group, 64)
    first_row = place(info, LINK, 3)[0] + 3 * half
    factor = split(unfold(link[...]))
    values = []
    for part in range(3):
        value = -2.0 * passes([factor], [right(own_right, info, LINK, part)])
        values.append(base[part, pl.ds(row, group), :] + masked(value, kept, mask_at(info, part), first_row))
    send_rows(info, tile, result, sem, row, *values).wait()


VMEM = pl.BlockSpec(memory_space=pltpu.VMEM)
SMEM = pl.BlockSpec(memory_space=pltpu.SMEM)
ANY = pl.BlockSpec(memory_space=pl.ANY)
HBM = pl.BlockSpec(memory_space=pltpu.HBM)


def call(body, name, scalars, arrays, outs, work=4, result=False, begun=(), unmoved=(), scratch=()):
    count = len(scalars) + len(arrays)
    return pl.pallas_call(
        body,
        out_shape=[jax.ShapeDtypeStruct(shape, kind) for shape, kind in outs],
        in_specs=[SMEM] * len(scalars) + [VMEM] * len(arrays) + [ANY] * len(begun) + [HBM] * len(unmoved),
        out_specs=[VMEM] * (len(outs) - result) + [ANY] * result,
        scratch_shapes=scratch,
        input_output_aliases={count: len(outs) - 1} if begun else {},
        compiler_params=pltpu.CompilerParams(vmem_limit_bytes=24 << 20),
        cost_estimate=pl.CostEstimate(flops=work * 1000000000, transcendentals=0, bytes_accessed=work * 5000000),
        name=name,
    )(*scalars, *arrays, *begun, *unmoved)


def on_device(p_tiles, square_kept, result_kept):
    side = p_tiles.shape[0]
    group = side // 3
    n_row, n_col = lax.axis_size("row"), lax.axis_size("col")
    info = jnp.stack([lax.axis_index("row") % 2, lax.axis_index("col") % 2]).astype(jnp.int32)
    strip = ((3 * side // 2, LANES), F32)
    slab = ((3 * group, LANES), F32)
    half_slab = ((3 * group // 2, LANES), F32)
    two_slabs = ((6 * group, LANES), F32)
    three_slabs = ((9 * group, LANES), F32)
    wide = ((side, WIDE), F32)
    three_wide = ((3, side, WIDE), F32)
    rights = ((2, 3 * WIDE, WIDE), BF16)

    def exchange(value, axis, even_step):
        size = n_row if axis == "row" else n_col
        return lax.ppermute(
            value, axis, [(i, (i + (even_step if i % 2 == 0 else -even_step)) % size) for i in range(size)]
        )

    mid, link_a, chip, held = call(
        pack_first_body,
        "pack_first",
        (info,),
        (),
        [strip, two_slabs, three_slabs, ((side, side), F32)],
        unmoved=(pltpu.with_memory_space_constraint(p_tiles, pltpu.HBM),),
        scratch=[pltpu.SemaphoreType.DMA((3,))],
    )
    link_a = exchange(link_a, "col", -1)
    partner_mid = exchange(mid, "row", 1)
    chip = exchange(chip, "col", 1)
    chip, tile = lax.optimization_barrier((chip, held))
    link_b, near, far = call(pack_rest_body, "pack_rest", (info,), (tile,), [slab, strip, strip])
    partner_near = exchange(near, "row", 1)
    link_b = exchange(link_b, "col", -1)
    passed_far = exchange(far, "row", -2)

    own_left, own_right, chip_left = call(
        prepare_body,
        "prepare",
        (info,),
        (held, chip),
        [((2, 3, side, WIDE), BF16), ((2, 3, 3 * WIDE, WIDE), BF16), ((2, 3, 2 * group, WIDE), BF16)],
    )
    partner_mid, own_left = lax.optimization_barrier((partner_mid, own_left))
    other_mid = exchange(partner_mid, "row", 2)
    begun, right_near = call(
        near_start_body, "near_start", (info,), (partner_mid, own_left, own_right, chip_left), [wide, rights]
    )
    s_near, near_link, link_left = call(
        near_body,
        "square_near",
        (info, square_kept),
        (link_a, begun, own_right, right_near),
        [wide, slab, ((2, 2, 2 * group, WIDE), BF16)],
    )
    near_link = exchange(near_link, "col", -1)
    passed_far, link_left = lax.optimization_barrier((passed_far, link_left))
    other_far = exchange(passed_far, "row", 1)
    begun, begun_mid = call(
        middle_products_body, "middle_products", (info,), (own_left, own_right, chip_left, link_left), [wide] * 2
    )
    begun_mid, mid_near = call(
        mid_start_body,
        "mid_start",
        (info,),
        (partner_near, begun_mid, own_left, chip_left, link_left),
        [wide, rights],
    )
    begun, begun_mid = lax.optimization_barrier((begun, begun_mid))
    s_far, far_link, sides_chip, link_left_far, right_far = call(
        far_body,
        "square_far",
        (info, square_kept),
        (link_b, other_mid, begun, s_near, own_left, chip_left),
        [wide, slab, two_slabs, ((2, 2 * group, WIDE), BF16), rights],
    )
    far_link = exchange(far_link, "col", -1)
    sides_chip = exchange(sides_chip, "col", 1)
    (total,) = call(
        cube_near_body,
        "cube_near",
        (info,),
        (near_link, s_near, s_far, right_near, right_far, mid_near),
        [three_wide],
    )
    total, other_far = lax.optimization_barrier((total, other_far))
    s_mid, mid_chip, link_first, link_second, mid_far = call(
        mid_body,
        "square_mid",
        (info, square_kept),
        (other_far, own_left, chip_left, link_left_far, begun_mid),
        [wide, slab, half_slab, half_slab, rights],
        work=0,
    )
    link_first = exchange(link_first, "col", -1)
    mid_chip = exchange(mid_chip, "col", 1)
    (base,) = call(
        cube_own_body,
        "cube_own",
        (info,),
        (total, s_near, s_mid, s_far, own_right, mid_far),
        [three_wide],
    )
    link_second, sides_chip = lax.optimization_barrier((link_second, sides_chip))
    link_second = exchange(link_second, "col", -1)
    result = ((side, side), F32)
    base, purified = call(
        cube_chip_body,
        "cube_chip",
        (info, result_kept),
        (far_link, sides_chip, mid_chip, own_right, right_near, right_far, mid_near, mid_far, base),
        [three_wide, result],
        result=True,
        scratch=[pltpu.VMEM((group, side), F32), pltpu.SemaphoreType.DMA(())],
    )
    for half, link in enumerate((link_first, link_second)):
        (purified,) = call(
            functools.partial(finish_body, half),
            ("finish_first", "finish_second")[half],
            (info, result_kept),
            (link, own_right, base),
            [result],
            result=True,
            begun=(purified,),
            scratch=[pltpu.VMEM((group, side), F32), pltpu.SemaphoreType.DMA(())],
        )
    return purified


def solution(mesh):
    return jax.shard_map(
        on_device,
        mesh=mesh,
        in_specs=(P("row", "col"), P("row", "col"), P("row", "col")),
        out_specs=P("row", "col"),
        check_vma=False,
    )
```
